32 devices in a mesh: group: 4 (over y, x), hidden: 8 (over z, core).
Axes of the slice: x: 2, y: 2, z: 4, core: 2. Of those that a mesh axis runs over, the one named last changes fastest.
Arguments:
- queries: bfloat16 [1536, 4096], P('group', 'hidden'), may hold values from -16 to 16, as said below
- key_rows: bfloat16 [1536, 512], P('group'), may hold values from -16 to 16
- value_rows: bfloat16 [1536, 512], P('group'), may hold values from -6 to 6
- out_proj: bfloat16 [4096, 2048], P('hidden'), may hold values from -0.09375 to 0.09375
- residual: bfloat16 [1536, 2048], P('group'), may hold values from -120 to 120
- norm_gain: float32 [2048], replicated, may hold values from 0.1 to 1.9
- w_gate: bfloat16 [32, 2048, 768], P('group', None, 'hidden'), may hold values from -0.125 to 0.125
- w_up: bfloat16 [32, 2048, 768], P('group', None, 'hidden'), may hold values from -0.125 to 0.125
- w_down: bfloat16 [32, 768, 2048], P('group', 'hidden'), may hold values from -0.21875 to 0.21875
- route_slot: int32 [1536, 8], P('group'), may hold values from 0 to 15, all different within a row; in each aligned block of 384 rows (0 to 383, 384 to 767, ...) at most 240 rows name the same one
- route_weight: float32 [1536, 8], P('group'), may hold values from 0.05 to 0.3
- fetch_list: int32 [4, 16], replicated, may hold values from 0 to 31, as said below
- cotangent: bfloat16 [1536, 2048], P('group'), may hold values from -6 to 6
Outputs:
- layer_out: bfloat16 [1536, 2048], P('group', 'hidden')
- grad_normed: bfloat16 [1536, 2048], P('group', 'hidden')
- grad_gate: bfloat16 [32, 2048, 768], P('group', None, 'hidden')
- grad_up: bfloat16 [32, 2048, 768], P('group', None, 'hidden')
- grad_down: bfloat16 [32, 768, 2048], P('group', 'hidden')
The draws below stay inside these ranges and needn't reach their ends.
Inputs may be any that keep to these rules, and one draw needn't show every extreme that they name: `queries`: queries and keys lie within the range. `route_slot`: within each group's 384 tokens no entry is named by more than 240 tokens, a bound that some block reaches; a token's 8 entries differ. `fetch_list`: entry f of every group's list is an expert owned by owner group f // 4, that is an id from (f // 4) * 8 to (f // 4) * 8 + 7; the ids of one group's list differ.
All inputs are finite; a program needn't handle non-finite values.
Results may differ from the reference program's by a relative error of at most 0.017.
Values may be sent and summed in bfloat16 or wider, within the bound.
A program may use at most 256 MiB of HBM per device.

```python
import math
import jax
import jax.numpy as jnp
import numpy as np
from jax import lax

D = 2048
FF = 768
HEADS = 32
KV_HEADS = 4
HEAD_DIM = 128
TOPK = 8
EXP_GROUP = 8
FETCH = 16
TOK_GROUP = 384
CAP = 240
EXPERTS = 32
TOKENS = 1536
N_GROUP = 4
N_HIDDEN = 8


def pair_draws(key):
    key_keys, key_queries = jax.random.split(jax.random.fold_in(key, 7), 2)
    keys_out = jnp.clip(jax.random.normal(key_keys, (TOKENS, KV_HEADS * HEAD_DIM), jnp.float32), -4.0, 4.0)
    queries_out = jnp.clip(jax.random.normal(key_queries, (TOKENS, HEADS * HEAD_DIM), jnp.float32), -4.0, 4.0)
    return (keys_out, queries_out)


def draw_queries(key, part):
    return pair_draws(key)[1].astype(jnp.bfloat16)


def draw_key_rows(key, part):
    return pair_draws(key)[0].astype(jnp.bfloat16)


def draw_residual(key, part):
    key_values = jax.random.fold_in(jax.random.fold_in(key, 3), 0)
    values = jnp.clip(jax.random.normal(key_values, (TOKENS, D), jnp.float32), -4.0, 4.0)
    return values.astype(jnp.bfloat16)


def draw_fetch_list(key, part):
    per_owner = FETCH // N_GROUP
    scores = jax.random.randint(jax.random.fold_in(key, 5), (N_GROUP, N_GROUP, EXP_GROUP), 0, 1 << 20) * EXP_GROUP
    scores = scores + jnp.arange(EXP_GROUP, dtype=jnp.int32)[None, None, :]
    order = jnp.argsort(scores, axis=-1, stable=True)[:, :, :per_owner]
    ids = order + (jnp.arange(N_GROUP, dtype=jnp.int32) * EXP_GROUP)[None, :, None]
    return ids.reshape(N_GROUP, FETCH).astype(jnp.int32)


def block_levels(key, extent, pieces, smallest, largest):
    factor_of, own = 1.0, jax.random.fold_in(key, 6)
    for dim, blocks in pieces:
        steps = jnp.exp(jax.random.uniform(jax.random.fold_in(own, dim), (blocks,), jnp.float32, smallest / len(pieces), largest / len(pieces)))
        factor_of = factor_of * jnp.repeat(steps, extent[dim] // blocks).reshape([-1 if axis == dim else 1 for axis in range(len(extent))])
    return factor_of


def deal_out(key, own, number, rows, amount, top, most, skew):
    ranking = jax.random.permutation(key, amount)
    crowded, usual = load_shares(amount, rows * top, most, skew, True), load_shares(amount, rows * top, most, skew, False)
    places = jnp.arange(amount)

    def named(sizes, offset_by):
        used = int((sizes > 0).sum())
        fixed = max(1, used // 4)
        moved = fixed + (places - fixed + offset_by * (used - fixed)) % max(1, amount - fixed)
        return jnp.zeros((amount,), jnp.int32).at[ranking[jnp.where(places < fixed, places, moved)]].set(jnp.asarray(sizes, jnp.int32))

    sizes = jnp.where(number % 4 == 0, named(crowded, number // 4), named(usual, number - number // 4 - 1))
    mixed = jax.random.permutation(jax.random.fold_in(own, 3), amount)
    giver, receiver = mixed[0:amount // 2 * 2:2], mixed[1:amount // 2 * 2:2]
    slack = jnp.minimum(sizes[giver] - 1, most - sizes[receiver]) // 2
    slack = jnp.where((giver == ranking[0]) | (receiver == ranking[0]) | (sizes[receiver] == 0), 0, jnp.maximum(slack, 0))
    moved = jax.random.randint(jax.random.fold_in(own, 4), (amount // 2,), 0, 1 << 20) % (slack + 1)
    sizes = sizes.at[giver].add(-moved).at[receiver].add(moved)
    items = jnp.searchsorted(jnp.cumsum(sizes), jnp.arange(rows * top), side="right").astype(jnp.int32)
    listing = items.reshape(top, rows).T
    listing = listing[jax.random.permutation(jax.random.fold_in(own, 1), rows)]
    offset_by = jax.random.randint(jax.random.fold_in(own, 2), (rows, 1), 0, top)
    return jnp.take_along_axis(listing, (jnp.arange(top)[None, :] + offset_by) % top, axis=1)


def load_shares(amount, total, bound, slope, full):
    weights = [(1 << 20) // math.isqrt(standing ** slope) + 1 for standing in range(1, amount + 1)]
    largest = bound if full else min(bound, max(-(-total // amount), total * weights[0] // sum(weights)))
    least = 1 if total - largest >= amount - 1 else 0
    counts, rest = [largest] + [least] * (amount - 1), total - largest - least * (amount - 1)
    while rest > 0:
        candidates = [i for i in range(1, amount) if counts[i] < largest] or [i for i in range(1, amount) if counts[i] < bound]
        whole, left = sum([weights[i] for i in candidates]), rest
        for i in candidates:
            addition = min(bound - counts[i], max(1, left * weights[i] // whole), rest)
            counts[i] = counts[i] + addition
            rest = rest - addition
    return np.array(counts)


def bell_draw(stream_key, dims, width, limit, pieces=(), kind=jnp.bfloat16):
    values = width * jax.random.normal(stream_key, dims, jnp.float32)
    if pieces:
        values = values * block_levels(stream_key, dims, pieces, -0.22, 0.18)
    return jnp.clip(values, -limit, limit).astype(kind)


def setup_inputs(seed: int = 0) -> dict:
    arg_keys = jax.random.split(jax.random.key(seed), 14)
    queries = draw_queries(jax.random.fold_in(arg_keys[13], 71), 0)
    key_rows = draw_key_rows(jax.random.fold_in(arg_keys[13], 71), 0)
    value_rows = bell_draw(arg_keys[2], (TOKENS, KV_HEADS * HEAD_DIM), 1.0, 6.0, ((0, 4),))
    out_proj = bell_draw(arg_keys[3], (HEADS * HEAD_DIM, D), (HEADS * HEAD_DIM) ** -0.5, 0.09375, ((0, 8),))
    residual = draw_residual(jax.random.fold_in(arg_keys[13], 71), 0)
    norm_gain = jnp.clip(1.0 + 0.18 * jax.random.normal(arg_keys[5], (D,), jnp.float32), 0.1, 1.9)
    w_gate = bell_draw(arg_keys[6], (EXPERTS, D, FF), D ** -0.5, 0.125, ((0, 4), (2, 8)))
    w_up = bell_draw(arg_keys[7], (EXPERTS, D, FF), D ** -0.5, 0.125, ((0, 4), (2, 8)))
    w_down = bell_draw(arg_keys[8], (EXPERTS, FF, D), FF ** -0.5, 0.21875, ((0, 4), (1, 8)))
    route_slot_keys = jax.random.split(jax.random.fold_in(arg_keys[9], 1), TOKENS // TOK_GROUP)
    route_slot_turns = jax.random.permutation(jax.random.fold_in(arg_keys[9], 3), TOKENS // TOK_GROUP)
    route_slot = jax.vmap(lambda own, number: deal_out(jax.random.fold_in(arg_keys[9], 2), own, number, TOK_GROUP, FETCH, TOPK, CAP, 2))(route_slot_keys, route_slot_turns).reshape((TOKENS, TOPK))
    route_weight = jnp.clip(0.05 + 0.25 * jax.random.uniform(arg_keys[10], (TOKENS, TOPK), jnp.float32) ** block_levels(arg_keys[10], (TOKENS, TOPK), ((0, 4),), -0.2, 0.2), 0.05, 0.3)
    fetch_list = draw_fetch_list(jax.random.fold_in(arg_keys[13], 71), 0)
    cotangent = bell_draw(arg_keys[12], (TOKENS, D), 1.0, 6.0, ((0, 4),))
    return dict(queries=queries, key_rows=key_rows, value_rows=value_rows, out_proj=out_proj, residual=residual, norm_gain=norm_gain, w_gate=w_gate, w_up=w_up, w_down=w_down, route_slot=route_slot, route_weight=route_weight, fetch_list=fetch_list, cotangent=cotangent)


epsilon = 1e-06

def attend(query_in, key_in, value_in):
    tokens_here = query_in.shape[0]
    query_heads = query_in.reshape(tokens_here, HEADS, HEAD_DIM).astype(jnp.float32)
    key_heads = jnp.repeat(key_in.reshape(tokens_here, KV_HEADS, HEAD_DIM).astype(jnp.float32), HEADS // KV_HEADS, axis=1)
    value_heads = jnp.repeat(value_in.reshape(tokens_here, KV_HEADS, HEAD_DIM).astype(jnp.float32), HEADS // KV_HEADS, axis=1)
    scores = jnp.einsum('thd,shd->hts', query_heads, key_heads) / math.sqrt(HEAD_DIM)
    row_pos = jnp.arange(tokens_here, dtype=jnp.int32)[:, None]
    col_pos = jnp.arange(tokens_here, dtype=jnp.int32)[None, :]
    scores = jnp.where(row_pos >= col_pos, scores, -1e+30)
    row_peak = lax.optimization_barrier(jnp.max(scores, axis=-1, keepdims=True))
    weights = jnp.exp(scores - row_peak)
    probabilities = (weights / lax.optimization_barrier(jnp.sum(weights, axis=-1, keepdims=True))).astype(jnp.bfloat16)
    mixed = jnp.einsum('hts,shd->thd', probabilities.astype(jnp.float32), value_heads)
    return mixed.astype(jnp.bfloat16).reshape(tokens_here, HEADS * HEAD_DIM)

def route_table(slots, weights, fetch_count, capacity):
    tokens_here = slots.shape[0]
    slot_ids = jnp.arange(fetch_count, dtype=jnp.int32)
    chosen = slots[:, :, None] == slot_ids[None, None, :]
    slot_weight = lax.optimization_barrier(jnp.sum(jnp.where(chosen, weights[:, :, None], 0.0), axis=1))
    is_used = jnp.any(chosen, axis=1)
    position = jnp.cumsum(is_used.astype(jnp.int32), axis=0) - 1
    target = jnp.where(is_used, slot_ids[None, :] * capacity + position, fetch_count * capacity).astype(jnp.int32)
    token_ids = jnp.broadcast_to(jnp.arange(tokens_here, dtype=jnp.int32)[:, None], (tokens_here, fetch_count))
    rows = jnp.zeros((fetch_count * capacity + 1,), jnp.int32).at[target.reshape(-1)].set(token_ids.reshape(-1))
    row_weight = jnp.zeros((fetch_count * capacity + 1,), weights.dtype).at[target.reshape(-1)].set(slot_weight.reshape(-1))
    return (rows[:-1].reshape(fetch_count, capacity), row_weight[:-1].reshape(fetch_count, capacity))

def sum_rounded(parts):
    rounded = lax.optimization_barrier(parts.astype(jnp.bfloat16))
    return lax.optimization_barrier(jnp.sum(rounded.astype(jnp.float32), axis=0))

def expert_block(routed_rows, routed_grad, row_weight, rows, gate_block, up_block, down_block):
    tokens_here = TOK_GROUP
    x_rows = routed_rows.astype(jnp.float32)
    gate_f = gate_block.astype(jnp.float32)
    up_f = up_block.astype(jnp.float32)
    down_f = down_block.astype(jnp.float32)
    pre_gate = jnp.einsum('fcd,fdh->fch', x_rows, gate_f)
    pre_up = jnp.einsum('fcd,fdh->fch', x_rows, up_f)
    sigmoid_gate = jax.nn.sigmoid(pre_gate)
    swish = pre_gate * sigmoid_gate
    activated = (swish * pre_up).astype(jnp.bfloat16)
    expert_out = jnp.einsum('fch,fhd->fcd', activated.astype(jnp.float32), down_f)
    flat_rows = rows.reshape(-1)
    out_part = jnp.zeros((tokens_here, D), jnp.float32).at[flat_rows].add((expert_out * row_weight[..., None]).reshape(-1, D))
    grad_rows = routed_grad.astype(jnp.float32)
    d_act = jnp.einsum('fcd,fhd->fch', grad_rows, down_f)
    d_gate = (d_act * pre_up * sigmoid_gate * (1.0 + pre_gate * (1.0 - sigmoid_gate))).astype(jnp.bfloat16)
    d_up = (d_act * swish).astype(jnp.bfloat16)
    grad_down_part = jnp.einsum('fch,fcd->fhd', activated.astype(jnp.float32), grad_rows).astype(jnp.bfloat16)
    grad_gate_part = jnp.einsum('fcd,fch->fdh', x_rows, d_gate.astype(jnp.float32)).astype(jnp.bfloat16)
    grad_up_part = jnp.einsum('fcd,fch->fdh', x_rows, d_up.astype(jnp.float32)).astype(jnp.bfloat16)
    d_rows = jnp.einsum('fch,fdh->fcd', d_gate.astype(jnp.float32), gate_f) + jnp.einsum('fch,fdh->fcd', d_up.astype(jnp.float32), up_f)
    input_part = jnp.zeros((tokens_here, D), jnp.float32).at[flat_rows].add(d_rows.reshape(-1, D))
    return (out_part, input_part, grad_gate_part, grad_up_part, grad_down_part)

def reference(queries, key_rows, value_rows, out_proj, residual, norm_gain, w_gate, w_up, w_down, route_slot, route_weight, fetch_list, cotangent):

    def by_group(array):
        return array.reshape((N_GROUP, TOK_GROUP) + array.shape[1:])
    head_cols = HEADS * HEAD_DIM // N_HIDDEN
    unit_block = FF // N_HIDDEN

    def one_group(carry, inputs):
        sum_gate, sum_up, sum_down = carry
        query_g, key_g, value_g, resid_g, slot_g, weight_g, cot_g, fetch_g = inputs
        mixed = attend(query_g, key_g, value_g)
        attn_parts = jnp.einsum('tnc,ncd->ntd', mixed.reshape(TOK_GROUP, N_HIDDEN, head_cols).astype(jnp.float32), out_proj.reshape(N_HIDDEN, head_cols, D).astype(jnp.float32))
        stream = resid_g.astype(jnp.float32) + sum_rounded(attn_parts)
        mean_square = lax.optimization_barrier(jnp.mean(stream * stream, axis=-1, keepdims=True))
        normed = (stream * lax.rsqrt(mean_square + epsilon) * norm_gain).astype(jnp.bfloat16)
        rows, row_weight = route_table(slot_g, weight_g, FETCH, CAP)
        routed_rows = normed[rows]
        routed_grad = (cot_g[rows].astype(jnp.float32) * row_weight[..., None]).astype(jnp.bfloat16)
        gate_sel = w_gate[fetch_g].reshape(FETCH, D, N_HIDDEN, unit_block).transpose(2, 0, 1, 3)
        up_sel = w_up[fetch_g].reshape(FETCH, D, N_HIDDEN, unit_block).transpose(2, 0, 1, 3)
        down_sel = w_down[fetch_g].reshape(FETCH, N_HIDDEN, unit_block, D).transpose(1, 0, 2, 3)

        def block_work(blocks):
            return expert_block(routed_rows, routed_grad, row_weight, rows, blocks[0], blocks[1], blocks[2])
        out_parts, input_parts, gate_parts, up_parts, down_parts = lax.map(block_work, (gate_sel, up_sel, down_sel))
        moe_out = sum_rounded(out_parts)
        grad_in = sum_rounded(input_parts)
        gate_full = gate_parts.transpose(1, 2, 0, 3).reshape(FETCH, D, FF)
        up_full = up_parts.transpose(1, 2, 0, 3).reshape(FETCH, D, FF)
        down_full = down_parts.transpose(1, 0, 2, 3).reshape(FETCH, FF, D)
        sum_gate = sum_gate.at[fetch_g].add(gate_full.astype(jnp.float32))
        sum_up = sum_up.at[fetch_g].add(up_full.astype(jnp.float32))
        sum_down = sum_down.at[fetch_g].add(down_full.astype(jnp.float32))
        outputs = ((stream + moe_out).astype(jnp.bfloat16), grad_in.astype(jnp.bfloat16))
        return ((sum_gate, sum_up, sum_down), outputs)
    start = (jnp.zeros((EXPERTS, D, FF), jnp.float32), jnp.zeros((EXPERTS, D, FF), jnp.float32), jnp.zeros((EXPERTS, FF, D), jnp.float32))
    inputs = (by_group(queries), by_group(key_rows), by_group(value_rows), by_group(residual), by_group(route_slot), by_group(route_weight), by_group(cotangent), fetch_list)
    sums, outputs = lax.scan(one_group, start, inputs)
    layer_out = outputs[0].reshape(TOKENS, D)
    grad_normed = outputs[1].reshape(TOKENS, D)
    return (layer_out, grad_normed, sums[0].astype(jnp.bfloat16), sums[1].astype(jnp.bfloat16), sums[2].astype(jnp.bfloat16))
```

```python
import functools
import math

import jax
import jax.numpy as jnp
from jax import lax
from jax.experimental import pallas as pl
from jax.experimental.pallas import tpu as pltpu
from jax.sharding import PartitionSpec as P

HEADS = 32
KV_HEADS = 4
HEAD_DIM = 128
EXP_GROUP = 8
FETCH = 16

epsilon = 1e-06


def attention_rows(query_in, key_block, value_block, heads_here):
    tokens_here = query_in.shape[0]
    query_heads = query_in.reshape(tokens_here, heads_here, HEAD_DIM)
    pos = jnp.arange(tokens_here, dtype=jnp.int32)
    scores = jnp.einsum(
        "thd,sd->hts", query_heads, key_block, preferred_element_type=jnp.float32
    ) / math.sqrt(HEAD_DIM)
    scores = jnp.where(pos[:, None] >= pos[None, :], scores, -1e30)
    row_peak = jnp.max(scores, axis=-1, keepdims=True)
    weights = jnp.exp(scores - row_peak)
    probabilities = (weights / jnp.sum(weights, axis=-1, keepdims=True)).astype(jnp.bfloat16)
    mixed = jnp.einsum("hts,sd->thd", probabilities, value_block, preferred_element_type=jnp.float32)
    return mixed.astype(jnp.bfloat16).reshape(tokens_here, heads_here * HEAD_DIM)


def dot(a, b, dims=((1,), (0,))):
    return lax.dot_general(a, b, (dims, ((), ())), preferred_element_type=jnp.float32)


def expert_kernel(per_owner, ids_ref, *refs):
    gates, refs = refs[:per_owner], refs[per_owner:]
    ups, refs = refs[:per_owner], refs[per_owner:]
    downs, refs = refs[:per_owner], refs[per_owner:]
    (
        y_ref, scale_ref,
        part_ref, gate_out, up_out, down_out,
        x2d, c2d, w_in, w_out, act, grads, act_turned, grads_turned, acc_gate, acc_up, acc_down, sems,
    ) = refs
    step = pl.program_id(0)
    blocks, width = y_ref.shape[1], y_ref.shape[4]
    tokens = x2d.shape[0]
    units = gates[0].shape[1]
    half = per_owner * units

    @pl.when(step == 0)
    def _():
        acc_gate[...] = jnp.zeros_like(acc_gate)
        acc_up[...] = jnp.zeros_like(acc_up)
        acc_down[...] = jnp.zeros_like(acc_down)

    for s in range(per_owner):
        w_in[s * units : (s + 1) * units, :] = gates[s][0]
        w_in[half + s * units : half + (s + 1) * units, :] = ups[s][0]
        w_out[s * units : (s + 1) * units, :] = downs[s][0]
    for h in range(blocks):
        x2d[:, h * width : (h + 1) * width] = y_ref[0, h, 0, :tokens]
        c2d[:, h * width : (h + 1) * width] = y_ref[0, h, 1, :tokens]

    scale = scale_ref[0]
    inverse = scale[:, per_owner : per_owner + 1]
    lane = lax.broadcasted_iota(jnp.int32, (tokens, half), 1)
    weight = jnp.broadcast_to(scale[:, :1], (tokens, half))
    for s in range(1, per_owner):
        weight = jnp.where(lane >= s * units, scale[:, s : s + 1], weight)
    turned = ((1,), (1,))
    pre_gate = dot(x2d[...], w_in[:half, :], turned) * inverse
    pre_up = dot(x2d[...], w_in[half:, :], turned) * inverse
    d_act = dot(c2d[...], w_out[...], turned) * weight
    sig = jax.nn.sigmoid(pre_gate)
    swish = pre_gate * sig
    weighted = swish * pre_up * weight
    d_gate = d_act * pre_up * sig * (1.0 + pre_gate * (1.0 - sig))
    d_up = d_act * swish
    act[...] = weighted.astype(act.dtype)
    grads[:, :half] = d_gate.astype(grads.dtype)
    grads[:, half:] = d_up.astype(grads.dtype)
    act_turned[...] = act[...].T
    grads_turned[:half, :] = (d_gate * inverse).astype(grads.dtype).T
    grads_turned[half:, :] = (d_up * inverse).astype(grads.dtype).T

    step_ids = [ids_ref[step * per_owner + s] for s in range(per_owner)]

    def add(acc, e, cols, value):
        acc[e, :, cols] = (acc[e, :, cols].astype(jnp.float32) + value).astype(acc.dtype)

    @pl.loop(0, blocks)
    def _(h):
        cols = pl.ds(pl.multiple_of(h * width, width), width)
        part_ref[0, h, 0] = dot(act[...], w_out[:, cols]).astype(part_ref.dtype)
        part_ref[0, h, 1] = dot(grads[...], w_in[:, cols]).astype(part_ref.dtype)
        down = dot(act_turned[...], c2d[:, cols])
        both = dot(grads_turned[...], x2d[:, cols])
        for s in range(per_owner):
            rows = slice(s * units, (s + 1) * units)
            add(acc_down, step_ids[s], cols, down[rows])
            add(acc_gate, step_ids[s], cols, both[rows])
            add(acc_up, step_ids[s], cols, both[half:][rows])

    @pl.when(step == pl.num_programs(0) - 1)
    def _():
        copies = [
            pltpu.make_async_copy(a, b, sems.at[i])
            for i, (a, b) in enumerate(
                ((acc_gate, gate_out), (acc_up, up_out), (acc_down, down_out))
            )
        ]
        for copy in copies:
            copy.start()
        for copy in copies:
            copy.wait()


def first_rows(count):
    return count // 24 * 16


def gather_kernel(groups, hidden, y_ref, out_ref, local_sem, send_sems, recv_sems):
    g, h = lax.axis_index("group"), lax.axis_index("hidden")
    chips = hidden // 2
    rows_all = y_ref.shape[1]
    cut = first_rows(rows_all)
    rows = (pl.ds(0, cut), pl.ds(cut, rows_all - cut))
    ahead = {"group": g, "hidden": lax.rem(h + 2, hidden)}
    behind = {"group": g, "hidden": lax.rem(h + hidden - 2, hidden)}
    partner = {"group": g, "hidden": h + 1 - 2 * lax.rem(h, 2)}
    peers = [{"group": lax.rem(g + k, groups), "hidden": h} for k in range(groups)]
    mesh_id = pl.DeviceIdType.MESH

    barrier = pltpu.get_barrier_semaphore()
    greeted = [ahead, behind, partner] + peers[1:]
    for device in greeted:
        pl.semaphore_signal(barrier, inc=1, device_id=device, device_id_type=mesh_id)
    pl.semaphore_wait(barrier, len(greeted))

    made = {}

    def send(key, source, g_from, h_from, part, device):
        number = len(made)
        target = out_ref.at[g_from, h_from, :, rows[part]]
        copy = pltpu.make_async_remote_copy(
            src_ref=target if source is None else source,
            dst_ref=target,
            send_sem=send_sems.at[number],
            recv_sem=recv_sems.at[number],
            device_id=device,
            device_id_type=mesh_id,
        )
        copy.start()
        made[key] = copy

    local = pltpu.make_async_copy(y_ref, out_ref.at[g, h], local_sem)
    local.start()
    own = [y_ref.at[:, rows[0]], y_ref.at[:, rows[1]]]
    group_of = [lax.rem(g + groups - k, groups) for k in range(groups)]
    hidden_of = [lax.rem(h + hidden - 2 * t, hidden) for t in range(chips)]
    send(("ring0", 1), own[0], g, h, 0, ahead)
    for k in range(1, groups):
        send(("peer1", 0, k), own[1], g, h, 1, peers[k])
    send(("ring1", 1, 0), own[1], g, h, 1, ahead)
    for k in range(1, groups):
        send(("peer0", 0, k), own[0], g, h, 0, peers[k])
    for part in range(2):
        send(("pair", part, 0, 0), own[part], g, h, part, partner)

    def arrive0(t):
        made[("ring0", t)].wait_recv()
        if t + 1 < chips:
            send(("ring0", t + 1), None, g, hidden_of[t], 0, ahead)
        for k in range(1, groups):
            send(("peer0", t, k), None, g, hidden_of[t], 0, peers[k])
        send(("pair", 0, t, 0), None, g, hidden_of[t], 0, partner)

    def arrive1(t, k):
        made[("ring1", t, k)].wait_recv()
        if t + 1 < chips:
            send(("ring1", t + 1, k), None, group_of[k], hidden_of[t], 1, ahead)
        send(("pair", 1, t, k), None, group_of[k], hidden_of[t], 1, partner)

    def arrive_peer(t, k):
        made[("peer0", t, k)].wait_recv()
        send(("pair", 0, t, k), None, group_of[k], hidden_of[t], 0, partner)

    arrive0(1)
    for k in range(1, groups):
        made[("peer1", 0, k)].wait_recv()
        send(("ring1", 1, k), None, group_of[k], h, 1, ahead)
        send(("pair", 1, 0, k), None, group_of[k], h, 1, partner)
    for t in range(1, chips):
        if t > 1:
            arrive0(t)
        for k in range(1, groups):
            arrive_peer(t - 1, k)
        for k in range(groups):
            arrive1(t, k)
    for k in range(1, groups):
        arrive_peer(chips - 1, k)
    for key, copy in made.items():
        if key[0] == "pair":
            copy.wait_recv()
        copy.wait_send()
    local.wait()


def gather_all(y, groups, hidden):
    chips = hidden // 2
    copies = (chips - 1) * (1 + groups) + (groups - 1) * (1 + chips) + 2 * chips * groups
    return pl.pallas_call(
        functools.partial(gather_kernel, groups, hidden),
        out_shape=jax.ShapeDtypeStruct((groups, hidden) + y.shape, y.dtype),
        in_specs=[pl.BlockSpec(memory_space=pltpu.VMEM)],
        out_specs=pl.BlockSpec(memory_space=pl.ANY),
        scratch_shapes=[
            pltpu.SemaphoreType.DMA,
            pltpu.SemaphoreType.DMA((copies,)),
            pltpu.SemaphoreType.DMA((copies,)),
        ],
        compiler_params=pltpu.CompilerParams(collective_id=0, has_side_effects=True),
        name="gather_all",
    )(y)


def reduce_kernel(
    groups, hidden, parts_ref, out_ref,
    own, pair_in, peer_in0, peer_in1, ring_in0, ring_in1, local_sems, send_sems, recv_sems,
):
    g, h = lax.axis_index("group"), lax.axis_index("hidden")
    chips = hidden // 2
    tokens = out_ref.shape[1]
    cut = first_rows(tokens)
    rows = (pl.ds(0, cut), pl.ds(cut, tokens - cut))
    ahead = {"group": g, "hidden": lax.rem(h + 2, hidden)}
    behind = {"group": g, "hidden": lax.rem(h + hidden - 2, hidden)}
    partner_h = h + 1 - 2 * lax.rem(h, 2)
    partner = {"group": g, "hidden": partner_h}
    group_of = [lax.rem(g + k, groups) for k in range(groups)]
    peers = [{"group": group_of[k], "hidden": h} for k in range(groups)]
    mesh_id = pl.DeviceIdType.MESH

    barrier = pltpu.get_barrier_semaphore()
    greeted = [ahead, behind, partner] + peers[1:]
    for device in greeted:
        pl.semaphore_signal(barrier, inc=1, device_id=device, device_id_type=mesh_id)
    pl.semaphore_wait(barrier, len(greeted))

    made = {}

    def send(key, source, target, device):
        number = len(made)
        copy = pltpu.make_async_remote_copy(
            src_ref=source,
            dst_ref=target,
            send_sem=send_sems.at[number],
            recv_sem=recv_sems.at[number],
            device_id=device,
            device_id_type=mesh_id,
        )
        copy.start()
        made[key] = copy

    def add(into, *others):
        total = into[...].astype(jnp.float32)
        for other in others:
            total = total + other[...].astype(jnp.float32)
        into[...] = total.astype(into.dtype)

    turns = list(range(1, chips)) + [0]
    loads = {}
    for t in turns:
        for k in range(groups):
            theirs = lax.rem(partner_h + hidden - 2 * t, hidden)
            send(("pair", t, k), parts_ref.at[group_of[k], theirs], pair_in.at[k, t], partner)
            mine = lax.rem(h + hidden - 2 * t, hidden)
            loads[t, k] = pltpu.make_async_copy(
                parts_ref.at[group_of[k], mine], own.at[k, t], local_sems.at[k * chips + t]
            )
            loads[t, k].start()

    def half(k, t, part):
        return own.at[k, t, :, rows[part]]

    last = chips - 1
    for t in turns:
        before = t - 1 if t else last
        for k in range(groups):
            loads[t, k].wait()
            made["pair", t, k].wait_recv()
            add(own.at[k, t], pair_in.at[k, t])
            if t == 1:
                send(("ring1", t, k), half(k, t, 1), ring_in1.at[t, k], ahead)
            if k:
                send(("peer0", t, k), half(k, t, 0), peer_in0.at[t, k], peers[k])
        if t != 1:
            for k in list(range(1, groups)) + [0]:
                made["ring1", before, k].wait_recv()
                add(half(k, t, 1), ring_in1.at[before, k])
                if t:
                    send(("ring1", t, k), half(k, t, 1), ring_in1.at[t, k], ahead)
                elif k:
                    send(("peer1", 0, k), half(k, t, 1), peer_in1.at[k], peers[k])
        arrived = []
        for k in range(1, groups):
            made["peer0", t, k].wait_recv()
            arrived.append(peer_in0.at[t, k])
        if t != 1:
            made["ring0", before].wait_recv()
            arrived.append(ring_in0.at[before])
        add(half(0, t, 0), *arrived)
        if t:
            send(("ring0", t), half(0, t, 0), ring_in0.at[t], ahead)
    for k in range(1, groups):
        made["peer1", 0, k].wait_recv()
    add(half(0, 0, 1), *[peer_in1.at[k] for k in range(1, groups)])
    out_ref[...] = own[0, 0]
    for copy in made.values():
        copy.wait_send()


def reduce_parts(parts, collective_id):
    groups, hidden, pieces, tokens, width = parts.shape
    chips = hidden // 2
    block = 2 * pieces * tokens * width
    if 3 * groups * chips * block > 40 << 20:
        flat = parts.reshape((groups * hidden,) + parts.shape[2:])
        return lax.psum_scatter(flat, ("group", "hidden"), scatter_dimension=0, tiled=True)[0]
    copies = (chips - 1) * (1 + groups) + (groups - 1) * (1 + chips) + chips * groups
    cut = first_rows(tokens)
    first, second = (pieces, cut, width), (pieces, tokens - cut, width)
    bf = parts.dtype
    return pl.pallas_call(
        functools.partial(reduce_kernel, groups, hidden),
        out_shape=jax.ShapeDtypeStruct(parts.shape[2:], bf),
        in_specs=[pl.BlockSpec(memory_space=pl.ANY)],
        out_specs=pl.BlockSpec(memory_space=pltpu.VMEM),
        scratch_shapes=[
            pltpu.VMEM((groups, chips) + parts.shape[2:], bf),
            pltpu.VMEM((groups, chips) + parts.shape[2:], bf),
            pltpu.VMEM((chips, groups) + first, bf),
            pltpu.VMEM((groups,) + second, bf),
            pltpu.VMEM((chips,) + first, bf),
            pltpu.VMEM((chips, groups) + second, bf),
            pltpu.SemaphoreType.DMA((chips * groups,)),
            pltpu.SemaphoreType.DMA((copies,)),
            pltpu.SemaphoreType.DMA((copies,)),
        ],
        compiler_params=pltpu.CompilerParams(
            collective_id=collective_id, has_side_effects=True, vmem_limit_bytes=40 << 20
        ),
        name=f"reduce_parts_{collective_id}",
    )(parts)


def to_rows(values, rows, width):
    high = lax.reduce_precision(values, 8, 7)
    rest = values - high
    mid = lax.reduce_precision(rest, 8, 7)
    flat = jnp.stack([high, mid, rest - mid]).reshape(-1).astype(jnp.bfloat16)
    return jnp.pad(flat, (0, rows * width - flat.shape[0])).reshape(rows, width)


def from_rows(block, count):
    flat = block.reshape(block.shape[:2] + (-1,))[:, :, : 3 * count].astype(jnp.float32)
    high, mid, low = (flat[:, :, i * count : (i + 1) * count] for i in range(3))
    return high + mid + low


def experts(order, ids, y, scale, w_gate, w_up, w_down):
    groups, blocks, _, rows, width = y.shape
    tokens = scale.shape[1]
    model = blocks * width
    per_owner = ids.shape[1]
    units = w_down.shape[1]
    half = per_owner * units
    ids_end = groups * per_owner

    def pick(s):
        return pl.BlockSpec((1, units, model), lambda k, n: (n[k * per_owner + s], 0, 0))

    bf = jnp.bfloat16
    parts = jax.ShapeDtypeStruct((groups, blocks, 2, tokens, width), bf)
    return pl.pallas_call(
        functools.partial(expert_kernel, per_owner),
        grid_spec=pltpu.PrefetchScalarGridSpec(
            num_scalar_prefetch=1,
            grid=(groups,),
            in_specs=[pick(s) for s in range(per_owner)] * 3
            + [
                pl.BlockSpec(
                    (1, blocks, 2, rows, width), lambda k, n: (n[ids_end + k], 0, 0, 0, 0)
                ),
                pl.BlockSpec(
                    (1, tokens, scale.shape[2]), lambda k, n: (n[ids_end + k], 0, 0)
                ),
            ],
            out_specs=[
                pl.BlockSpec((1,) + parts.shape[1:], lambda k, n: (n[ids_end + k], 0, 0, 0, 0)),
            ]
            + [pl.BlockSpec(memory_space=pl.ANY)] * 3,
            scratch_shapes=[
                pltpu.VMEM((tokens, model), bf),
                pltpu.VMEM((tokens, model), bf),
                pltpu.VMEM((2 * half, model), bf),
                pltpu.VMEM((half, model), bf),
                pltpu.VMEM((tokens, half), bf),
                pltpu.VMEM((tokens, 2 * half), bf),
                pltpu.VMEM((half, tokens), bf),
                pltpu.VMEM((2 * half, tokens), bf),
                pltpu.VMEM(w_down.shape, bf),
                pltpu.VMEM(w_down.shape, bf),
                pltpu.VMEM(w_down.shape, bf),
                pltpu.SemaphoreType.DMA((3,)),
            ],
        ),
        out_shape=[parts] + [jax.ShapeDtypeStruct(w_down.shape, bf)] * 3,
        compiler_params=pltpu.CompilerParams(vmem_limit_bytes=56 << 20),
        name="experts",
    )(
        jnp.concatenate([ids.reshape(-1), order]),
        *([w_gate] * per_owner + [w_up] * per_owner + [w_down] * per_owner),
        y,
        scale,
    )


def shards(
    queries,
    key_rows,
    value_rows,
    out_proj,
    residual,
    norm_gain,
    w_gate,
    w_up,
    w_down,
    route_slot,
    route_weight,
    fetch_list,
    cotangent,
):
    tokens_here, model = cotangent.shape
    hidden_index = lax.axis_index("hidden")
    hidden_count = lax.axis_size("hidden")
    group_index = lax.axis_index("group")
    group_count = lax.axis_size("group")
    per_owner = FETCH // group_count

    chosen = route_slot[:, :, None] == jnp.arange(FETCH, dtype=jnp.int32)[None, None, :]
    slot_weight = jnp.sum(jnp.where(chosen, route_weight[:, :, None], 0.0), axis=1)
    order = (group_index + jnp.arange(group_count, dtype=jnp.int32)) % group_count
    own_cols = lax.dynamic_slice_in_dim(fetch_list, group_index * per_owner, per_owner, 1)
    ids = jnp.take(own_cols - group_index * EXP_GROUP, order, axis=0)

    heads_here = queries.shape[1] // HEAD_DIM
    kv_index = hidden_index * heads_here // (HEADS // KV_HEADS)
    key_block = lax.dynamic_slice_in_dim(key_rows, kv_index * HEAD_DIM, HEAD_DIM, 1)
    value_block = lax.dynamic_slice_in_dim(value_rows, kv_index * HEAD_DIM, HEAD_DIM, 1)
    mixed = attention_rows(queries, key_block, value_block, heads_here)
    partial_value = jnp.dot(mixed, out_proj, preferred_element_type=jnp.float32)
    share_width = model // hidden_count
    first_col = hidden_index * share_width
    blocks = partial_value.astype(jnp.bfloat16).reshape(tokens_here, hidden_count, share_width)
    attn_share = reduce_parts(jnp.swapaxes(blocks, 0, 1)[None, :, None], 2)[0]
    stream = lax.dynamic_slice_in_dim(residual, first_col, share_width, 1).astype(
        jnp.float32
    ) + attn_share.astype(jnp.float32)
    gain = lax.dynamic_slice_in_dim(norm_gain, first_col, share_width, 0)
    squares = jnp.sum(stream * stream, axis=-1)
    gained = (stream * gain).astype(jnp.bfloat16)
    slots_here = FETCH // hidden_count
    slots = lax.dynamic_slice_in_dim(slot_weight.T, hidden_index * slots_here, slots_here, 0)
    extra = -(-3 * slots_here * tokens_here // (16 * share_width)) * 16
    cot_share = lax.dynamic_slice_in_dim(cotangent, first_col, share_width, 1)
    y = jnp.stack(
        [
            jnp.concatenate([gained, to_rows(squares, extra, share_width)]),
            jnp.concatenate([cot_share, to_rows(slots, extra, share_width)]),
        ]
    )
    y_all = gather_all(y, group_count, hidden_count)
    squares_all = from_rows(y_all[:, :, 0, tokens_here:], tokens_here).sum(axis=1)
    inverse = lax.rsqrt(squares_all / model + epsilon)
    weights = from_rows(y_all[:, :, 1, tokens_here:], slots_here * tokens_here)
    weights = weights.reshape(group_count, FETCH, tokens_here)
    weights = lax.dynamic_slice_in_dim(weights, group_index * per_owner, per_owner, 1)
    scale = jnp.concatenate([weights, inverse[:, None, :]], axis=1)
    scale = jnp.pad(scale, ((0, 0), (0, 8 - scale.shape[1]), (0, 0)))
    scale = jnp.swapaxes(scale, 1, 2)
    parts, grad_gate, grad_up, grad_down = experts(
        order,
        ids,
        y_all,
        scale,
        jnp.swapaxes(w_gate, 1, 2),
        jnp.swapaxes(w_up, 1, 2),
        w_down,
    )
    grad_gate = jnp.swapaxes(grad_gate, 1, 2)
    grad_up = jnp.swapaxes(grad_up, 1, 2)
    sums = reduce_parts(parts, 1)
    layer_out = (stream + sums[0].astype(jnp.float32)).astype(jnp.bfloat16)
    return (layer_out, sums[1], grad_gate, grad_up, grad_down)


def solution(mesh):
    return jax.shard_map(
        shards,
        mesh=mesh,
        in_specs=(
            P("group", "hidden"),
            P("group", None),
            P("group", None),
            P("hidden", None),
            P("group", None),
            P(),
            P("group", None, "hidden"),
            P("group", None, "hidden"),
            P("group", "hidden", None),
            P("group", None),
            P("group", None),
            P(),
            P("group", None),
        ),
        out_specs=(
            P("group", "hidden"),
            P("group", "hidden"),
            P("group", None, "hidden"),
            P("group", None, "hidden"),
            P("group", "hidden", None),
        ),
        check_vma=False,
    )
```

```python
import functools
import math

import jax
import jax.numpy as jnp
from jax import lax
from jax.experimental import pallas as pl
from jax.experimental.pallas import tpu as pltpu
from jax.sharding import PartitionSpec as P

HEADS = 32
KV_HEADS = 4
HEAD_DIM = 128
EXP_GROUP = 8
FETCH = 16

epsilon = 1e-06


def attention_rows(query_in, key_block, value_block, heads_here):
    tokens_here = query_in.shape[0]
    query_heads = query_in.reshape(tokens_here, heads_here, HEAD_DIM)
    pos = jnp.arange(tokens_here, dtype=jnp.int32)
    scores = jnp.einsum(
        "thd,sd->hts", query_heads, key_block, preferred_element_type=jnp.float32
    ) / math.sqrt(HEAD_DIM)
    scores = jnp.where(pos[:, None] >= pos[None, :], scores, -1e30)
    row_peak = jnp.max(scores, axis=-1, keepdims=True)
    weights = jnp.exp(scores - row_peak)
    probabilities = (weights / jnp.sum(weights, axis=-1, keepdims=True)).astype(jnp.bfloat16)
    mixed = jnp.einsum("hts,sd->thd", probabilities, value_block, preferred_element_type=jnp.float32)
    return mixed.astype(jnp.bfloat16).reshape(tokens_here, heads_here * HEAD_DIM)


def dot(a, b, dims=((1,), (0,))):
    return lax.dot_general(a, b, (dims, ((), ())), preferred_element_type=jnp.float32)


def expert_kernel(per_owner, ids_ref, *refs):
    gates, refs = refs[:per_owner], refs[per_owner:]
    ups, refs = refs[:per_owner], refs[per_owner:]
    downs, refs = refs[:per_owner], refs[per_owner:]
    (
        y_ref, scale_ref,
        part_ref, gate_out, up_out, down_out,
        x2d, c2d, w_in, w_out, act, grads, act_turned, grads_turned, acc_gate, acc_up, acc_down, sems,
    ) = refs
    step = pl.program_id(0)
    blocks, width = y_ref.shape[1], y_ref.shape[4]
    tokens = x2d.shape[0]
    units = gates[0].shape[1]
    half = per_owner * units

    @pl.when(step == 0)
    def _():
        acc_gate[...] = jnp.zeros_like(acc_gate)
        acc_up[...] = jnp.zeros_like(acc_up)
        acc_down[...] = jnp.zeros_like(acc_down)

    for s in range(per_owner):
        w_in[s * units : (s + 1) * units, :] = gates[s][0]
        w_in[half + s * units : half + (s + 1) * units, :] = ups[s][0]
        w_out[s * units : (s + 1) * units, :] = downs[s][0]
    for h in range(blocks):
        x2d[:, h * width : (h + 1) * width] = y_ref[0, h, 0, :tokens]
        c2d[:, h * width : (h + 1) * width] = y_ref[0, h, 1, :tokens]

    scale = scale_ref[0]
    inverse = scale[:, per_owner : per_owner + 1]
    lane = lax.broadcasted_iota(jnp.int32, (tokens, half), 1)
    weight = jnp.broadcast_to(scale[:, :1], (tokens, half))
    for s in range(1, per_owner):
        weight = jnp.where(lane >= s * units, scale[:, s : s + 1], weight)
    turned = ((1,), (1,))
    pre_gate = dot(x2d[...], w_in[:half, :], turned) * inverse
    pre_up = dot(x2d[...], w_in[half:, :], turned) * inverse
    d_act = dot(c2d[...], w_out[...], turned) * weight
    sig = jax.nn.sigmoid(pre_gate)
    swish = pre_gate * sig
    weighted = swish * pre_up * weight
    d_gate = d_act * pre_up * sig * (1.0 + pre_gate * (1.0 - sig))
    d_up = d_act * swish
    act[...] = weighted.astype(act.dtype)
    grads[:, :half] = d_gate.astype(grads.dtype)
    grads[:, half:] = d_up.astype(grads.dtype)
    act_turned[...] = act[...].T
    grads_turned[:half, :] = (d_gate * inverse).astype(grads.dtype).T
    grads_turned[half:, :] = (d_up * inverse).astype(grads.dtype).T

    step_ids = [ids_ref[step * per_owner + s] for s in range(per_owner)]

    def add(acc, e, cols, value):
        acc[e, :, cols] = (acc[e, :, cols].astype(jnp.float32) + value).astype(acc.dtype)

    @pl.loop(0, blocks)
    def _(h):
        cols = pl.ds(pl.multiple_of(h * width, width), width)
        part_ref[0, h, 0] = dot(act[...], w_out[:, cols]).astype(part_ref.dtype)
        part_ref[0, h, 1] = dot(grads[...], w_in[:, cols]).astype(part_ref.dtype)
        down = dot(act_turned[...], c2d[:, cols])
        both = dot(grads_turned[...], x2d[:, cols])
        for s in range(per_owner):
            rows = slice(s * units, (s + 1) * units)
            add(acc_down, step_ids[s], cols, down[rows])
            add(acc_gate, step_ids[s], cols, both[rows])
            add(acc_up, step_ids[s], cols, both[half:][rows])

    @pl.when(step == pl.num_programs(0) - 1)
    def _():
        copies = [
            pltpu.make_async_copy(a, b, sems.at[i])
            for i, (a, b) in enumerate(
                ((acc_gate, gate_out), (acc_up, up_out), (acc_down, down_out))
            )
        ]
        for copy in copies:
            copy.start()
        for copy in copies:
            copy.wait()


def first_rows(count):
    return count // 24 * 16


def gather_kernel(groups, hidden, y_ref, out_ref, local_sem, send_sems, recv_sems):
    g, h = lax.axis_index("group"), lax.axis_index("hidden")
    chips = hidden // 2
    rows_all = y_ref.shape[1]
    cut = first_rows(rows_all)
    rows = (pl.ds(0, cut), pl.ds(cut, rows_all - cut))
    ahead = {"group": g, "hidden": lax.rem(h + 2, hidden)}
    behind = {"group": g, "hidden": lax.rem(h + hidden - 2, hidden)}
    partner = {"group": g, "hidden": h + 1 - 2 * lax.rem(h, 2)}
    peers = [{"group": lax.rem(g + k, groups), "hidden": h} for k in range(groups)]
    mesh_id = pl.DeviceIdType.MESH

    barrier = pltpu.get_barrier_semaphore()
    greeted = [ahead, behind, partner] + peers[1:]
    for device in greeted:
        pl.semaphore_signal(barrier, inc=1, device_id=device, device_id_type=mesh_id)
    pl.semaphore_wait(barrier, len(greeted))

    made = {}

    def send(key, source, g_from, h_from, part, device):
        number = len(made)
        target = out_ref.at[g_from, h_from, :, rows[part]]
        copy = pltpu.make_async_remote_copy(
            src_ref=target if source is None else source,
            dst_ref=target,
            send_sem=send_sems.at[number],
            recv_sem=recv_sems.at[number],
            device_id=device,
            device_id_type=mesh_id,
        )
        copy.start()
        made[key] = copy

    local = pltpu.make_async_copy(y_ref, out_ref.at[g, h], local_sem)
    local.start()
    own = [y_ref.at[:, rows[0]], y_ref.at[:, rows[1]]]
    group_of = [lax.rem(g + groups - k, groups) for k in range(groups)]
    hidden_of = [lax.rem(h + hidden - 2 * t, hidden) for t in range(chips)]
    send(("ring0", 1), own[0], g, h, 0, ahead)
    for k in range(1, groups):
        send(("peer1", 0, k), own[1], g, h, 1, peers[k])
    send(("ring1", 1, 0), own[1], g, h, 1, ahead)
    for k in range(1, groups):
        send(("peer0", 0, k), own[0], g, h, 0, peers[k])
    for part in range(2):
        send(("pair", part, 0, 0), own[part], g, h, part, partner)

    def arrive0(t):
        made[("ring0", t)].wait_recv()
        if t + 1 < chips:
            send(("ring0", t + 1), None, g, hidden_of[t], 0, ahead)
        for k in range(1, groups):
            send(("peer0", t, k), None, g, hidden_of[t], 0, peers[k])
        send(("pair", 0, t, 0), None, g, hidden_of[t], 0, partner)

    def arrive1(t, k):
        made[("ring1", t, k)].wait_recv()
        if t + 1 < chips:
            send(("ring1", t + 1, k), None, group_of[k], hidden_of[t], 1, ahead)
        send(("pair", 1, t, k), None, group_of[k], hidden_of[t], 1, partner)

    def arrive_peer(t, k):
        made[("peer0", t, k)].wait_recv()
        send(("pair", 0, t, k), None, group_of[k], hidden_of[t], 0, partner)

    arrive0(1)
    for k in range(1, groups):
        made[("peer1", 0, k)].wait_recv()
        send(("ring1", 1, k), None, group_of[k], h, 1, ahead)
        send(("pair", 1, 0, k), None, group_of[k], h, 1, partner)
    for t in range(1, chips):
        if t > 1:
            arrive0(t)
        for k in range(1, groups):
            arrive_peer(t - 1, k)
        for k in range(groups):
            arrive1(t, k)
    for k in range(1, groups):
        arrive_peer(chips - 1, k)
    for key, copy in made.items():
        if key[0] == "pair":
            copy.wait_recv()
        copy.wait_send()
    local.wait()


def gather_all(y, groups, hidden):
    chips = hidden // 2
    copies = (chips - 1) * (1 + groups) + (groups - 1) * (1 + chips) + 2 * chips * groups
    return pl.pallas_call(
        functools.partial(gather_kernel, groups, hidden),
        out_shape=jax.ShapeDtypeStruct((groups, hidden) + y.shape, y.dtype),
        in_specs=[pl.BlockSpec(memory_space=pltpu.VMEM)],
        out_specs=pl.BlockSpec(memory_space=pl.ANY),
        scratch_shapes=[
            pltpu.SemaphoreType.DMA,
            pltpu.SemaphoreType.DMA((copies,)),
            pltpu.SemaphoreType.DMA((copies,)),
        ],
        compiler_params=pltpu.CompilerParams(collective_id=0, has_side_effects=True),
        name="gather_all",
    )(y)


def reduce_kernel(
    groups, hidden, parts_ref, out_ref,
    own, pair_in, peer_in0, peer_in1, ring_in0, ring_in1, local_sems, send_sems, recv_sems,
):
    g, h = lax.axis_index("group"), lax.axis_index("hidden")
    chips = hidden // 2
    tokens = out_ref.shape[1]
    cut = first_rows(tokens)
    rows = (pl.ds(0, cut), pl.ds(cut, tokens - cut))
    ahead = {"group": g, "hidden": lax.rem(h + 2, hidden)}
    behind = {"group": g, "hidden": lax.rem(h + hidden - 2, hidden)}
    partner_h = h + 1 - 2 * lax.rem(h, 2)
    partner = {"group": g, "hidden": partner_h}
    group_of = [lax.rem(g + k, groups) for k in range(groups)]
    peers = [{"group": group_of[k], "hidden": h} for k in range(groups)]
    mesh_id = pl.DeviceIdType.MESH

    barrier = pltpu.get_barrier_semaphore()
    greeted = [ahead, behind, partner] + peers[1:]
    for device in greeted:
        pl.semaphore_signal(barrier, inc=1, device_id=device, device_id_type=mesh_id)
    pl.semaphore_wait(barrier, len(greeted))

    made = {}

    def send(key, source, target, device):
        number = len(made)
        copy = pltpu.make_async_remote_copy(
            src_ref=source,
            dst_ref=target,
            send_sem=send_sems.at[number],
            recv_sem=recv_sems.at[number],
            device_id=device,
            device_id_type=mesh_id,
        )
        copy.start()
        made[key] = copy

    def add(into, *others):
        total = into[...].astype(jnp.float32)
        for other in others:
            total = total + other[...].astype(jnp.float32)
        into[...] = total.astype(into.dtype)

    turns = list(range(1, chips)) + [0]
    loads = {}
    for t in turns:
        for k in range(groups):
            theirs = lax.rem(partner_h + hidden - 2 * t, hidden)
            send(("pair", t, k), parts_ref.at[group_of[k], theirs], pair_in.at[k, t], partner)
            mine = lax.rem(h + hidden - 2 * t, hidden)
            loads[t, k] = pltpu.make_async_copy(
                parts_ref.at[group_of[k], mine], own.at[k, t], local_sems.at[k * chips + t]
            )
            loads[t, k].start()

    def half(k, t, part):
        return own.at[k, t, :, rows[part]]

    last = chips - 1
    for t in turns:
        before = t - 1 if t else last
        for k in range(groups):
            loads[t, k].wait()
            made["pair", t, k].wait_recv()
            add(own.at[k, t], pair_in.at[k, t])
            if t == 1:
                send(("ring1", t, k), half(k, t, 1), ring_in1.at[t, k], ahead)
            if k:
                send(("peer0", t, k), half(k, t, 0), peer_in0.at[t, k], peers[k])
        if t != 1:
            for k in list(range(1, groups)) + [0]:
                made["ring1", before, k].wait_recv()
                add(half(k, t, 1), ring_in1.at[before, k])
                if t:
                    send(("ring1", t, k), half(k, t, 1), ring_in1.at[t, k], ahead)
                elif k:
                    send(("peer1", 0, k), half(k, t, 1), peer_in1.at[k], peers[k])
        arrived = []
        for k in range(1, groups):
            made["peer0", t, k].wait_recv()
            arrived.append(peer_in0.at[t, k])
        if t != 1:
            made["ring0", before].wait_recv()
            arrived.append(ring_in0.at[before])
        add(half(0, t, 0), *arrived)
        if t:
            send(("ring0", t), half(0, t, 0), ring_in0.at[t], ahead)
    for k in range(1, groups):
        made["peer1", 0, k].wait_recv()
    add(half(0, 0, 1), *[peer_in1.at[k] for k in range(1, groups)])
    out_ref[...] = own[0, 0]
    for copy in made.values():
        copy.wait_send()


def reduce_parts(parts, collective_id):
    groups, hidden, pieces, tokens, width = parts.shape
    chips = hidden // 2
    block = 2 * pieces * tokens * width
    if 3 * groups * chips * block > 40 << 20:
        flat = parts.reshape((groups * hidden,) + parts.shape[2:])
        return lax.psum_scatter(flat, ("group", "hidden"), scatter_dimension=0, tiled=True)[0]
    copies = (chips - 1) * (1 + groups) + (groups - 1) * (1 + chips) + chips * groups
    cut = first_rows(tokens)
    first, second = (pieces, cut, width), (pieces, tokens - cut, width)
    bf = parts.dtype
    return pl.pallas_call(
        functools.partial(reduce_kernel, groups, hidden),
        out_shape=jax.ShapeDtypeStruct(parts.shape[2:], bf),
        in_specs=[pl.BlockSpec(memory_space=pl.ANY)],
        out_specs=pl.BlockSpec(memory_space=pltpu.VMEM),
        scratch_shapes=[
            pltpu.VMEM((groups, chips) + parts.shape[2:], bf),
            pltpu.VMEM((groups, chips) + parts.shape[2:], bf),
            pltpu.VMEM((chips, groups) + first, bf),
            pltpu.VMEM((groups,) + second, bf),
            pltpu.VMEM((chips,) + first, bf),
            pltpu.VMEM((chips, groups) + second, bf),
            pltpu.SemaphoreType.DMA((chips * groups,)),
            pltpu.SemaphoreType.DMA((copies,)),
            pltpu.SemaphoreType.DMA((copies,)),
        ],
        compiler_params=pltpu.CompilerParams(
            collective_id=collective_id, has_side_effects=True, vmem_limit_bytes=40 << 20
        ),
        name=f"reduce_parts_{collective_id}",
    )(parts)


def to_rows(values, rows, width):
    high = lax.reduce_precision(values, 8, 7)
    rest = values - high
    mid = lax.reduce_precision(rest, 8, 7)
    flat = jnp.stack([high, mid, rest - mid]).reshape(-1).astype(jnp.bfloat16)
    return jnp.pad(flat, (0, rows * width - flat.shape[0])).reshape(rows, width)


def from_rows(block, count):
    flat = block.reshape(block.shape[:2] + (-1,))[:, :, : 3 * count].astype(jnp.float32)
    high, mid, low = (flat[:, :, i * count : (i + 1) * count] for i in range(3))
    return high + mid + low


def experts(order, ids, y, scale, w_gate, w_up, w_down):
    groups, blocks, _, rows, width = y.shape
    tokens = scale.shape[1]
    model = blocks * width
    per_owner = ids.shape[1]
    units = w_down.shape[1]
    half = per_owner * units
    ids_end = groups * per_owner

    def pick(s):
        return pl.BlockSpec((1, units, model), lambda k, n: (n[k * per_owner + s], 0, 0))

    bf = jnp.bfloat16
    parts = jax.ShapeDtypeStruct((groups, blocks, 2, tokens, width), bf)
    return pl.pallas_call(
        functools.partial(expert_kernel, per_owner),
        grid_spec=pltpu.PrefetchScalarGridSpec(
            num_scalar_prefetch=1,
            grid=(groups,),
            in_specs=[pick(s) for s in range(per_owner)] * 3
            + [
                pl.BlockSpec(
                    (1, blocks, 2, rows, width), lambda k, n: (n[ids_end + k], 0, 0, 0, 0)
                ),
                pl.BlockSpec(
                    (1, tokens, scale.shape[2]), lambda k, n: (n[ids_end + k], 0, 0)
                ),
            ],
            out_specs=[
                pl.BlockSpec((1,) + parts.shape[1:], lambda k, n: (n[ids_end + k], 0, 0, 0, 0)),
            ]
            + [pl.BlockSpec(memory_space=pl.ANY)] * 3,
            scratch_shapes=[
                pltpu.VMEM((tokens, model), bf),
                pltpu.VMEM((tokens, model), bf),
                pltpu.VMEM((2 * half, model), bf),
                pltpu.VMEM((half, model), bf),
                pltpu.VMEM((tokens, half), bf),
                pltpu.VMEM((tokens, 2 * half), bf),
                pltpu.VMEM((half, tokens), bf),
                pltpu.VMEM((2 * half, tokens), bf),
                pltpu.VMEM(w_down.shape, bf),
                pltpu.VMEM(w_down.shape, bf),
                pltpu.VMEM(w_down.shape, bf),
                pltpu.SemaphoreType.DMA((3,)),
            ],
        ),
        out_shape=[parts] + [jax.ShapeDtypeStruct(w_down.shape, bf)] * 3,
        compiler_params=pltpu.CompilerParams(vmem_limit_bytes=56 << 20),
        name="experts",
    )(
        jnp.concatenate([ids.reshape(-1), order]),
        *([w_gate] * per_owner + [w_up] * per_owner + [w_down] * per_owner),
        y,
        scale,
    )


def pair_groups(g, i):
    across, along = 1 - i // 2, 1 - lax.rem(i, 2)
    gx, gy = lax.rem(g, 2), g // 2
    return lax.rem(gy + along, 2) * 2 + lax.rem(gx + across, 2)


def fused_kernel(
    groups, hidden, per_owner,
    ids_ref, seat_ref, y_ref, scale_ref, gate_ref, up_ref, down_ref,
    out_ref, gate_out, up_out, down_out,
    w_gate, w_up, w_down, xs, cs, w_in, w_out, act, grads, act_turned, grads_turned,
    slot_gate, slot_up, slot_down, acc_gate, acc_up, acc_down,
    own, stage, pair_in, peer_in0, peer_in1, ring_in0, ring_in1,
    load_sems, fetch_sems, pair_sems, ring1_sems, peer0_sems, peer1_sems, ring0_sems,
):
    g, h = lax.axis_index("group"), lax.axis_index("hidden")
    chips = hidden // 2
    owned, units, model = w_gate.shape
    tokens, width = out_ref.shape[1], out_ref.shape[2]
    half = per_owner * units
    last, final = chips - 1, groups - 1
    cut = first_rows(tokens)
    rows = (pl.ds(0, cut), pl.ds(cut, tokens - cut))
    ahead = {"group": g, "hidden": lax.rem(h + 2, hidden)}
    behind = {"group": g, "hidden": lax.rem(h + hidden - 2, hidden)}
    partner_h = h + 1 - 2 * lax.rem(h, 2)
    partner = {"group": g, "hidden": partner_h}
    mesh_id = pl.DeviceIdType.MESH

    def peer(i):
        return {"group": pair_groups(g, i), "hidden": h}

    barrier = pltpu.get_barrier_semaphore()
    greeted = [ahead, behind, partner] + [peer(i) for i in range(final)]
    for device in greeted:
        pl.semaphore_signal(barrier, inc=1, device_id=device, device_id_type=mesh_id)

    loads = [
        pltpu.make_async_copy(a, b, load_sems.at[n])
        for n, (a, b) in enumerate(((gate_ref, w_gate), (up_ref, w_up), (down_ref, w_down)))
    ]
    stores = [
        pltpu.make_async_copy(a, b, load_sems.at[n])
        for n, (a, b) in enumerate(((acc_gate, gate_out), (acc_up, up_out), (acc_down, down_out)))
    ]

    def fetches(i):
        slot = lax.rem(i, 2)
        source = pair_groups(g, i)
        copies = []
        for b in range(hidden):
            for p, target in enumerate((xs, cs)):
                copies.append(
                    pltpu.make_async_copy(
                        y_ref.at[source, b, p, pl.ds(0, tokens)],
                        target.at[slot, :, pl.ds(b * width, width)],
                        fetch_sems.at[slot, p, b],
                    )
                )
        return copies

    for copy in fetches(0):
        copy.start()
    for copy in loads:
        copy.start()

    acc_gate[...] = jnp.zeros_like(acc_gate)
    acc_up[...] = jnp.zeros_like(acc_up)
    acc_down[...] = jnp.zeros_like(acc_down)
    for buffer in (slot_gate, slot_up, slot_down):
        buffer[per_owner] = jnp.zeros(buffer.shape[1:], buffer.dtype)

    def remote(source, target, sems, index, device):
        return pltpu.make_async_remote_copy(
            src_ref=source,
            dst_ref=target,
            send_sem=sems.at[(0,) + index],
            recv_sem=sems.at[(1,) + index],
            device_id=device,
            device_id_type=mesh_id,
        )

    def part_of(i, t, part):
        return own.at[i, t, :, rows[part]]

    def pair_copy(i, t):
        return remote(stage.at[i, t], pair_in.at[i, t], pair_sems, (i, t), partner)

    def ring1_copy(i, t):
        return remote(part_of(i, t, 1), ring_in1.at[i, t], ring1_sems, (i, t), ahead)

    def peer0_copy(i, t):
        return remote(part_of(i, t, 0), peer_in0.at[i, t], peer0_sems, (i, t), peer(i))

    def peer1_copy(i):
        return remote(part_of(i, 0, 1), peer_in1.at[i], peer1_sems, (i,), peer(i))

    def ring0_copy(t):
        return remote(part_of(final, t, 0), ring_in0.at[t], ring0_sems, (t,), ahead)

    def add(into, *others):
        total = into[...].astype(jnp.float32)
        for other in others:
            total = total + other[...].astype(jnp.float32)
        into[...] = total.astype(into.dtype)

    def pair_task(i, t):
        pair_copy(i, t).wait_recv()
        add(own.at[i, t], pair_in.at[i, t])

        @pl.when(t == 1)
        def _():
            ring1_copy(i, t).start()

        @pl.when(i < final)
        def _():
            peer0_copy(i, t).start()

    def ring_task(i, t):
        before = t - 1 if t else last
        ring1_copy(i, before).wait_recv()
        add(part_of(i, t, 1), ring_in1.at[i, before])
        if t:
            ring1_copy(i, t).start()

    def finish_task(t):
        arrived = []
        for i in range(final):
            peer0_copy(i, t).wait_recv()
            arrived.append(peer_in0.at[i, t])
        if t != 1:
            before = t - 1 if t else last
            ring0_copy(before).wait_recv()
            arrived.append(ring_in0.at[before])
        add(part_of(final, t, 0), *arrived)
        if t:
            ring0_copy(t).start()

    pl.semaphore_wait(barrier, len(greeted))
    for copy in loads:
        copy.wait()

    turned = ((1,), (1,))

    @pl.loop(0, groups)
    def _(i):
        slot = lax.rem(i, 2)
        group = pair_groups(g, i)

        @pl.when(i < final)
        def _():
            for copy in fetches(i + 1):
                copy.start()

        for s in range(per_owner):
            e = ids_ref[group * per_owner + s]
            w_in[s * units : (s + 1) * units, :] = w_gate[e]
            w_in[half + s * units : half + (s + 1) * units, :] = w_up[e]
            w_out[s * units : (s + 1) * units, :] = w_down[e]
        scale = scale_ref[group]
        inverse = scale[:, per_owner : per_owner + 1]
        lane = lax.broadcasted_iota(jnp.int32, (tokens, half), 1)
        weight = jnp.broadcast_to(scale[:, :1], (tokens, half))
        for s in range(1, per_owner):
            weight = jnp.where(lane >= s * units, scale[:, s : s + 1], weight)
        for copy in fetches(i):
            copy.wait()
        pre_gate = dot(xs[slot], w_in[:half, :], turned) * inverse
        pre_up = dot(xs[slot], w_in[half:, :], turned) * inverse
        d_act = dot(cs[slot], w_out[...], turned) * weight
        sig = jax.nn.sigmoid(pre_gate)
        swish = pre_gate * sig
        weighted = swish * pre_up * weight
        d_gate = d_act * pre_up * sig * (1.0 + pre_gate * (1.0 - sig))
        d_up = d_act * swish
        act[...] = weighted.astype(act.dtype)
        grads[:, :half] = d_gate.astype(grads.dtype)
        grads[:, half:] = d_up.astype(grads.dtype)
        act_turned[...] = act[...].T
        grads_turned[:half, :] = (d_gate * inverse).astype(grads.dtype).T
        grads_turned[half:, :] = (d_up * inverse).astype(grads.dtype).T

        @pl.loop(0, chips)
        def _(j):
            t = lax.rem(j + 1, chips)
            back = hidden - 2 * t
            for whose, target in ((partner_h, stage), (h, own)):
                first = pl.multiple_of(lax.rem(whose + back, hidden) * width, width)
                cols = pl.ds(first, width)
                target[i, t, 0] = dot(act[...], w_out[:, cols]).astype(target.dtype)
                target[i, t, 1] = dot(grads[...], w_in[:, cols]).astype(target.dtype)
                if whose is partner_h:
                    pair_copy(i, t).start()

            @pl.when(j > 0)
            def _():
                pair_task(i, j)

            @pl.when((i > 0) & (j == 1))
            def _():
                ring_task(i - 1, 0)
                peer1_copy(i - 1).start()

        pair_task(i, 0)
        ring_task(i, 2)

        @pl.when(i == final)
        def _():
            finish_task(1)

        @pl.loop(0, hidden)
        def _(b):
            cols = pl.ds(pl.multiple_of(b * width, width), width)
            down = dot(act_turned[...], cs[slot, :, cols])
            both = dot(grads_turned[...], xs[slot, :, cols])
            for s in range(per_owner):
                slot_down[s] = down[s * units : (s + 1) * units]
                slot_gate[s] = both[s * units : (s + 1) * units]
                slot_up[s] = both[half + s * units : half + (s + 1) * units]
            for e in range(owned):
                seat = seat_ref[group * owned + e]
                for total, value in ((acc_down, slot_down), (acc_gate, slot_gate), (acc_up, slot_up)):
                    total[e, :, cols] = (total[e, :, cols].astype(jnp.float32) + value[seat]).astype(
                        total.dtype
                    )

        ring_task(i, 3)

    for copy in stores:
        copy.start()
    finish_task(2)
    ring_task(final, 0)
    finish_task(3)
    finish_task(0)
    for i in range(final):
        peer1_copy(i).wait_recv()
    add(part_of(final, 0, 1), *[peer_in1.at[i] for i in range(final)])
    out_ref[...] = own[final, 0]
    for i in range(groups):
        for t in range(chips):
            pair_copy(i, t).wait_send()
            if t:
                ring1_copy(i, t).wait_send()
            if i < final:
                peer0_copy(i, t).wait_send()
    for i in range(final):
        peer1_copy(i).wait_send()
    for t in range(1, chips):
        ring0_copy(t).wait_send()
    for copy in stores:
        copy.wait()


def fused_experts(ids, seats, y, scale, w_gate, w_up, w_down, hidden):
    groups = y.shape[0]
    width = y.shape[4]
    tokens = scale.shape[1]
    chips = hidden // 2
    owned, units, model = w_down.shape
    per_owner = ids.shape[0] // groups
    half = per_owner * units
    cut = first_rows(tokens)
    first, second = (2, cut, width), (2, tokens - cut, width)
    block = (2, tokens, width)
    bf = jnp.bfloat16
    anywhere = pl.BlockSpec(memory_space=pl.ANY)
    scalars = pl.BlockSpec(memory_space=pltpu.SMEM)
    dma = pltpu.SemaphoreType.DMA
    return pl.pallas_call(
        functools.partial(fused_kernel, groups, hidden, per_owner),
        in_specs=[scalars, scalars, anywhere, pl.BlockSpec(memory_space=pltpu.VMEM)] + [anywhere] * 3,
        out_specs=[pl.BlockSpec(memory_space=pltpu.VMEM)] + [anywhere] * 3,
        out_shape=[jax.ShapeDtypeStruct(block, bf)] + [jax.ShapeDtypeStruct(w_down.shape, bf)] * 3,
        scratch_shapes=[pltpu.VMEM(w_down.shape, bf)] * 3
        + [
            pltpu.VMEM((2, tokens, model), bf),
            pltpu.VMEM((2, tokens, model), bf),
            pltpu.VMEM((2 * half, model), bf),
            pltpu.VMEM((half, model), bf),
            pltpu.VMEM((tokens, half), bf),
            pltpu.VMEM((tokens, 2 * half), bf),
            pltpu.VMEM((half, tokens), bf),
            pltpu.VMEM((2 * half, tokens), bf),
        ]
        + [pltpu.VMEM((per_owner + 1, units, width), jnp.float32)] * 3
        + [pltpu.VMEM(w_down.shape, bf)] * 3
        + [
            pltpu.VMEM((groups, chips) + block, bf),
            pltpu.VMEM((groups, chips) + block, bf),
            pltpu.VMEM((groups, chips) + block, bf),
            pltpu.VMEM((groups - 1, chips) + first, bf),
            pltpu.VMEM((groups - 1,) + second, bf),
            pltpu.VMEM((chips,) + first, bf),
            pltpu.VMEM((groups, chips) + second, bf),
            dma((3,)),
            dma((2, 2, hidden)),
            dma((2, groups, chips)),
            dma((2, groups, chips)),
            dma((2, groups - 1, chips)),
            dma((2, groups - 1)),
            dma((2, chips)),
        ],
        compiler_params=pltpu.CompilerParams(
            collective_id=1, has_side_effects=True, vmem_limit_bytes=63 << 20
        ),
        name="fused_experts",
    )(ids, seats, y, scale, w_gate, w_up, w_down)


def shards(
    queries,
    key_rows,
    value_rows,
    out_proj,
    residual,
    norm_gain,
    w_gate,
    w_up,
    w_down,
    route_slot,
    route_weight,
    fetch_list,
    cotangent,
):
    tokens_here, model = cotangent.shape
    hidden_index = lax.axis_index("hidden")
    hidden_count = lax.axis_size("hidden")
    group_index = lax.axis_index("group")
    group_count = lax.axis_size("group")
    per_owner = FETCH // group_count

    chosen = route_slot[:, :, None] == jnp.arange(FETCH, dtype=jnp.int32)[None, None, :]
    slot_weight = jnp.sum(jnp.where(chosen, route_weight[:, :, None], 0.0), axis=1)
    order = (group_index + jnp.arange(group_count, dtype=jnp.int32)) % group_count
    own_cols = lax.dynamic_slice_in_dim(fetch_list, group_index * per_owner, per_owner, 1)
    ids = jnp.take(own_cols - group_index * EXP_GROUP, order, axis=0)

    heads_here = queries.shape[1] // HEAD_DIM
    kv_index = hidden_index * heads_here // (HEADS // KV_HEADS)
    key_block = lax.dynamic_slice_in_dim(key_rows, kv_index * HEAD_DIM, HEAD_DIM, 1)
    value_block = lax.dynamic_slice_in_dim(value_rows, kv_index * HEAD_DIM, HEAD_DIM, 1)
    mixed = attention_rows(queries, key_block, value_block, heads_here)
    partial_value = jnp.dot(mixed, out_proj, preferred_element_type=jnp.float32)
    share_width = model // hidden_count
    first_col = hidden_index * share_width
    blocks = partial_value.astype(jnp.bfloat16).reshape(tokens_here, hidden_count, share_width)
    attn_share = reduce_parts(jnp.swapaxes(blocks, 0, 1)[None, :, None], 2)[0]
    stream = lax.dynamic_slice_in_dim(residual, first_col, share_width, 1).astype(
        jnp.float32
    ) + attn_share.astype(jnp.float32)
    gain = lax.dynamic_slice_in_dim(norm_gain, first_col, share_width, 0)
    squares = jnp.sum(stream * stream, axis=-1)
    gained = (stream * gain).astype(jnp.bfloat16)
    slots_here = FETCH // hidden_count
    slots = lax.dynamic_slice_in_dim(slot_weight.T, hidden_index * slots_here, slots_here, 0)
    extra = -(-3 * slots_here * tokens_here // (16 * share_width)) * 16
    cot_share = lax.dynamic_slice_in_dim(cotangent, first_col, share_width, 1)
    y = jnp.stack(
        [
            jnp.concatenate([gained, to_rows(squares, extra, share_width)]),
            jnp.concatenate([cot_share, to_rows(slots, extra, share_width)]),
        ]
    )
    y_all = gather_all(y, group_count, hidden_count)
    squares_all = from_rows(y_all[:, :, 0, tokens_here:], tokens_here).sum(axis=1)
    inverse = lax.rsqrt(squares_all / model + epsilon)
    weights = from_rows(y_all[:, :, 1, tokens_here:], slots_here * tokens_here)
    weights = weights.reshape(group_count, FETCH, tokens_here)
    weights = lax.dynamic_slice_in_dim(weights, group_index * per_owner, per_owner, 1)
    scale = jnp.concatenate([weights, inverse[:, None, :]], axis=1)
    scale = jnp.pad(scale, ((0, 0), (0, 8 - scale.shape[1]), (0, 0)))
    scale = jnp.swapaxes(scale, 1, 2)
    weights_here = (jnp.swapaxes(w_gate, 1, 2), jnp.swapaxes(w_up, 1, 2), w_down)
    if group_count == 4:
        listed = own_cols - group_index * EXP_GROUP
        same = listed[:, :, None] == jnp.arange(EXP_GROUP, dtype=jnp.int32)
        place = jnp.arange(per_owner, dtype=jnp.int32)[None, :, None] - per_owner
        seats = per_owner + jnp.sum(jnp.where(same, place, 0), axis=1)
        sums, grad_gate, grad_up, grad_down = fused_experts(
            listed.reshape(-1), seats.reshape(-1), y_all, scale, *weights_here, hidden_count
        )
    else:
        parts, grad_gate, grad_up, grad_down = experts(order, ids, y_all, scale, *weights_here)
        sums = reduce_parts(parts, 1)
    grad_gate = jnp.swapaxes(grad_gate, 1, 2)
    grad_up = jnp.swapaxes(grad_up, 1, 2)
    layer_out = (stream + sums[0].astype(jnp.float32)).astype(jnp.bfloat16)
    return (layer_out, sums[1], grad_gate, grad_up, grad_down)


def solution(mesh):
    return jax.shard_map(
        shards,
        mesh=mesh,
        in_specs=(
            P("group", "hidden"),
            P("group", None),
            P("group", None),
            P("hidden", None),
            P("group", None),
            P(),
            P("group", None, "hidden"),
            P("group", None, "hidden"),
            P("group", "hidden", None),
            P("group", None),
            P("group", None),
            P(),
            P("group", None),
        ),
        out_specs=(
            P("group", "hidden"),
            P("group", "hidden"),
            P("group", None, "hidden"),
            P("group", None, "hidden"),
            P("group", "hidden", None),
        ),
        check_vma=False,
    )
```

```python
import functools
import math

import jax
import jax.numpy as jnp
from jax import lax
from jax.experimental import pallas as pl
from jax.experimental.pallas import tpu as pltpu
from jax.sharding import PartitionSpec as P

HEADS = 32
KV_HEADS = 4
HEAD_DIM = 128
EXP_GROUP = 8
FETCH = 16

epsilon = 1e-06


def attention_rows(query_in, key_block, value_block, heads_here):
    tokens_here = query_in.shape[0]
    query_heads = query_in.reshape(tokens_here, heads_here, HEAD_DIM)
    pos = jnp.arange(tokens_here, dtype=jnp.int32)
    scores = jnp.einsum(
        "thd,sd->hts", query_heads, key_block, preferred_element_type=jnp.float32
    ) / math.sqrt(HEAD_DIM)
    scores = jnp.where(pos[:, None] >= pos[None, :], scores, -1e30)
    row_peak = jnp.max(scores, axis=-1, keepdims=True)
    weights = jnp.exp(scores - row_peak)
    probabilities = (weights / jnp.sum(weights, axis=-1, keepdims=True)).astype(jnp.bfloat16)
    mixed = jnp.einsum("hts,sd->thd", probabilities, value_block, preferred_element_type=jnp.float32)
    return mixed.astype(jnp.bfloat16).reshape(tokens_here, heads_here * HEAD_DIM)


def dot(a, b, dims=((1,), (0,))):
    return lax.dot_general(a, b, (dims, ((), ())), preferred_element_type=jnp.float32)


def expert_kernel(per_owner, ids_ref, *refs):
    gates, refs = refs[:per_owner], refs[per_owner:]
    ups, refs = refs[:per_owner], refs[per_owner:]
    downs, refs = refs[:per_owner], refs[per_owner:]
    (
        y_ref, scale_ref,
        part_ref, gate_out, up_out, down_out,
        x2d, c2d, w_in, w_out, act, grads, act_turned, grads_turned, acc_gate, acc_up, acc_down, sems,
    ) = refs
    step = pl.program_id(0)
    blocks, width = y_ref.shape[1], y_ref.shape[4]
    tokens = x2d.shape[0]
    units = gates[0].shape[1]
    half = per_owner * units

    @pl.when(step == 0)
    def _():
        acc_gate[...] = jnp.zeros_like(acc_gate)
        acc_up[...] = jnp.zeros_like(acc_up)
        acc_down[...] = jnp.zeros_like(acc_down)

    for s in range(per_owner):
        w_in[s * units : (s + 1) * units, :] = gates[s][0]
        w_in[half + s * units : half + (s + 1) * units, :] = ups[s][0]
        w_out[s * units : (s + 1) * units, :] = downs[s][0]
    for h in range(blocks):
        x2d[:, h * width : (h + 1) * width] = y_ref[0, h, 0, :tokens]
        c2d[:, h * width : (h + 1) * width] = y_ref[0, h, 1, :tokens]

    scale = scale_ref[0]
    inverse = scale[:, per_owner : per_owner + 1]
    lane = lax.broadcasted_iota(jnp.int32, (tokens, half), 1)
    weight = jnp.broadcast_to(scale[:, :1], (tokens, half))
    for s in range(1, per_owner):
        weight = jnp.where(lane >= s * units, scale[:, s : s + 1], weight)
    turned = ((1,), (1,))
    pre_gate = dot(x2d[...], w_in[:half, :], turned) * inverse
    pre_up = dot(x2d[...], w_in[half:, :], turned) * inverse
    d_act = dot(c2d[...], w_out[...], turned) * weight
    sig = jax.nn.sigmoid(pre_gate)
    swish = pre_gate * sig
    weighted = swish * pre_up * weight
    d_gate = d_act * pre_up * sig * (1.0 + pre_gate * (1.0 - sig))
    d_up = d_act * swish
    act[...] = weighted.astype(act.dtype)
    grads[:, :half] = d_gate.astype(grads.dtype)
    grads[:, half:] = d_up.astype(grads.dtype)
    act_turned[...] = act[...].T
    grads_turned[:half, :] = (d_gate * inverse).astype(grads.dtype).T
    grads_turned[half:, :] = (d_up * inverse).astype(grads.dtype).T

    step_ids = [ids_ref[step * per_owner + s] for s in range(per_owner)]

    def add(acc, e, cols, value):
        acc[e, :, cols] = (acc[e, :, cols].astype(jnp.float32) + value).astype(acc.dtype)

    @pl.loop(0, blocks)
    def _(h):
        cols = pl.ds(pl.multiple_of(h * width, width), width)
        part_ref[0, h, 0] = dot(act[...], w_out[:, cols]).astype(part_ref.dtype)
        part_ref[0, h, 1] = dot(grads[...], w_in[:, cols]).astype(part_ref.dtype)
        down = dot(act_turned[...], c2d[:, cols])
        both = dot(grads_turned[...], x2d[:, cols])
        for s in range(per_owner):
            rows = slice(s * units, (s + 1) * units)
            add(acc_down, step_ids[s], cols, down[rows])
            add(acc_gate, step_ids[s], cols, both[rows])
            add(acc_up, step_ids[s], cols, both[half:][rows])

    @pl.when(step == pl.num_programs(0) - 1)
    def _():
        copies = [
            pltpu.make_async_copy(a, b, sems.at[i])
            for i, (a, b) in enumerate(
                ((acc_gate, gate_out), (acc_up, up_out), (acc_down, down_out))
            )
        ]
        for copy in copies:
            copy.start()
        for copy in copies:
            copy.wait()


def first_rows(count):
    return count // 24 * 16


def gather_kernel(groups, hidden, y_ref, out_ref, local_sem, send_sems, recv_sems):
    g, h = lax.axis_index("group"), lax.axis_index("hidden")
    chips = hidden // 2
    rows_all = y_ref.shape[1]
    cut = first_rows(rows_all)
    rows = (pl.ds(0, cut), pl.ds(cut, rows_all - cut))
    ahead = {"group": g, "hidden": lax.rem(h + 2, hidden)}
    behind = {"group": g, "hidden": lax.rem(h + hidden - 2, hidden)}
    partner = {"group": g, "hidden": h + 1 - 2 * lax.rem(h, 2)}
    peers = [{"group": lax.rem(g + k, groups), "hidden": h} for k in range(groups)]
    mesh_id = pl.DeviceIdType.MESH

    barrier = pltpu.get_barrier_semaphore()
    greeted = [ahead, behind, partner] + peers[1:]
    for device in greeted:
        pl.semaphore_signal(barrier, inc=1, device_id=device, device_id_type=mesh_id)
    pl.semaphore_wait(barrier, len(greeted))

    made = {}

    def send(key, source, g_from, h_from, part, device):
        number = len(made)
        target = out_ref.at[g_from, h_from, :, rows[part]]
        copy = pltpu.make_async_remote_copy(
            src_ref=target if source is None else source,
            dst_ref=target,
            send_sem=send_sems.at[number],
            recv_sem=recv_sems.at[number],
            device_id=device,
            device_id_type=mesh_id,
        )
        copy.start()
        made[key] = copy

    local = pltpu.make_async_copy(y_ref, out_ref.at[g, h], local_sem)
    local.start()
    own = [y_ref.at[:, rows[0]], y_ref.at[:, rows[1]]]
    group_of = [lax.rem(g + groups - k, groups) for k in range(groups)]
    hidden_of = [lax.rem(h + hidden - 2 * t, hidden) for t in range(chips)]
    send(("ring0", 1), own[0], g, h, 0, ahead)
    for k in range(1, groups):
        send(("peer1", 0, k), own[1], g, h, 1, peers[k])
    send(("ring1", 1, 0), own[1], g, h, 1, ahead)
    for k in range(1, groups):
        send(("peer0", 0, k), own[0], g, h, 0, peers[k])
    for part in range(2):
        send(("pair", part, 0, 0), own[part], g, h, part, partner)

    def arrive0(t):
        made[("ring0", t)].wait_recv()
        if t + 1 < chips:
            send(("ring0", t + 1), None, g, hidden_of[t], 0, ahead)
        for k in range(1, groups):
            send(("peer0", t, k), None, g, hidden_of[t], 0, peers[k])
        send(("pair", 0, t, 0), None, g, hidden_of[t], 0, partner)

    def arrive1(t, k):
        made[("ring1", t, k)].wait_recv()
        if t + 1 < chips:
            send(("ring1", t + 1, k), None, group_of[k], hidden_of[t], 1, ahead)
        send(("pair", 1, t, k), None, group_of[k], hidden_of[t], 1, partner)

    def arrive_peer(t, k):
        made[("peer0", t, k)].wait_recv()
        send(("pair", 0, t, k), None, group_of[k], hidden_of[t], 0, partner)

    arrive0(1)
    for k in range(1, groups):
        made[("peer1", 0, k)].wait_recv()
        send(("ring1", 1, k), None, group_of[k], h, 1, ahead)
        send(("pair", 1, 0, k), None, group_of[k], h, 1, partner)
    for t in range(1, chips):
        if t > 1:
            arrive0(t)
        for k in range(1, groups):
            arrive_peer(t - 1, k)
        for k in range(groups):
            arrive1(t, k)
    for k in range(1, groups):
        arrive_peer(chips - 1, k)
    for key, copy in made.items():
        if key[0] == "pair":
            copy.wait_recv()
        copy.wait_send()
    local.wait()


def gather_all(y, groups, hidden):
    chips = hidden // 2
    copies = (chips - 1) * (1 + groups) + (groups - 1) * (1 + chips) + 2 * chips * groups
    return pl.pallas_call(
        functools.partial(gather_kernel, groups, hidden),
        out_shape=jax.ShapeDtypeStruct((groups, hidden) + y.shape, y.dtype),
        in_specs=[pl.BlockSpec(memory_space=pltpu.VMEM)],
        out_specs=pl.BlockSpec(memory_space=pl.ANY),
        scratch_shapes=[
            pltpu.SemaphoreType.DMA,
            pltpu.SemaphoreType.DMA((copies,)),
            pltpu.SemaphoreType.DMA((copies,)),
        ],
        compiler_params=pltpu.CompilerParams(collective_id=0, has_side_effects=True),
        name="gather_all",
    )(y)


def reduce_kernel(
    groups, hidden, parts_ref, out_ref,
    own, pair_in, peer_in0, peer_in1, ring_in0, ring_in1, local_sems, send_sems, recv_sems,
):
    g, h = lax.axis_index("group"), lax.axis_index("hidden")
    chips = hidden // 2
    tokens = out_ref.shape[1]
    cut = first_rows(tokens)
    rows = (pl.ds(0, cut), pl.ds(cut, tokens - cut))
    ahead = {"group": g, "hidden": lax.rem(h + 2, hidden)}
    behind = {"group": g, "hidden": lax.rem(h + hidden - 2, hidden)}
    partner_h = h + 1 - 2 * lax.rem(h, 2)
    partner = {"group": g, "hidden": partner_h}
    group_of = [lax.rem(g + k, groups) for k in range(groups)]
    peers = [{"group": group_of[k], "hidden": h} for k in range(groups)]
    mesh_id = pl.DeviceIdType.MESH

    barrier = pltpu.get_barrier_semaphore()
    greeted = [ahead, behind, partner] + peers[1:]
    for device in greeted:
        pl.semaphore_signal(barrier, inc=1, device_id=device, device_id_type=mesh_id)
    pl.semaphore_wait(barrier, len(greeted))

    made = {}

    def send(key, source, target, device):
        number = len(made)
        copy = pltpu.make_async_remote_copy(
            src_ref=source,
            dst_ref=target,
            send_sem=send_sems.at[number],
            recv_sem=recv_sems.at[number],
            device_id=device,
            device_id_type=mesh_id,
        )
        copy.start()
        made[key] = copy

    def add(into, *others):
        total = into[...].astype(jnp.float32)
        for other in others:
            total = total + other[...].astype(jnp.float32)
        into[...] = total.astype(into.dtype)

    turns = list(range(1, chips)) + [0]
    loads = {}
    for t in turns:
        for k in range(groups):
            theirs = lax.rem(partner_h + hidden - 2 * t, hidden)
            send(("pair", t, k), parts_ref.at[group_of[k], theirs], pair_in.at[k, t], partner)
            mine = lax.rem(h + hidden - 2 * t, hidden)
            loads[t, k] = pltpu.make_async_copy(
                parts_ref.at[group_of[k], mine], own.at[k, t], local_sems.at[k * chips + t]
            )
            loads[t, k].start()

    def half(k, t, part):
        return own.at[k, t, :, rows[part]]

    last = chips - 1
    for t in turns:
        before = t - 1 if t else last
        for k in range(groups):
            loads[t, k].wait()
            made["pair", t, k].wait_recv()
            add(own.at[k, t], pair_in.at[k, t])
            if t == 1:
                send(("ring1", t, k), half(k, t, 1), ring_in1.at[t, k], ahead)
            if k:
                send(("peer0", t, k), half(k, t, 0), peer_in0.at[t, k], peers[k])
        if t != 1:
            for k in list(range(1, groups)) + [0]:
                made["ring1", before, k].wait_recv()
                add(half(k, t, 1), ring_in1.at[before, k])
                if t:
                    send(("ring1", t, k), half(k, t, 1), ring_in1.at[t, k], ahead)
                elif k:
                    send(("peer1", 0, k), half(k, t, 1), peer_in1.at[k], peers[k])
        arrived = []
        for k in range(1, groups):
            made["peer0", t, k].wait_recv()
            arrived.append(peer_in0.at[t, k])
        if t != 1:
            made["ring0", before].wait_recv()
            arrived.append(ring_in0.at[before])
        add(half(0, t, 0), *arrived)
        if t:
            send(("ring0", t), half(0, t, 0), ring_in0.at[t], ahead)
    for k in range(1, groups):
        made["peer1", 0, k].wait_recv()
    add(half(0, 0, 1), *[peer_in1.at[k] for k in range(1, groups)])
    out_ref[...] = own[0, 0]
    for copy in made.values():
        copy.wait_send()


def reduce_parts(parts, collective_id):
    groups, hidden, pieces, tokens, width = parts.shape
    chips = hidden // 2
    block = 2 * pieces * tokens * width
    if 3 * groups * chips * block > 40 << 20:
        flat = parts.reshape((groups * hidden,) + parts.shape[2:])
        return lax.psum_scatter(flat, ("group", "hidden"), scatter_dimension=0, tiled=True)[0]
    copies = (chips - 1) * (1 + groups) + (groups - 1) * (1 + chips) + chips * groups
    cut = first_rows(tokens)
    first, second = (pieces, cut, width), (pieces, tokens - cut, width)
    bf = parts.dtype
    return pl.pallas_call(
        functools.partial(reduce_kernel, groups, hidden),
        out_shape=jax.ShapeDtypeStruct(parts.shape[2:], bf),
        in_specs=[pl.BlockSpec(memory_space=pl.ANY)],
        out_specs=pl.BlockSpec(memory_space=pltpu.VMEM),
        scratch_shapes=[
            pltpu.VMEM((groups, chips) + parts.shape[2:], bf),
            pltpu.VMEM((groups, chips) + parts.shape[2:], bf),
            pltpu.VMEM((chips, groups) + first, bf),
            pltpu.VMEM((groups,) + second, bf),
            pltpu.VMEM((chips,) + first, bf),
            pltpu.VMEM((chips, groups) + second, bf),
            pltpu.SemaphoreType.DMA((chips * groups,)),
            pltpu.SemaphoreType.DMA((copies,)),
            pltpu.SemaphoreType.DMA((copies,)),
        ],
        compiler_params=pltpu.CompilerParams(
            collective_id=collective_id, has_side_effects=True, vmem_limit_bytes=40 << 20
        ),
        name=f"reduce_parts_{collective_id}",
    )(parts)


def to_rows(values, rows, width):
    high = lax.reduce_precision(values, 8, 7)
    rest = values - high
    mid = lax.reduce_precision(rest, 8, 7)
    flat = jnp.stack([high, mid, rest - mid]).reshape(-1).astype(jnp.bfloat16)
    return jnp.pad(flat, (0, rows * width - flat.shape[0])).reshape(rows, width)


def from_rows(block, count):
    flat = block.reshape(block.shape[:2] + (-1,))[:, :, : 3 * count].astype(jnp.float32)
    high, mid, low = (flat[:, :, i * count : (i + 1) * count] for i in range(3))
    return high + mid + low


def experts(order, ids, y, scale, w_gate, w_up, w_down):
    groups, blocks, _, rows, width = y.shape
    tokens = scale.shape[1]
    model = blocks * width
    per_owner = ids.shape[1]
    units = w_down.shape[1]
    half = per_owner * units
    ids_end = groups * per_owner

    def pick(s):
        return pl.BlockSpec((1, units, model), lambda k, n: (n[k * per_owner + s], 0, 0))

    bf = jnp.bfloat16
    parts = jax.ShapeDtypeStruct((groups, blocks, 2, tokens, width), bf)
    return pl.pallas_call(
        functools.partial(expert_kernel, per_owner),
        grid_spec=pltpu.PrefetchScalarGridSpec(
            num_scalar_prefetch=1,
            grid=(groups,),
            in_specs=[pick(s) for s in range(per_owner)] * 3
            + [
                pl.BlockSpec(
                    (1, blocks, 2, rows, width), lambda k, n: (n[ids_end + k], 0, 0, 0, 0)
                ),
                pl.BlockSpec(
                    (1, tokens, scale.shape[2]), lambda k, n: (n[ids_end + k], 0, 0)
                ),
            ],
            out_specs=[
                pl.BlockSpec((1,) + parts.shape[1:], lambda k, n: (n[ids_end + k], 0, 0, 0, 0)),
            ]
            + [pl.BlockSpec(memory_space=pl.ANY)] * 3,
            scratch_shapes=[
                pltpu.VMEM((tokens, model), bf),
                pltpu.VMEM((tokens, model), bf),
                pltpu.VMEM((2 * half, model), bf),
                pltpu.VMEM((half, model), bf),
                pltpu.VMEM((tokens, half), bf),
                pltpu.VMEM((tokens, 2 * half), bf),
                pltpu.VMEM((half, tokens), bf),
                pltpu.VMEM((2 * half, tokens), bf),
                pltpu.VMEM(w_down.shape, bf),
                pltpu.VMEM(w_down.shape, bf),
                pltpu.VMEM(w_down.shape, bf),
                pltpu.SemaphoreType.DMA((3,)),
            ],
        ),
        out_shape=[parts] + [jax.ShapeDtypeStruct(w_down.shape, bf)] * 3,
        compiler_params=pltpu.CompilerParams(vmem_limit_bytes=56 << 20),
        name="experts",
    )(
        jnp.concatenate([ids.reshape(-1), order]),
        *([w_gate] * per_owner + [w_up] * per_owner + [w_down] * per_owner),
        y,
        scale,
    )


def pair_groups(g, i):
    across, along = 1 - i // 2, 1 - lax.rem(i, 2)
    gx, gy = lax.rem(g, 2), g // 2
    return lax.rem(gy + along, 2) * 2 + lax.rem(gx + across, 2)


def fused_kernel(
    groups, hidden, per_owner,
    ids_ref, seat_ref, y_ref, scale_ref, gate_ref, up_ref, down_ref,
    out_ref, gate_out, up_out, down_out,
    w_gate, w_up, w_down, xs, cs, w_in, w_out, act, grads, act_turned, grads_turned,
    slot_gate, slot_up, slot_down,
    own, stage, pair_in, diag_in, peer_in0, peer_in1, ring_in0, ring_in1,
    load_sems, fetch_sems, pair_sems, ring1_sems, diag_sems, peer0_sems, peer1_sems, ring0_sems,
):
    g, h = lax.axis_index("group"), lax.axis_index("hidden")
    chips = hidden // 2
    owned, units, model = w_gate.shape
    tokens, width = out_ref.shape[1], out_ref.shape[2]
    half = per_owner * units
    last, final = chips - 1, groups - 1
    cut = first_rows(tokens)
    rows = (pl.ds(0, cut), pl.ds(cut, tokens - cut))
    via = (pl.ds(0, cut // 2), pl.ds(cut // 2, cut // 2))
    ahead = {"group": g, "hidden": lax.rem(h + 2, hidden)}
    behind = {"group": g, "hidden": lax.rem(h + hidden - 2, hidden)}
    partner_h = h + 1 - 2 * lax.rem(h, 2)
    partner = {"group": g, "hidden": partner_h}
    mesh_id = pl.DeviceIdType.MESH

    def peer(i):
        return {"group": pair_groups(g, i), "hidden": h}

    barrier = pltpu.get_barrier_semaphore()
    greeted = [ahead, behind, partner] + [peer(i) for i in range(final)]
    for device in greeted:
        pl.semaphore_signal(barrier, inc=1, device_id=device, device_id_type=mesh_id)

    loads = [
        pltpu.make_async_copy(a, b, load_sems.at[n])
        for n, (a, b) in enumerate(((gate_ref, w_gate), (up_ref, w_up), (down_ref, w_down)))
    ]
    stores = [
        pltpu.make_async_copy(a, b, load_sems.at[n])
        for n, (a, b) in enumerate(((w_gate, gate_out), (w_up, up_out), (w_down, down_out)))
    ]

    def fetches(i):
        slot = lax.rem(i, 2)
        source = pair_groups(g, i)
        copies = []
        for b in range(hidden):
            for p, target in enumerate((xs, cs)):
                copies.append(
                    pltpu.make_async_copy(
                        y_ref.at[source, b, p, pl.ds(0, tokens)],
                        target.at[slot, :, pl.ds(b * width, width)],
                        fetch_sems.at[slot, p, b],
                    )
                )
        return copies

    for copy in fetches(0):
        copy.start()
    for copy in loads:
        copy.start()

    for buffer in (slot_gate, slot_up, slot_down):
        buffer[per_owner] = jnp.zeros(buffer.shape[1:], buffer.dtype)

    def remote(source, target, sems, index, device):
        return pltpu.make_async_remote_copy(
            src_ref=source,
            dst_ref=target,
            send_sem=sems.at[(0,) + index],
            recv_sem=sems.at[(1,) + index],
            device_id=device,
            device_id_type=mesh_id,
        )

    def part_of(i, t, part):
        return own.at[i, t, :, rows[part]]

    def pair_copy(i, t):
        return remote(stage.at[i, t], pair_in.at[i, t], pair_sems, (i, t), partner)

    def ring1_copy(i, t):
        return remote(part_of(i, t, 1), ring_in1.at[i, t], ring1_sems, (i, t), ahead)

    def diag_copy(n, t):
        source = own.at[0, t, :, via[n]]
        return remote(source, diag_in.at[n, t], diag_sems, (n, t), peer(n + 1))

    def peer0_copy(i, t):
        return remote(part_of(i, t, 0), peer_in0.at[i - 1, t], peer0_sems, (i - 1, t), peer(i))

    def peer1_copy(i):
        return remote(part_of(i, 0, 1), peer_in1.at[i], peer1_sems, (i,), peer(i))

    def ring0_copy(t):
        return remote(part_of(final, t, 0), ring_in0.at[t], ring0_sems, (t,), ahead)

    def add(into, *others):
        total = into[...].astype(jnp.float32)
        for other in others:
            total = total + other[...].astype(jnp.float32)
        into[...] = total.astype(into.dtype)

    def pair_task(i, t):
        pair_copy(i, t).wait_recv()
        add(own.at[i, t], pair_in.at[i, t])

        @pl.when(t == 1)
        def _():
            ring1_copy(i, t).start()

        @pl.when(i == 0)
        def _():
            for n in range(2):
                diag_copy(n, t).start()

        for n, step in ((1, 1), (0, 2)):

            @pl.when(i == step)
            def _():
                diag_copy(n, t).wait_recv()
                add(own.at[step, t, :, via[n]], diag_in.at[n, t])
                peer0_copy(step, t).start()

    def ring_task(i, t):
        before = t - 1 if t else last
        ring1_copy(i, before).wait_recv()
        add(part_of(i, t, 1), ring_in1.at[i, before])
        if t:
            ring1_copy(i, t).start()

    def finish_task(t):
        arrived = []
        for i in range(1, final):
            peer0_copy(i, t).wait_recv()
            arrived.append(peer_in0.at[i - 1, t])
        if t != 1:
            before = t - 1 if t else last
            ring0_copy(before).wait_recv()
            arrived.append(ring_in0.at[before])
        add(part_of(final, t, 0), *arrived)
        if t:
            ring0_copy(t).start()

    pl.semaphore_wait(barrier, len(greeted))
    for copy in loads:
        copy.wait()

    turned = ((1,), (1,))

    @pl.loop(0, groups)
    def _(i):
        slot = lax.rem(i, 2)
        group = pair_groups(g, i)

        @pl.when(i < final)
        def _():
            for copy in fetches(i + 1):
                copy.start()

        for s in range(per_owner):
            e = ids_ref[group * per_owner + s]
            w_in[s * units : (s + 1) * units, :] = w_gate[e]
            w_in[half + s * units : half + (s + 1) * units, :] = w_up[e]
            w_out[s * units : (s + 1) * units, :] = w_down[e]
        scale = scale_ref[group]
        inverse = scale[:, per_owner : per_owner + 1]
        lane = lax.broadcasted_iota(jnp.int32, (tokens, half), 1)
        weight = jnp.broadcast_to(scale[:, :1], (tokens, half))
        for s in range(1, per_owner):
            weight = jnp.where(lane >= s * units, scale[:, s : s + 1], weight)
        for copy in fetches(i):
            copy.wait()
        pre_gate = dot(xs[slot], w_in[:half, :], turned) * inverse
        pre_up = dot(xs[slot], w_in[half:, :], turned) * inverse
        d_act = dot(cs[slot], w_out[...], turned) * weight
        sig = jax.nn.sigmoid(pre_gate)
        swish = pre_gate * sig
        weighted = swish * pre_up * weight
        d_gate = d_act * pre_up * sig * (1.0 + pre_gate * (1.0 - sig))
        d_up = d_act * swish
        act[...] = weighted.astype(act.dtype)
        grads[:, :half] = d_gate.astype(grads.dtype)
        grads[:, half:] = d_up.astype(grads.dtype)
        act_turned[i] = act[...].T
        grads_turned[i, :half, :] = (d_gate * inverse).astype(grads.dtype).T
        grads_turned[i, half:, :] = (d_up * inverse).astype(grads.dtype).T

        @pl.when(i > 0)
        def _():
            ring_task(i - 1, 2)

        @pl.when(i > 1)
        def _():
            ring_task(i - 2, 0)
            peer1_copy(i - 2).start()

        @pl.loop(0, chips)
        def _(j):
            t = lax.rem(j + 1, chips)
            back = hidden - 2 * t
            for whose, target in ((partner_h, stage), (h, own)):
                first = pl.multiple_of(lax.rem(whose + back, hidden) * width, width)
                cols = pl.ds(first, width)
                target[i, t, 0] = dot(act[...], w_out[:, cols]).astype(target.dtype)
                target[i, t, 1] = dot(grads[...], w_in[:, cols]).astype(target.dtype)
                if whose is partner_h:
                    pair_copy(i, t).start()

            @pl.when(j > 0)
            def _():
                pair_task(i, j)

        pair_task(i, 0)

        @pl.when(i > 0)
        def _():
            ring_task(i - 1, 3)

    for buffer in (w_gate, w_up, w_down):
        buffer[...] = jnp.zeros_like(buffer)

    def finish_last():
        for i in range(final):
            peer1_copy(i).wait_recv()
        add(part_of(final, 0, 1), *[peer_in1.at[i] for i in range(final)])

    def finish_ring():
        ring_task(final - 1, 0)
        peer1_copy(final - 1).start()

    tasks = (
        (2, lambda: ring_task(final, 2)),
        (3, lambda: finish_task(1)),
        (6, finish_ring),
        (9, lambda: ring_task(final, 3)),
        (13, lambda: finish_task(2)),
        (16, lambda: ring_task(final, 0)),
        (23, lambda: finish_task(3)),
    )

    @pl.loop(0, groups * hidden)
    def _(n):
        i, b = final - n // hidden, lax.rem(n, hidden)
        slot = lax.rem(i, 2)
        group = pair_groups(g, i)

        @pl.when((b == 0) & (n > 0) & (i > 0))
        def _():
            for copy in fetches(i - 1):
                copy.start()

        @pl.when((b == 0) & (i < final - 1))
        def _():
            for copy in fetches(i):
                copy.wait()

        cols = pl.ds(pl.multiple_of(b * width, width), width)
        down = dot(act_turned[i], cs[slot, :, cols])
        both = dot(grads_turned[i], xs[slot, :, cols])
        for s in range(per_owner):
            slot_down[s] = down[s * units : (s + 1) * units]
            slot_gate[s] = both[s * units : (s + 1) * units]
            slot_up[s] = both[half + s * units : half + (s + 1) * units]
        for e in range(owned):
            seat = seat_ref[group * owned + e]
            for total, value in ((w_down, slot_down), (w_gate, slot_gate), (w_up, slot_up)):
                total[e, :, cols] = (total[e, :, cols].astype(jnp.float32) + value[seat]).astype(
                    total.dtype
                )
        for at, task in tasks:
            pl.when(n == at)(task)

    for copy in stores:
        copy.start()
    finish_task(0)
    finish_last()
    out_ref[...] = own[final, 0]
    for i in range(groups):
        for t in range(chips):
            pair_copy(i, t).wait_send()
            if t:
                ring1_copy(i, t).wait_send()
            if 0 < i < final:
                peer0_copy(i, t).wait_send()
    for t in range(chips):
        for n in range(2):
            diag_copy(n, t).wait_send()
    for i in range(final):
        peer1_copy(i).wait_send()
    for t in range(1, chips):
        ring0_copy(t).wait_send()
    for copy in stores:
        copy.wait()


def fused_experts(ids, seats, y, scale, w_gate, w_up, w_down, hidden):
    groups = y.shape[0]
    width = y.shape[4]
    tokens = scale.shape[1]
    chips = hidden // 2
    owned, units, model = w_down.shape
    per_owner = ids.shape[0] // groups
    half = per_owner * units
    cut = first_rows(tokens)
    first, second = (2, cut, width), (2, tokens - cut, width)
    block = (2, tokens, width)
    bf = jnp.bfloat16
    anywhere = pl.BlockSpec(memory_space=pl.ANY)
    scalars = pl.BlockSpec(memory_space=pltpu.SMEM)
    dma = pltpu.SemaphoreType.DMA
    return pl.pallas_call(
        functools.partial(fused_kernel, groups, hidden, per_owner),
        in_specs=[scalars, scalars, anywhere, pl.BlockSpec(memory_space=pltpu.VMEM)] + [anywhere] * 3,
        out_specs=[pl.BlockSpec(memory_space=pltpu.VMEM)] + [anywhere] * 3,
        out_shape=[jax.ShapeDtypeStruct(block, bf)] + [jax.ShapeDtypeStruct(w_down.shape, bf)] * 3,
        scratch_shapes=[pltpu.VMEM(w_down.shape, bf)] * 3
        + [
            pltpu.VMEM((2, tokens, model), bf),
            pltpu.VMEM((2, tokens, model), bf),
            pltpu.VMEM((2 * half, model), bf),
            pltpu.VMEM((half, model), bf),
            pltpu.VMEM((tokens, half), bf),
            pltpu.VMEM((tokens, 2 * half), bf),
            pltpu.VMEM((groups, half, tokens), bf),
            pltpu.VMEM((groups, 2 * half, tokens), bf),
        ]
        + [pltpu.VMEM((per_owner + 1, units, width), jnp.float32)] * 3
        + [
            pltpu.VMEM((groups, chips) + block, bf),
            pltpu.VMEM((groups, chips) + block, bf),
            pltpu.VMEM((groups, chips) + block, bf),
            pltpu.VMEM((2, chips, 2, cut // 2, width), bf),
            pltpu.VMEM((groups - 2, chips) + first, bf),
            pltpu.VMEM((groups - 1,) + second, bf),
            pltpu.VMEM((chips,) + first, bf),
            pltpu.VMEM((groups, chips) + second, bf),
            dma((3,)),
            dma((2, 2, hidden)),
            dma((2, groups, chips)),
            dma((2, groups, chips)),
            dma((2, 2, chips)),
            dma((2, groups - 2, chips)),
            dma((2, groups - 1)),
            dma((2, chips)),
        ],
        compiler_params=pltpu.CompilerParams(
            collective_id=1, has_side_effects=True, vmem_limit_bytes=63 << 20
        ),
        name="fused_experts",
    )(ids, seats, y, scale, w_gate, w_up, w_down)


def shards(
    queries,
    key_rows,
    value_rows,
    out_proj,
    residual,
    norm_gain,
    w_gate,
    w_up,
    w_down,
    route_slot,
    route_weight,
    fetch_list,
    cotangent,
):
    tokens_here, model = cotangent.shape
    hidden_index = lax.axis_index("hidden")
    hidden_count = lax.axis_size("hidden")
    group_index = lax.axis_index("group")
    group_count = lax.axis_size("group")
    per_owner = FETCH // group_count

    chosen = route_slot[:, :, None] == jnp.arange(FETCH, dtype=jnp.int32)[None, None, :]
    slot_weight = jnp.sum(jnp.where(chosen, route_weight[:, :, None], 0.0), axis=1)
    order = (group_index + jnp.arange(group_count, dtype=jnp.int32)) % group_count
    own_cols = lax.dynamic_slice_in_dim(fetch_list, group_index * per_owner, per_owner, 1)
    ids = jnp.take(own_cols - group_index * EXP_GROUP, order, axis=0)

    heads_here = queries.shape[1] // HEAD_DIM
    kv_index = hidden_index * heads_here // (HEADS // KV_HEADS)
    key_block = lax.dynamic_slice_in_dim(key_rows, kv_index * HEAD_DIM, HEAD_DIM, 1)
    value_block = lax.dynamic_slice_in_dim(value_rows, kv_index * HEAD_DIM, HEAD_DIM, 1)
    mixed = attention_rows(queries, key_block, value_block, heads_here)
    partial_value = jnp.dot(mixed, out_proj, preferred_element_type=jnp.float32)
    share_width = model // hidden_count
    first_col = hidden_index * share_width
    blocks = partial_value.astype(jnp.bfloat16).reshape(tokens_here, hidden_count, share_width)
    attn_share = reduce_parts(jnp.swapaxes(blocks, 0, 1)[None, :, None], 2)[0]
    stream = lax.dynamic_slice_in_dim(residual, first_col, share_width, 1).astype(
        jnp.float32
    ) + attn_share.astype(jnp.float32)
    gain = lax.dynamic_slice_in_dim(norm_gain, first_col, share_width, 0)
    squares = jnp.sum(stream * stream, axis=-1)
    gained = (stream * gain).astype(jnp.bfloat16)
    slots_here = FETCH // hidden_count
    slots = lax.dynamic_slice_in_dim(slot_weight.T, hidden_index * slots_here, slots_here, 0)
    extra = -(-3 * slots_here * tokens_here // (16 * share_width)) * 16
    cot_share = lax.dynamic_slice_in_dim(cotangent, first_col, share_width, 1)
    y = jnp.stack(
        [
            jnp.concatenate([gained, to_rows(squares, extra, share_width)]),
            jnp.concatenate([cot_share, to_rows(slots, extra, share_width)]),
        ]
    )
    y_all = gather_all(y, group_count, hidden_count)
    squares_all = from_rows(y_all[:, :, 0, tokens_here:], tokens_here).sum(axis=1)
    inverse = lax.rsqrt(squares_all / model + epsilon)
    weights = from_rows(y_all[:, :, 1, tokens_here:], slots_here * tokens_here)
    weights = weights.reshape(group_count, FETCH, tokens_here)
    weights = lax.dynamic_slice_in_dim(weights, group_index * per_owner, per_owner, 1)
    scale = jnp.concatenate([weights, inverse[:, None, :]], axis=1)
    scale = jnp.pad(scale, ((0, 0), (0, 8 - scale.shape[1]), (0, 0)))
    scale = jnp.swapaxes(scale, 1, 2)
    weights_here = (jnp.swapaxes(w_gate, 1, 2), jnp.swapaxes(w_up, 1, 2), w_down)
    if group_count == 4:
        listed = own_cols - group_index * EXP_GROUP
        same = listed[:, :, None] == jnp.arange(EXP_GROUP, dtype=jnp.int32)
        place = jnp.arange(per_owner, dtype=jnp.int32)[None, :, None] - per_owner
        seats = per_owner + jnp.sum(jnp.where(same, place, 0), axis=1)
        sums, grad_gate, grad_up, grad_down = fused_experts(
            listed.reshape(-1), seats.reshape(-1), y_all, scale, *weights_here, hidden_count
        )
    else:
        parts, grad_gate, grad_up, grad_down = experts(order, ids, y_all, scale, *weights_here)
        sums = reduce_parts(parts, 1)
    grad_gate = jnp.swapaxes(grad_gate, 1, 2)
    grad_up = jnp.swapaxes(grad_up, 1, 2)
    layer_out = (stream + sums[0].astype(jnp.float32)).astype(jnp.bfloat16)
    return (layer_out, sums[1], grad_gate, grad_up, grad_down)


def solution(mesh):
    return jax.shard_map(
        shards,
        mesh=mesh,
        in_specs=(
            P("group", "hidden"),
            P("group", None),
            P("group", None),
            P("hidden", None),
            P("group", None),
            P(),
            P("group", None, "hidden"),
            P("group", None, "hidden"),
            P("group", "hidden", None),
            P("group", None),
            P("group", None),
            P(),
            P("group", None),
        ),
        out_specs=(
            P("group", "hidden"),
            P("group", "hidden"),
            P("group", None, "hidden"),
            P("group", None, "hidden"),
            P("group", "hidden", None),
        ),
        check_vma=False,
    )
```

```python
import functools
import math

import jax
import jax.numpy as jnp
from jax import lax
from jax.experimental import pallas as pl
from jax.experimental.pallas import tpu as pltpu
from jax.sharding import PartitionSpec as P

HEADS = 32
KV_HEADS = 4
HEAD_DIM = 128
EXP_GROUP = 8
FETCH = 16

epsilon = 1e-06


def attention_rows(query_in, key_block, value_block, heads_here):
    tokens_here = query_in.shape[0]
    query_heads = query_in.reshape(tokens_here, heads_here, HEAD_DIM)
    pos = jnp.arange(tokens_here, dtype=jnp.int32)
    scores = jnp.einsum(
        "thd,sd->hts", query_heads, key_block, preferred_element_type=jnp.float32
    ) / math.sqrt(HEAD_DIM)
    scores = jnp.where(pos[:, None] >= pos[None, :], scores, -1e30)
    row_peak = jnp.max(scores, axis=-1, keepdims=True)
    weights = jnp.exp(scores - row_peak)
    probabilities = (weights / jnp.sum(weights, axis=-1, keepdims=True)).astype(jnp.bfloat16)
    mixed = jnp.einsum("hts,sd->thd", probabilities, value_block, preferred_element_type=jnp.float32)
    return mixed.astype(jnp.bfloat16).reshape(tokens_here, heads_here * HEAD_DIM)


def dot(a, b, dims=((1,), (0,))):
    return lax.dot_general(a, b, (dims, ((), ())), preferred_element_type=jnp.float32)


def expert_kernel(per_owner, ids_ref, *refs):
    gates, refs = refs[:per_owner], refs[per_owner:]
    ups, refs = refs[:per_owner], refs[per_owner:]
    downs, refs = refs[:per_owner], refs[per_owner:]
    (
        y_ref, scale_ref,
        part_ref, gate_out, up_out, down_out,
        x2d, c2d, w_in, w_out, act, grads, act_turned, grads_turned, acc_gate, acc_up, acc_down, sems,
    ) = refs
    step = pl.program_id(0)
    blocks, width = y_ref.shape[1], y_ref.shape[4]
    tokens = x2d.shape[0]
    units = gates[0].shape[1]
    half = per_owner * units

    @pl.when(step == 0)
    def _():
        acc_gate[...] = jnp.zeros_like(acc_gate)
        acc_up[...] = jnp.zeros_like(acc_up)
        acc_down[...] = jnp.zeros_like(acc_down)

    for s in range(per_owner):
        w_in[s * units : (s + 1) * units, :] = gates[s][0]
        w_in[half + s * units : half + (s + 1) * units, :] = ups[s][0]
        w_out[s * units : (s + 1) * units, :] = downs[s][0]
    for h in range(blocks):
        x2d[:, h * width : (h + 1) * width] = y_ref[0, h, 0, :tokens]
        c2d[:, h * width : (h + 1) * width] = y_ref[0, h, 1, :tokens]

    scale = scale_ref[0]
    inverse = scale[:, per_owner : per_owner + 1]
    lane = lax.broadcasted_iota(jnp.int32, (tokens, half), 1)
    weight = jnp.broadcast_to(scale[:, :1], (tokens, half))
    for s in range(1, per_owner):
        weight = jnp.where(lane >= s * units, scale[:, s : s + 1], weight)
    turned = ((1,), (1,))
    pre_gate = dot(x2d[...], w_in[:half, :], turned) * inverse
    pre_up = dot(x2d[...], w_in[half:, :], turned) * inverse
    d_act = dot(c2d[...], w_out[...], turned) * weight
    sig = jax.nn.sigmoid(pre_gate)
    swish = pre_gate * sig
    weighted = swish * pre_up * weight
    d_gate = d_act * pre_up * sig * (1.0 + pre_gate * (1.0 - sig))
    d_up = d_act * swish
    act[...] = weighted.astype(act.dtype)
    grads[:, :half] = d_gate.astype(grads.dtype)
    grads[:, half:] = d_up.astype(grads.dtype)
    act_turned[...] = act[...].T
    grads_turned[:half, :] = (d_gate * inverse).astype(grads.dtype).T
    grads_turned[half:, :] = (d_up * inverse).astype(grads.dtype).T

    step_ids = [ids_ref[step * per_owner + s] for s in range(per_owner)]

    def add(acc, e, cols, value):
        acc[e, :, cols] = (acc[e, :, cols].astype(jnp.float32) + value).astype(acc.dtype)

    @pl.loop(0, blocks)
    def _(h):
        cols = pl.ds(pl.multiple_of(h * width, width), width)
        part_ref[0, h, 0] = dot(act[...], w_out[:, cols]).astype(part_ref.dtype)
        part_ref[0, h, 1] = dot(grads[...], w_in[:, cols]).astype(part_ref.dtype)
        down = dot(act_turned[...], c2d[:, cols])
        both = dot(grads_turned[...], x2d[:, cols])
        for s in range(per_owner):
            rows = slice(s * units, (s + 1) * units)
            add(acc_down, step_ids[s], cols, down[rows])
            add(acc_gate, step_ids[s], cols, both[rows])
            add(acc_up, step_ids[s], cols, both[half:][rows])

    @pl.when(step == pl.num_programs(0) - 1)
    def _():
        copies = [
            pltpu.make_async_copy(a, b, sems.at[i])
            for i, (a, b) in enumerate(
                ((acc_gate, gate_out), (acc_up, up_out), (acc_down, down_out))
            )
        ]
        for copy in copies:
            copy.start()
        for copy in copies:
            copy.wait()


def first_rows(count):
    return count // 24 * 16


def gather_kernel(groups, hidden, y_ref, out_ref, local_sem, send_sems, recv_sems):
    g, h = lax.axis_index("group"), lax.axis_index("hidden")
    chips = hidden // 2
    rows_all = y_ref.shape[1]
    cut = first_rows(rows_all)
    rows = (pl.ds(0, cut), pl.ds(cut, rows_all - cut))
    ahead = {"group": g, "hidden": lax.rem(h + 2, hidden)}
    behind = {"group": g, "hidden": lax.rem(h + hidden - 2, hidden)}
    partner = {"group": g, "hidden": h + 1 - 2 * lax.rem(h, 2)}
    peers = [{"group": lax.rem(g + k, groups), "hidden": h} for k in range(groups)]
    mesh_id = pl.DeviceIdType.MESH

    barrier = pltpu.get_barrier_semaphore()
    greeted = [ahead, behind, partner] + peers[1:]
    for device in greeted:
        pl.semaphore_signal(barrier, inc=1, device_id=device, device_id_type=mesh_id)
    pl.semaphore_wait(barrier, len(greeted))

    made = {}

    def send(key, source, g_from, h_from, part, device):
        number = len(made)
        target = out_ref.at[g_from, h_from, :, rows[part]]
        copy = pltpu.make_async_remote_copy(
            src_ref=target if source is None else source,
            dst_ref=target,
            send_sem=send_sems.at[number],
            recv_sem=recv_sems.at[number],
            device_id=device,
            device_id_type=mesh_id,
        )
        copy.start()
        made[key] = copy

    local = pltpu.make_async_copy(y_ref, out_ref.at[g, h], local_sem)
    local.start()
    own = [y_ref.at[:, rows[0]], y_ref.at[:, rows[1]]]
    group_of = [lax.rem(g + groups - k, groups) for k in range(groups)]
    hidden_of = [lax.rem(h + hidden - 2 * t, hidden) for t in range(chips)]
    send(("ring0", 1), own[0], g, h, 0, ahead)
    for k in range(1, groups):
        send(("peer1", 0, k), own[1], g, h, 1, peers[k])
    send(("ring1", 1, 0), own[1], g, h, 1, ahead)
    for k in range(1, groups):
        send(("peer0", 0, k), own[0], g, h, 0, peers[k])
    for part in range(2):
        send(("pair", part, 0, 0), own[part], g, h, part, partner)

    def arrive0(t):
        made[("ring0", t)].wait_recv()
        if t + 1 < chips:
            send(("ring0", t + 1), None, g, hidden_of[t], 0, ahead)
        for k in range(1, groups):
            send(("peer0", t, k), None, g, hidden_of[t], 0, peers[k])
        send(("pair", 0, t, 0), None, g, hidden_of[t], 0, partner)

    def arrive1(t, k):
        made[("ring1", t, k)].wait_recv()
        if t + 1 < chips:
            send(("ring1", t + 1, k), None, group_of[k], hidden_of[t], 1, ahead)
        send(("pair", 1, t, k), None, group_of[k], hidden_of[t], 1, partner)

    def arrive_peer(t, k):
        made[("peer0", t, k)].wait_recv()
        send(("pair", 0, t, k), None, group_of[k], hidden_of[t], 0, partner)

    arrive0(1)
    for k in range(1, groups):
        made[("peer1", 0, k)].wait_recv()
        send(("ring1", 1, k), None, group_of[k], h, 1, ahead)
        send(("pair", 1, 0, k), None, group_of[k], h, 1, partner)
    for t in range(1, chips):
        if t > 1:
            arrive0(t)
        for k in range(1, groups):
            arrive_peer(t - 1, k)
        for k in range(groups):
            arrive1(t, k)
    for k in range(1, groups):
        arrive_peer(chips - 1, k)
    for key, copy in made.items():
        if key[0] == "pair":
            copy.wait_recv()
        copy.wait_send()
    local.wait()


def gather_all(y, groups, hidden):
    chips = hidden // 2
    copies = (chips - 1) * (1 + groups) + (groups - 1) * (1 + chips) + 2 * chips * groups
    return pl.pallas_call(
        functools.partial(gather_kernel, groups, hidden),
        out_shape=jax.ShapeDtypeStruct((groups, hidden) + y.shape, y.dtype),
        in_specs=[pl.BlockSpec(memory_space=pltpu.VMEM)],
        out_specs=pl.BlockSpec(memory_space=pl.ANY),
        scratch_shapes=[
            pltpu.SemaphoreType.DMA,
            pltpu.SemaphoreType.DMA((copies,)),
            pltpu.SemaphoreType.DMA((copies,)),
        ],
        compiler_params=pltpu.CompilerParams(collective_id=0, has_side_effects=True),
        name="gather_all",
    )(y)


def reduce_kernel(
    groups, hidden, parts_ref, out_ref,
    own, pair_in, peer_in0, peer_in1, ring_in0, ring_in1, local_sems, send_sems, recv_sems,
):
    g, h = lax.axis_index("group"), lax.axis_index("hidden")
    chips = hidden // 2
    tokens = out_ref.shape[1]
    cut = first_rows(tokens)
    rows = (pl.ds(0, cut), pl.ds(cut, tokens - cut))
    ahead = {"group": g, "hidden": lax.rem(h + 2, hidden)}
    behind = {"group": g, "hidden": lax.rem(h + hidden - 2, hidden)}
    partner_h = h + 1 - 2 * lax.rem(h, 2)
    partner = {"group": g, "hidden": partner_h}
    group_of = [lax.rem(g + k, groups) for k in range(groups)]
    peers = [{"group": group_of[k], "hidden": h} for k in range(groups)]
    mesh_id = pl.DeviceIdType.MESH

    barrier = pltpu.get_barrier_semaphore()
    greeted = [ahead, behind, partner] + peers[1:]
    for device in greeted:
        pl.semaphore_signal(barrier, inc=1, device_id=device, device_id_type=mesh_id)
    pl.semaphore_wait(barrier, len(greeted))

    made = {}

    def send(key, source, target, device):
        number = len(made)
        copy = pltpu.make_async_remote_copy(
            src_ref=source,
            dst_ref=target,
            send_sem=send_sems.at[number],
            recv_sem=recv_sems.at[number],
            device_id=device,
            device_id_type=mesh_id,
        )
        copy.start()
        made[key] = copy

    def add(into, *others):
        total = into[...].astype(jnp.float32)
        for other in others:
            total = total + other[...].astype(jnp.float32)
        into[...] = total.astype(into.dtype)

    turns = list(range(1, chips)) + [0]
    loads = {}
    for t in turns:
        for k in range(groups):
            theirs = lax.rem(partner_h + hidden - 2 * t, hidden)
            send(("pair", t, k), parts_ref.at[group_of[k], theirs], pair_in.at[k, t], partner)
            mine = lax.rem(h + hidden - 2 * t, hidden)
            loads[t, k] = pltpu.make_async_copy(
                parts_ref.at[group_of[k], mine], own.at[k, t], local_sems.at[k * chips + t]
            )
            loads[t, k].start()

    def half(k, t, part):
        return own.at[k, t, :, rows[part]]

    last = chips - 1
    for t in turns:
        before = t - 1 if t else last
        for k in range(groups):
            loads[t, k].wait()
            made["pair", t, k].wait_recv()
            add(own.at[k, t], pair_in.at[k, t])
            if t == 1:
                send(("ring1", t, k), half(k, t, 1), ring_in1.at[t, k], ahead)
            if k:
                send(("peer0", t, k), half(k, t, 0), peer_in0.at[t, k], peers[k])
        if t != 1:
            for k in list(range(1, groups)) + [0]:
                made["ring1", before, k].wait_recv()
                add(half(k, t, 1), ring_in1.at[before, k])
                if t:
                    send(("ring1", t, k), half(k, t, 1), ring_in1.at[t, k], ahead)
                elif k:
                    send(("peer1", 0, k), half(k, t, 1), peer_in1.at[k], peers[k])
        arrived = []
        for k in range(1, groups):
            made["peer0", t, k].wait_recv()
            arrived.append(peer_in0.at[t, k])
        if t != 1:
            made["ring0", before].wait_recv()
            arrived.append(ring_in0.at[before])
        add(half(0, t, 0), *arrived)
        if t:
            send(("ring0", t), half(0, t, 0), ring_in0.at[t], ahead)
    for k in range(1, groups):
        made["peer1", 0, k].wait_recv()
    add(half(0, 0, 1), *[peer_in1.at[k] for k in range(1, groups)])
    out_ref[...] = own[0, 0]
    for copy in made.values():
        copy.wait_send()


def reduce_parts(parts, collective_id):
    groups, hidden, pieces, tokens, width = parts.shape
    chips = hidden // 2
    block = 2 * pieces * tokens * width
    if 3 * groups * chips * block > 40 << 20:
        flat = parts.reshape((groups * hidden,) + parts.shape[2:])
        return lax.psum_scatter(flat, ("group", "hidden"), scatter_dimension=0, tiled=True)[0]
    copies = (chips - 1) * (1 + groups) + (groups - 1) * (1 + chips) + chips * groups
    cut = first_rows(tokens)
    first, second = (pieces, cut, width), (pieces, tokens - cut, width)
    bf = parts.dtype
    return pl.pallas_call(
        functools.partial(reduce_kernel, groups, hidden),
        out_shape=jax.ShapeDtypeStruct(parts.shape[2:], bf),
        in_specs=[pl.BlockSpec(memory_space=pl.ANY)],
        out_specs=pl.BlockSpec(memory_space=pltpu.VMEM),
        scratch_shapes=[
            pltpu.VMEM((groups, chips) + parts.shape[2:], bf),
            pltpu.VMEM((groups, chips) + parts.shape[2:], bf),
            pltpu.VMEM((chips, groups) + first, bf),
            pltpu.VMEM((groups,) + second, bf),
            pltpu.VMEM((chips,) + first, bf),
            pltpu.VMEM((chips, groups) + second, bf),
            pltpu.SemaphoreType.DMA((chips * groups,)),
            pltpu.SemaphoreType.DMA((copies,)),
            pltpu.SemaphoreType.DMA((copies,)),
        ],
        compiler_params=pltpu.CompilerParams(
            collective_id=collective_id, has_side_effects=True, vmem_limit_bytes=40 << 20
        ),
        name=f"reduce_parts_{collective_id}",
    )(parts)


def to_rows(values, rows, width):
    high = lax.reduce_precision(values, 8, 7)
    rest = values - high
    mid = lax.reduce_precision(rest, 8, 7)
    flat = jnp.stack([high, mid, rest - mid]).reshape(-1).astype(jnp.bfloat16)
    return jnp.pad(flat, (0, rows * width - flat.shape[0])).reshape(rows, width)


def from_rows(block, count):
    flat = block.reshape(block.shape[:2] + (-1,))[:, :, : 3 * count].astype(jnp.float32)
    high, mid, low = (flat[:, :, i * count : (i + 1) * count] for i in range(3))
    return high + mid + low


def experts(order, ids, y, scale, w_gate, w_up, w_down):
    groups, blocks, _, rows, width = y.shape
    tokens = scale.shape[1]
    model = blocks * width
    per_owner = ids.shape[1]
    units = w_down.shape[1]
    half = per_owner * units
    ids_end = groups * per_owner

    def pick(s):
        return pl.BlockSpec((1, units, model), lambda k, n: (n[k * per_owner + s], 0, 0))

    bf = jnp.bfloat16
    parts = jax.ShapeDtypeStruct((groups, blocks, 2, tokens, width), bf)
    return pl.pallas_call(
        functools.partial(expert_kernel, per_owner),
        grid_spec=pltpu.PrefetchScalarGridSpec(
            num_scalar_prefetch=1,
            grid=(groups,),
            in_specs=[pick(s) for s in range(per_owner)] * 3
            + [
                pl.BlockSpec(
                    (1, blocks, 2, rows, width), lambda k, n: (n[ids_end + k], 0, 0, 0, 0)
                ),
                pl.BlockSpec(
                    (1, tokens, scale.shape[2]), lambda k, n: (n[ids_end + k], 0, 0)
                ),
            ],
            out_specs=[
                pl.BlockSpec((1,) + parts.shape[1:], lambda k, n: (n[ids_end + k], 0, 0, 0, 0)),
            ]
            + [pl.BlockSpec(memory_space=pl.ANY)] * 3,
            scratch_shapes=[
                pltpu.VMEM((tokens, model), bf),
                pltpu.VMEM((tokens, model), bf),
                pltpu.VMEM((2 * half, model), bf),
                pltpu.VMEM((half, model), bf),
                pltpu.VMEM((tokens, half), bf),
                pltpu.VMEM((tokens, 2 * half), bf),
                pltpu.VMEM((half, tokens), bf),
                pltpu.VMEM((2 * half, tokens), bf),
                pltpu.VMEM(w_down.shape, bf),
                pltpu.VMEM(w_down.shape, bf),
                pltpu.VMEM(w_down.shape, bf),
                pltpu.SemaphoreType.DMA((3,)),
            ],
        ),
        out_shape=[parts] + [jax.ShapeDtypeStruct(w_down.shape, bf)] * 3,
        compiler_params=pltpu.CompilerParams(vmem_limit_bytes=56 << 20),
        name="experts",
    )(
        jnp.concatenate([ids.reshape(-1), order]),
        *([w_gate] * per_owner + [w_up] * per_owner + [w_down] * per_owner),
        y,
        scale,
    )


def pair_groups(g, i):
    across, along = 1 - i // 2, 1 - lax.rem(i, 2)
    gx, gy = lax.rem(g, 2), g // 2
    return lax.rem(gy + along, 2) * 2 + lax.rem(gx + across, 2)


def front_kernel(
    groups, hidden, q_ref, k_ref, v_ref, proj_ref, cot_ref, slot_ref,
    out_ref, cot_all, slot_all,
    mixed, own, stage, pair_in, ring_in,
    local_sem, slot_sems, cot_sems, pair_sems, ring_sems,
):
    g, h = lax.axis_index("group"), lax.axis_index("hidden")
    chips = hidden // 2
    last, final = chips - 1, groups - 1
    tokens, width = out_ref.shape
    heads_here = q_ref.shape[1] // HEAD_DIM
    ahead = {"group": g, "hidden": lax.rem(h + 2, hidden)}
    behind = {"group": g, "hidden": lax.rem(h + hidden - 2, hidden)}
    partner_h = h + 1 - 2 * lax.rem(h, 2)
    partner = {"group": g, "hidden": partner_h}
    mesh_id = pl.DeviceIdType.MESH
    source = [pair_groups(g, i) for i in range(groups)]
    peers = [{"group": source[i], "hidden": h} for i in range(final)]

    barrier = pltpu.get_barrier_semaphore()
    greeted = [ahead, behind, partner] + peers
    for device in greeted:
        pl.semaphore_signal(barrier, inc=1, device_id=device, device_id_type=mesh_id)
    pl.semaphore_wait(barrier, len(greeted))

    def remote(source_ref, target, sems, index, device):
        return pltpu.make_async_remote_copy(
            src_ref=source_ref,
            dst_ref=target,
            send_sem=sems.at[(0,) + index],
            recv_sem=sems.at[(1,) + index],
            device_id=device,
            device_id_type=mesh_id,
        )

    quarter = tokens // 4
    base = lax.rem(h, 2) * (2 * quarter)

    def piece(n):
        return pl.ds(pl.multiple_of(base + n * quarter, quarter), quarter)

    def landed(i, n):
        return cot_all.at[source[i], piece(n)]

    made = {}

    def send(key, source_ref, target, device):
        copy = remote(source_ref, target, cot_sems, (len(made),), device)
        copy.start()
        made[key] = copy

    for i, n in ((1, 0), (2, 1), (1, 1), (2, 0)):
        send(("near", i, n), cot_ref.at[piece(n)], cot_all.at[g, piece(n)], peers[i])
    slots = [remote(slot_ref, slot_all.at[g], slot_sems, (i,), peers[i]) for i in range(final)]
    for copy in slots:
        copy.start()
    local = pltpu.make_async_copy(cot_ref, cot_all.at[g], local_sem)
    local.start()
    slot_all[g] = slot_ref[...]

    def pass_on(i, n, forward):
        made["far" if i == 0 else "near", i, n].wait_recv()
        if forward:
            send(("far", 0, n), landed(i, n), landed(i, n), peers[3 - i])
        send(("pair", i, n), landed(i, n), landed(i, n), partner)

    kv = h * heads_here // (HEADS // KV_HEADS)
    kv_cols = pl.ds(pl.multiple_of(kv * HEAD_DIM, HEAD_DIM), HEAD_DIM)
    keys, values = k_ref[:, kv_cols], v_ref[:, kv_cols]
    seen = lax.broadcasted_iota(jnp.int32, (tokens, tokens), 0) >= lax.broadcasted_iota(
        jnp.int32, (tokens, tokens), 1
    )
    for head in range(heads_here):
        cols = slice(head * HEAD_DIM, (head + 1) * HEAD_DIM)
        scores = dot(q_ref[:, cols], keys, ((1,), (1,))) / math.sqrt(HEAD_DIM)
        scores = jnp.where(seen, scores, -1e30)
        weights = jnp.exp(scores - jnp.max(scores, axis=-1, keepdims=True))
        total = jnp.sum(weights, axis=-1, keepdims=True)
        mixed[:, cols] = dot((weights / total).astype(mixed.dtype), values).astype(mixed.dtype)

    def pair_copy(t):
        return remote(stage.at[t], pair_in.at[t], pair_sems, (t,), partner)

    def ring_copy(t):
        return remote(own.at[t], ring_in.at[t], ring_sems, (t,), ahead)

    def add(into, *others):
        total = into[...].astype(jnp.float32)
        for other in others:
            total = total + other[...].astype(jnp.float32)
        into[...] = total.astype(into.dtype)

    def reduce_task(t):
        pair_copy(t).wait_recv()
        if t == 1:
            add(own.at[t], pair_in.at[t])
        else:
            before = t - 1 if t else last
            ring_copy(before).wait_recv()
            add(own.at[t], pair_in.at[t], ring_in.at[before])
        if t:
            ring_copy(t).start()

    @pl.loop(0, chips)
    def _(j):
        t = lax.rem(j + 1, chips)
        for whose, target in ((partner_h, stage), (h, own)):
            first = pl.multiple_of(lax.rem(whose + hidden - 2 * t, hidden) * width, width)
            target[t] = dot(mixed[...], proj_ref[:, pl.ds(first, width)]).astype(target.dtype)
            if whose is partner_h:
                pair_copy(t).start()

        @pl.when(j == 1)
        def _():
            reduce_task(1)

    pass_on(1, 0, True)
    pass_on(2, 1, True)
    for t in list(range(2, chips)) + [0]:
        reduce_task(t)
        if t == 2:
            pass_on(1, 1, False)
            pass_on(2, 0, False)
    pass_on(0, 0, False)
    pass_on(0, 1, False)
    out_ref[...] = own[0]
    for key, copy in made.items():
        if key[0] == "pair":
            copy.wait_recv()
        copy.wait_send()
    for copy in slots:
        copy.wait()
    for t in range(chips):
        pair_copy(t).wait_send()
        if t:
            ring_copy(t).wait_send()
    local.wait()


def front(queries, key_rows, value_rows, out_proj, cotangent, slots, groups, hidden):
    tokens, model = cotangent.shape
    width = model // hidden
    chips = hidden // 2
    bf = queries.dtype
    vmem = pl.BlockSpec(memory_space=pltpu.VMEM)
    dma = pltpu.SemaphoreType.DMA
    block = pltpu.VMEM((chips, tokens, width), bf)
    return pl.pallas_call(
        functools.partial(front_kernel, groups, hidden),
        in_specs=[vmem] * 6,
        out_specs=[vmem, pl.BlockSpec(memory_space=pl.ANY), vmem],
        out_shape=[
            jax.ShapeDtypeStruct((tokens, width), bf),
            jax.ShapeDtypeStruct((groups,) + cotangent.shape, bf),
            jax.ShapeDtypeStruct((groups,) + slots.shape, slots.dtype),
        ],
        scratch_shapes=[
            pltpu.VMEM(queries.shape, bf), block, block, block, block,
            dma, dma((2, groups - 1)), dma((2, 12)), dma((2, chips)), dma((2, chips)),
        ],
        compiler_params=pltpu.CompilerParams(
            collective_id=2, has_side_effects=True, vmem_limit_bytes=40 << 20
        ),
        name="front",
    )(queries, key_rows, value_rows, out_proj, cotangent, slots)


def fused_kernel(
    groups, hidden, per_owner,
    ids_ref, seat_ref, y_ref, cot_ref, scale_ref, gate_ref, up_ref, down_ref,
    out_ref, gate_out, up_out, down_out,
    w_gate, w_up, w_down, xs, cs, w_in, w_out, act, grads, act_turned, grads_turned,
    slot_gate, slot_up, slot_down,
    own, stage, pair_in, diag_in, peer_in0, peer_in1, ring_in0, ring_in1,
    load_sems, fetch_sems, pair_sems, ring1_sems, diag_sems, peer0_sems, peer1_sems, ring0_sems,
):
    g, h = lax.axis_index("group"), lax.axis_index("hidden")
    chips = hidden // 2
    owned, units, model = w_gate.shape
    tokens, width = out_ref.shape[1], out_ref.shape[2]
    half = per_owner * units
    last, final = chips - 1, groups - 1
    cut = first_rows(tokens)
    rows = (pl.ds(0, cut), pl.ds(cut, tokens - cut))
    via = (pl.ds(0, cut // 2), pl.ds(cut // 2, cut // 2))
    ahead = {"group": g, "hidden": lax.rem(h + 2, hidden)}
    behind = {"group": g, "hidden": lax.rem(h + hidden - 2, hidden)}
    partner_h = h + 1 - 2 * lax.rem(h, 2)
    partner = {"group": g, "hidden": partner_h}
    mesh_id = pl.DeviceIdType.MESH

    def peer(i):
        return {"group": pair_groups(g, i), "hidden": h}

    barrier = pltpu.get_barrier_semaphore()
    greeted = [ahead, behind, partner] + [peer(i) for i in range(final)]
    for device in greeted:
        pl.semaphore_signal(barrier, inc=1, device_id=device, device_id_type=mesh_id)

    loads = [
        pltpu.make_async_copy(a, b, load_sems.at[n])
        for n, (a, b) in enumerate(((gate_ref, w_gate), (up_ref, w_up), (down_ref, w_down)))
    ]
    stores = [
        pltpu.make_async_copy(a, b, load_sems.at[n])
        for n, (a, b) in enumerate(((w_gate, gate_out), (w_up, up_out), (w_down, down_out)))
    ]

    def fetches(i):
        slot = lax.rem(i, 2)
        source = pair_groups(g, i)
        copies = [
            pltpu.make_async_copy(cot_ref.at[source], cs.at[slot], fetch_sems.at[slot, hidden])
        ]
        for b in range(hidden):
            copies.append(
                pltpu.make_async_copy(
                    y_ref.at[source, b, 0, pl.ds(0, tokens)],
                    xs.at[slot, :, pl.ds(b * width, width)],
                    fetch_sems.at[slot, b],
                )
            )
        return copies

    for copy in fetches(0):
        copy.start()
    for copy in loads:
        copy.start()

    for buffer in (slot_gate, slot_up, slot_down):
        buffer[per_owner] = jnp.zeros(buffer.shape[1:], buffer.dtype)

    def remote(source, target, sems, index, device):
        return pltpu.make_async_remote_copy(
            src_ref=source,
            dst_ref=target,
            send_sem=sems.at[(0,) + index],
            recv_sem=sems.at[(1,) + index],
            device_id=device,
            device_id_type=mesh_id,
        )

    def part_of(i, t, part):
        return own.at[i, t, :, rows[part]]

    def pair_copy(i, t):
        return remote(stage.at[i, t], pair_in.at[i, t], pair_sems, (i, t), partner)

    def ring1_copy(i, t):
        return remote(part_of(i, t, 1), ring_in1.at[i, t], ring1_sems, (i, t), ahead)

    def diag_copy(n, t):
        source = own.at[0, t, :, via[n]]
        return remote(source, diag_in.at[n, t], diag_sems, (n, t), peer(n + 1))

    def peer0_copy(i, t):
        return remote(part_of(i, t, 0), peer_in0.at[i - 1, t], peer0_sems, (i - 1, t), peer(i))

    def peer1_copy(i):
        return remote(part_of(i, 0, 1), peer_in1.at[i], peer1_sems, (i,), peer(i))

    def ring0_copy(t):
        return remote(part_of(final, t, 0), ring_in0.at[t], ring0_sems, (t,), ahead)

    def add(into, *others):
        total = into[...].astype(jnp.float32)
        for other in others:
            total = total + other[...].astype(jnp.float32)
        into[...] = total.astype(into.dtype)

    def pair_task(i, t):
        pair_copy(i, t).wait_recv()
        add(own.at[i, t], pair_in.at[i, t])

        @pl.when(t == 1)
        def _():
            ring1_copy(i, t).start()

        @pl.when(i == 0)
        def _():
            for n in range(2):
                diag_copy(n, t).start()

        for n, step in ((1, 1), (0, 2)):

            @pl.when(i == step)
            def _():
                diag_copy(n, t).wait_recv()
                add(own.at[step, t, :, via[n]], diag_in.at[n, t])
                peer0_copy(step, t).start()

    def ring_task(i, t):
        before = t - 1 if t else last
        ring1_copy(i, before).wait_recv()
        add(part_of(i, t, 1), ring_in1.at[i, before])
        if t:
            ring1_copy(i, t).start()

    def finish_task(t):
        arrived = []
        for i in range(1, final):
            peer0_copy(i, t).wait_recv()
            arrived.append(peer_in0.at[i - 1, t])
        if t != 1:
            before = t - 1 if t else last
            ring0_copy(before).wait_recv()
            arrived.append(ring_in0.at[before])
        add(part_of(final, t, 0), *arrived)
        if t:
            ring0_copy(t).start()

    pl.semaphore_wait(barrier, len(greeted))
    for copy in loads:
        copy.wait()

    turned = ((1,), (1,))

    @pl.loop(0, groups)
    def _(i):
        slot = lax.rem(i, 2)
        group = pair_groups(g, i)

        @pl.when(i < final)
        def _():
            for copy in fetches(i + 1):
                copy.start()

        for s in range(per_owner):
            e = ids_ref[group * per_owner + s]
            w_in[s * units : (s + 1) * units, :] = w_gate[e]
            w_in[half + s * units : half + (s + 1) * units, :] = w_up[e]
            w_out[s * units : (s + 1) * units, :] = w_down[e]
        scale = scale_ref[group]
        inverse = scale[:, per_owner : per_owner + 1]
        lane = lax.broadcasted_iota(jnp.int32, (tokens, half), 1)
        weight = jnp.broadcast_to(scale[:, :1], (tokens, half))
        for s in range(1, per_owner):
            weight = jnp.where(lane >= s * units, scale[:, s : s + 1], weight)
        for copy in fetches(i):
            copy.wait()
        pre_gate = dot(xs[slot], w_in[:half, :], turned) * inverse
        pre_up = dot(xs[slot], w_in[half:, :], turned) * inverse
        d_act = dot(cs[slot], w_out[...], turned) * weight
        sig = jax.nn.sigmoid(pre_gate)
        swish = pre_gate * sig
        weighted = swish * pre_up * weight
        d_gate = d_act * pre_up * sig * (1.0 + pre_gate * (1.0 - sig))
        d_up = d_act * swish
        act[...] = weighted.astype(act.dtype)
        grads[:, :half] = d_gate.astype(grads.dtype)
        grads[:, half:] = d_up.astype(grads.dtype)
        act_turned[i] = act[...].T
        grads_turned[i, :half, :] = (d_gate * inverse).astype(grads.dtype).T
        grads_turned[i, half:, :] = (d_up * inverse).astype(grads.dtype).T

        @pl.when(i > 0)
        def _():
            ring_task(i - 1, 2)

        @pl.when(i > 1)
        def _():
            ring_task(i - 2, 0)
            peer1_copy(i - 2).start()

        @pl.loop(0, chips)
        def _(j):
            t = lax.rem(j + 1, chips)
            back = hidden - 2 * t
            for whose, target in ((partner_h, stage), (h, own)):
                first = pl.multiple_of(lax.rem(whose + back, hidden) * width, width)
                cols = pl.ds(first, width)
                target[i, t, 0] = dot(act[...], w_out[:, cols]).astype(target.dtype)
                target[i, t, 1] = dot(grads[...], w_in[:, cols]).astype(target.dtype)
                if whose is partner_h:
                    pair_copy(i, t).start()

            @pl.when(j > 0)
            def _():
                pair_task(i, j)

        pair_task(i, 0)

        @pl.when(i > 0)
        def _():
            ring_task(i - 1, 3)

    for buffer in (w_gate, w_up, w_down):
        buffer[...] = jnp.zeros_like(buffer)

    def finish_last():
        for i in range(final):
            peer1_copy(i).wait_recv()
        add(part_of(final, 0, 1), *[peer_in1.at[i] for i in range(final)])

    def finish_ring():
        ring_task(final - 1, 0)
        peer1_copy(final - 1).start()

    tasks = (
        (2, lambda: ring_task(final, 2)),
        (3, lambda: finish_task(1)),
        (6, finish_ring),
        (9, lambda: ring_task(final, 3)),
        (13, lambda: finish_task(2)),
        (16, lambda: ring_task(final, 0)),
        (23, lambda: finish_task(3)),
    )

    @pl.loop(0, groups * hidden)
    def _(n):
        i, b = final - n // hidden, lax.rem(n, hidden)
        slot = lax.rem(i, 2)
        group = pair_groups(g, i)

        @pl.when((b == 0) & (n > 0) & (i > 0))
        def _():
            for copy in fetches(i - 1):
                copy.start()

        @pl.when((b == 0) & (i < final - 1))
        def _():
            for copy in fetches(i):
                copy.wait()

        cols = pl.ds(pl.multiple_of(b * width, width), width)
        down = dot(act_turned[i], cs[slot, :, cols])
        both = dot(grads_turned[i], xs[slot, :, cols])
        for s in range(per_owner):
            slot_down[s] = down[s * units : (s + 1) * units]
            slot_gate[s] = both[s * units : (s + 1) * units]
            slot_up[s] = both[half + s * units : half + (s + 1) * units]
        for e in range(owned):
            seat = seat_ref[group * owned + e]
            for total, value in ((w_down, slot_down), (w_gate, slot_gate), (w_up, slot_up)):
                total[e, :, cols] = (total[e, :, cols].astype(jnp.float32) + value[seat]).astype(
                    total.dtype
                )
        for at, task in tasks:
            pl.when(n == at)(task)

    for copy in stores:
        copy.start()
    finish_task(0)
    finish_last()
    out_ref[...] = own[final, 0]
    for i in range(groups):
        for t in range(chips):
            pair_copy(i, t).wait_send()
            if t:
                ring1_copy(i, t).wait_send()
            if 0 < i < final:
                peer0_copy(i, t).wait_send()
    for t in range(chips):
        for n in range(2):
            diag_copy(n, t).wait_send()
    for i in range(final):
        peer1_copy(i).wait_send()
    for t in range(1, chips):
        ring0_copy(t).wait_send()
    for copy in stores:
        copy.wait()


def fused_experts(ids, seats, y, cot, scale, w_gate, w_up, w_down, hidden):
    groups = y.shape[0]
    width = y.shape[4]
    tokens = scale.shape[1]
    chips = hidden // 2
    owned, units, model = w_down.shape
    per_owner = ids.shape[0] // groups
    half = per_owner * units
    cut = first_rows(tokens)
    first, second = (2, cut, width), (2, tokens - cut, width)
    block = (2, tokens, width)
    bf = jnp.bfloat16
    anywhere = pl.BlockSpec(memory_space=pl.ANY)
    scalars = pl.BlockSpec(memory_space=pltpu.SMEM)
    dma = pltpu.SemaphoreType.DMA
    return pl.pallas_call(
        functools.partial(fused_kernel, groups, hidden, per_owner),
        in_specs=[scalars, scalars, anywhere, anywhere, pl.BlockSpec(memory_space=pltpu.VMEM)]
        + [anywhere] * 3,
        out_specs=[pl.BlockSpec(memory_space=pltpu.VMEM)] + [anywhere] * 3,
        out_shape=[jax.ShapeDtypeStruct(block, bf)] + [jax.ShapeDtypeStruct(w_down.shape, bf)] * 3,
        scratch_shapes=[pltpu.VMEM(w_down.shape, bf)] * 3
        + [
            pltpu.VMEM((2, tokens, model), bf),
            pltpu.VMEM((2, tokens, model), bf),
            pltpu.VMEM((2 * half, model), bf),
            pltpu.VMEM((half, model), bf),
            pltpu.VMEM((tokens, half), bf),
            pltpu.VMEM((tokens, 2 * half), bf),
            pltpu.VMEM((groups, half, tokens), bf),
            pltpu.VMEM((groups, 2 * half, tokens), bf),
        ]
        + [pltpu.VMEM((per_owner + 1, units, width), jnp.float32)] * 3
        + [
            pltpu.VMEM((groups, chips) + block, bf),
            pltpu.VMEM((groups, chips) + block, bf),
            pltpu.VMEM((groups, chips) + block, bf),
            pltpu.VMEM((2, chips, 2, cut // 2, width), bf),
            pltpu.VMEM((groups - 2, chips) + first, bf),
            pltpu.VMEM((groups - 1,) + second, bf),
            pltpu.VMEM((chips,) + first, bf),
            pltpu.VMEM((groups, chips) + second, bf),
            dma((3,)),
            dma((2, hidden + 1)),
            dma((2, groups, chips)),
            dma((2, groups, chips)),
            dma((2, 2, chips)),
            dma((2, groups - 2, chips)),
            dma((2, groups - 1)),
            dma((2, chips)),
        ],
        compiler_params=pltpu.CompilerParams(
            collective_id=1, has_side_effects=True, vmem_limit_bytes=63 << 20
        ),
        name="fused_experts",
    )(ids, seats, y, cot, scale, w_gate, w_up, w_down)


def shards(
    queries,
    key_rows,
    value_rows,
    out_proj,
    residual,
    norm_gain,
    w_gate,
    w_up,
    w_down,
    route_slot,
    route_weight,
    fetch_list,
    cotangent,
):
    tokens_here, model = cotangent.shape
    hidden_index = lax.axis_index("hidden")
    hidden_count = lax.axis_size("hidden")
    group_index = lax.axis_index("group")
    group_count = lax.axis_size("group")
    per_owner = FETCH // group_count

    chosen = route_slot[:, :, None] == jnp.arange(FETCH, dtype=jnp.int32)[None, None, :]
    slot_weight = jnp.sum(jnp.where(chosen, route_weight[:, :, None], 0.0), axis=1)
    own_cols = lax.dynamic_slice_in_dim(fetch_list, group_index * per_owner, per_owner, 1)
    listed = own_cols - group_index * EXP_GROUP
    heads_here = queries.shape[1] // HEAD_DIM
    share_width = model // hidden_count
    first_col = hidden_index * share_width
    weights_here = (jnp.swapaxes(w_gate, 1, 2), jnp.swapaxes(w_up, 1, 2), w_down)
    fused = group_count == 4
    if fused:
        attn_share, cot_all, slot_all = front(
            queries, key_rows, value_rows, out_proj, cotangent, slot_weight.T,
            group_count, hidden_count,
        )
    else:
        kv_index = hidden_index * heads_here // (HEADS // KV_HEADS)
        key_block = lax.dynamic_slice_in_dim(key_rows, kv_index * HEAD_DIM, HEAD_DIM, 1)
        value_block = lax.dynamic_slice_in_dim(value_rows, kv_index * HEAD_DIM, HEAD_DIM, 1)
        mixed = attention_rows(queries, key_block, value_block, heads_here)
        partial_value = jnp.dot(mixed, out_proj, preferred_element_type=jnp.float32)
        blocks = partial_value.astype(jnp.bfloat16).reshape(tokens_here, hidden_count, share_width)
        attn_share = reduce_parts(jnp.swapaxes(blocks, 0, 1)[None, :, None], 2)[0]
    stream = lax.dynamic_slice_in_dim(residual, first_col, share_width, 1).astype(
        jnp.float32
    ) + attn_share.astype(jnp.float32)
    gain = lax.dynamic_slice_in_dim(norm_gain, first_col, share_width, 0)
    squares = jnp.sum(stream * stream, axis=-1)
    gained = (stream * gain).astype(jnp.bfloat16)
    slots_here = FETCH // hidden_count
    extra = -(-3 * slots_here * tokens_here // (16 * share_width)) * 16
    y = jnp.concatenate([gained, to_rows(squares, extra, share_width)])[None]
    if not fused:
        slots = lax.dynamic_slice_in_dim(slot_weight.T, hidden_index * slots_here, slots_here, 0)
        cot_share = lax.dynamic_slice_in_dim(cotangent, first_col, share_width, 1)
        y = jnp.concatenate(
            [y, jnp.concatenate([cot_share, to_rows(slots, extra, share_width)])[None]]
        )
    y_all = gather_all(y, group_count, hidden_count)
    squares_all = from_rows(y_all[:, :, 0, tokens_here:], tokens_here).sum(axis=1)
    inverse = lax.rsqrt(squares_all / model + epsilon)
    if fused:
        weights = slot_all
    else:
        weights = from_rows(y_all[:, :, 1, tokens_here:], slots_here * tokens_here)
        weights = weights.reshape(group_count, FETCH, tokens_here)
    weights = lax.dynamic_slice_in_dim(weights, group_index * per_owner, per_owner, 1)
    scale = jnp.concatenate([weights, inverse[:, None, :]], axis=1)
    scale = jnp.pad(scale, ((0, 0), (0, 8 - scale.shape[1]), (0, 0)))
    scale = jnp.swapaxes(scale, 1, 2)
    if fused:
        same = listed[:, :, None] == jnp.arange(EXP_GROUP, dtype=jnp.int32)
        place = jnp.arange(per_owner, dtype=jnp.int32)[None, :, None] - per_owner
        seats = per_owner + jnp.sum(jnp.where(same, place, 0), axis=1)
        sums, grad_gate, grad_up, grad_down = fused_experts(
            listed.reshape(-1), seats.reshape(-1), y_all, cot_all, scale, *weights_here, hidden_count
        )
    else:
        order = (group_index + jnp.arange(group_count, dtype=jnp.int32)) % group_count
        ids = jnp.take(listed, order, axis=0)
        parts, grad_gate, grad_up, grad_down = experts(order, ids, y_all, scale, *weights_here)
        sums = reduce_parts(parts, 1)
    grad_gate = jnp.swapaxes(grad_gate, 1, 2)
    grad_up = jnp.swapaxes(grad_up, 1, 2)
    layer_out = (stream + sums[0].astype(jnp.float32)).astype(jnp.bfloat16)
    return (layer_out, sums[1], grad_gate, grad_up, grad_down)


def solution(mesh):
    return jax.shard_map(
        shards,
        mesh=mesh,
        in_specs=(
            P("group", "hidden"),
            P("group", None),
            P("group", None),
            P("hidden", None),
            P("group", None),
            P(),
            P("group", None, "hidden"),
            P("group", None, "hidden"),
            P("group", "hidden", None),
            P("group", None),
            P("group", None),
            P(),
            P("group", None),
        ),
        out_specs=(
            P("group", "hidden"),
            P("group", "hidden"),
            P("group", None, "hidden"),
            P("group", None, "hidden"),
            P("group", "hidden", None),
        ),
        check_vma=False,
    )
```

```python
import functools
import math

import jax
import jax.numpy as jnp
from jax import lax
from jax.experimental import pallas as pl
from jax.experimental.pallas import tpu as pltpu
from jax.sharding import PartitionSpec as P

HEADS = 32
KV_HEADS = 4
HEAD_DIM = 128
EXP_GROUP = 8
FETCH = 16

epsilon = 1e-06


def attention_rows(query_in, key_block, value_block, heads_here):
    tokens_here = query_in.shape[0]
    query_heads = query_in.reshape(tokens_here, heads_here, HEAD_DIM)
    pos = jnp.arange(tokens_here, dtype=jnp.int32)
    scores = jnp.einsum(
        "thd,sd->hts", query_heads, key_block, preferred_element_type=jnp.float32
    ) / math.sqrt(HEAD_DIM)
    scores = jnp.where(pos[:, None] >= pos[None, :], scores, -1e30)
    row_peak = jnp.max(scores, axis=-1, keepdims=True)
    weights = jnp.exp(scores - row_peak)
    probabilities = (weights / jnp.sum(weights, axis=-1, keepdims=True)).astype(jnp.bfloat16)
    mixed = jnp.einsum("hts,sd->thd", probabilities, value_block, preferred_element_type=jnp.float32)
    return mixed.astype(jnp.bfloat16).reshape(tokens_here, heads_here * HEAD_DIM)


def dot(a, b, dims=((1,), (0,))):
    return lax.dot_general(a, b, (dims, ((), ())), preferred_element_type=jnp.float32)


def expert_kernel(per_owner, ids_ref, *refs):
    gates, refs = refs[:per_owner], refs[per_owner:]
    ups, refs = refs[:per_owner], refs[per_owner:]
    downs, refs = refs[:per_owner], refs[per_owner:]
    (
        y_ref, scale_ref,
        part_ref, gate_out, up_out, down_out,
        x2d, c2d, w_in, w_out, act, grads, act_turned, grads_turned, acc_gate, acc_up, acc_down, sems,
    ) = refs
    step = pl.program_id(0)
    blocks, width = y_ref.shape[1], y_ref.shape[4]
    tokens = x2d.shape[0]
    units = gates[0].shape[1]
    half = per_owner * units

    @pl.when(step == 0)
    def _():
        acc_gate[...] = jnp.zeros_like(acc_gate)
        acc_up[...] = jnp.zeros_like(acc_up)
        acc_down[...] = jnp.zeros_like(acc_down)

    for s in range(per_owner):
        w_in[s * units : (s + 1) * units, :] = gates[s][0]
        w_in[half + s * units : half + (s + 1) * units, :] = ups[s][0]
        w_out[s * units : (s + 1) * units, :] = downs[s][0]
    for h in range(blocks):
        x2d[:, h * width : (h + 1) * width] = y_ref[0, h, 0, :tokens]
        c2d[:, h * width : (h + 1) * width] = y_ref[0, h, 1, :tokens]

    scale = scale_ref[0]
    inverse = scale[:, per_owner : per_owner + 1]
    lane = lax.broadcasted_iota(jnp.int32, (tokens, half), 1)
    weight = jnp.broadcast_to(scale[:, :1], (tokens, half))
    for s in range(1, per_owner):
        weight = jnp.where(lane >= s * units, scale[:, s : s + 1], weight)
    turned = ((1,), (1,))
    pre_gate = dot(x2d[...], w_in[:half, :], turned) * inverse
    pre_up = dot(x2d[...], w_in[half:, :], turned) * inverse
    d_act = dot(c2d[...], w_out[...], turned) * weight
    sig = jax.nn.sigmoid(pre_gate)
    swish = pre_gate * sig
    weighted = swish * pre_up * weight
    d_gate = d_act * pre_up * sig * (1.0 + pre_gate * (1.0 - sig))
    d_up = d_act * swish
    act[...] = weighted.astype(act.dtype)
    grads[:, :half] = d_gate.astype(grads.dtype)
    grads[:, half:] = d_up.astype(grads.dtype)
    act_turned[...] = act[...].T
    grads_turned[:half, :] = (d_gate * inverse).astype(grads.dtype).T
    grads_turned[half:, :] = (d_up * inverse).astype(grads.dtype).T

    step_ids = [ids_ref[step * per_owner + s] for s in range(per_owner)]

    def add(acc, e, cols, value):
        acc[e, :, cols] = (acc[e, :, cols].astype(jnp.float32) + value).astype(acc.dtype)

    @pl.loop(0, blocks)
    def _(h):
        cols = pl.ds(pl.multiple_of(h * width, width), width)
        part_ref[0, h, 0] = dot(act[...], w_out[:, cols]).astype(part_ref.dtype)
        part_ref[0, h, 1] = dot(grads[...], w_in[:, cols]).astype(part_ref.dtype)
        down = dot(act_turned[...], c2d[:, cols])
        both = dot(grads_turned[...], x2d[:, cols])
        for s in range(per_owner):
            rows = slice(s * units, (s + 1) * units)
            add(acc_down, step_ids[s], cols, down[rows])
            add(acc_gate, step_ids[s], cols, both[rows])
            add(acc_up, step_ids[s], cols, both[half:][rows])

    @pl.when(step == pl.num_programs(0) - 1)
    def _():
        copies = [
            pltpu.make_async_copy(a, b, sems.at[i])
            for i, (a, b) in enumerate(
                ((acc_gate, gate_out), (acc_up, up_out), (acc_down, down_out))
            )
        ]
        for copy in copies:
            copy.start()
        for copy in copies:
            copy.wait()


def first_rows(count):
    return count // 24 * 16


def gather_kernel(groups, hidden, y_ref, out_ref, local_sem, send_sems, recv_sems):
    g, h = lax.axis_index("group"), lax.axis_index("hidden")
    chips = hidden // 2
    rows_all = y_ref.shape[1]
    cut = first_rows(rows_all)
    rows = (pl.ds(0, cut), pl.ds(cut, rows_all - cut))
    ahead = {"group": g, "hidden": lax.rem(h + 2, hidden)}
    behind = {"group": g, "hidden": lax.rem(h + hidden - 2, hidden)}
    partner = {"group": g, "hidden": h + 1 - 2 * lax.rem(h, 2)}
    peers = [{"group": lax.rem(g + k, groups), "hidden": h} for k in range(groups)]
    mesh_id = pl.DeviceIdType.MESH

    barrier = pltpu.get_barrier_semaphore()
    greeted = [ahead, behind, partner] + peers[1:]
    for device in greeted:
        pl.semaphore_signal(barrier, inc=1, device_id=device, device_id_type=mesh_id)
    pl.semaphore_wait(barrier, len(greeted))

    made = {}

    def send(key, source, g_from, h_from, part, device):
        number = len(made)
        target = out_ref.at[g_from, h_from, :, rows[part]]
        copy = pltpu.make_async_remote_copy(
            src_ref=target if source is None else source,
            dst_ref=target,
            send_sem=send_sems.at[number],
            recv_sem=recv_sems.at[number],
            device_id=device,
            device_id_type=mesh_id,
        )
        copy.start()
        made[key] = copy

    local = pltpu.make_async_copy(y_ref, out_ref.at[g, h], local_sem)
    local.start()
    own = [y_ref.at[:, rows[0]], y_ref.at[:, rows[1]]]
    group_of = [lax.rem(g + groups - k, groups) for k in range(groups)]
    hidden_of = [lax.rem(h + hidden - 2 * t, hidden) for t in range(chips)]
    send(("ring0", 1), own[0], g, h, 0, ahead)
    for k in range(1, groups):
        send(("peer1", 0, k), own[1], g, h, 1, peers[k])
    send(("ring1", 1, 0), own[1], g, h, 1, ahead)
    for k in range(1, groups):
        send(("peer0", 0, k), own[0], g, h, 0, peers[k])
    for part in range(2):
        send(("pair", part, 0, 0), own[part], g, h, part, partner)

    def arrive0(t):
        made[("ring0", t)].wait_recv()
        if t + 1 < chips:
            send(("ring0", t + 1), None, g, hidden_of[t], 0, ahead)
        for k in range(1, groups):
            send(("peer0", t, k), None, g, hidden_of[t], 0, peers[k])
        send(("pair", 0, t, 0), None, g, hidden_of[t], 0, partner)

    def arrive1(t, k):
        made[("ring1", t, k)].wait_recv()
        if t + 1 < chips:
            send(("ring1", t + 1, k), None, group_of[k], hidden_of[t], 1, ahead)
        send(("pair", 1, t, k), None, group_of[k], hidden_of[t], 1, partner)

    def arrive_peer(t, k):
        made[("peer0", t, k)].wait_recv()
        send(("pair", 0, t, k), None, group_of[k], hidden_of[t], 0, partner)

    arrive0(1)
    for k in range(1, groups):
        made[("peer1", 0, k)].wait_recv()
        send(("ring1", 1, k), None, group_of[k], h, 1, ahead)
        send(("pair", 1, 0, k), None, group_of[k], h, 1, partner)
    for t in range(1, chips):
        if t > 1:
            arrive0(t)
        for k in range(1, groups):
            arrive_peer(t - 1, k)
        for k in range(groups):
            arrive1(t, k)
    for k in range(1, groups):
        arrive_peer(chips - 1, k)
    for key, copy in made.items():
        if key[0] == "pair":
            copy.wait_recv()
        copy.wait_send()
    local.wait()


def gather_all(y, groups, hidden):
    chips = hidden // 2
    copies = (chips - 1) * (1 + groups) + (groups - 1) * (1 + chips) + 2 * chips * groups
    return pl.pallas_call(
        functools.partial(gather_kernel, groups, hidden),
        out_shape=jax.ShapeDtypeStruct((groups, hidden) + y.shape, y.dtype),
        in_specs=[pl.BlockSpec(memory_space=pltpu.VMEM)],
        out_specs=pl.BlockSpec(memory_space=pl.ANY),
        scratch_shapes=[
            pltpu.SemaphoreType.DMA,
            pltpu.SemaphoreType.DMA((copies,)),
            pltpu.SemaphoreType.DMA((copies,)),
        ],
        compiler_params=pltpu.CompilerParams(collective_id=0, has_side_effects=True),
        name="gather_all",
    )(y)


def reduce_kernel(
    groups, hidden, parts_ref, out_ref,
    own, pair_in, peer_in0, peer_in1, ring_in0, ring_in1, local_sems, send_sems, recv_sems,
):
    g, h = lax.axis_index("group"), lax.axis_index("hidden")
    chips = hidden // 2
    tokens = out_ref.shape[1]
    cut = first_rows(tokens)
    rows = (pl.ds(0, cut), pl.ds(cut, tokens - cut))
    ahead = {"group": g, "hidden": lax.rem(h + 2, hidden)}
    behind = {"group": g, "hidden": lax.rem(h + hidden - 2, hidden)}
    partner_h = h + 1 - 2 * lax.rem(h, 2)
    partner = {"group": g, "hidden": partner_h}
    group_of = [lax.rem(g + k, groups) for k in range(groups)]
    peers = [{"group": group_of[k], "hidden": h} for k in range(groups)]
    mesh_id = pl.DeviceIdType.MESH

    barrier = pltpu.get_barrier_semaphore()
    greeted = [ahead, behind, partner] + peers[1:]
    for device in greeted:
        pl.semaphore_signal(barrier, inc=1, device_id=device, device_id_type=mesh_id)
    pl.semaphore_wait(barrier, len(greeted))

    made = {}

    def send(key, source, target, device):
        number = len(made)
        copy = pltpu.make_async_remote_copy(
            src_ref=source,
            dst_ref=target,
            send_sem=send_sems.at[number],
            recv_sem=recv_sems.at[number],
            device_id=device,
            device_id_type=mesh_id,
        )
        copy.start()
        made[key] = copy

    def add(into, *others):
        total = into[...].astype(jnp.float32)
        for other in others:
            total = total + other[...].astype(jnp.float32)
        into[...] = total.astype(into.dtype)

    turns = list(range(1, chips)) + [0]
    loads = {}
    for t in turns:
        for k in range(groups):
            theirs = lax.rem(partner_h + hidden - 2 * t, hidden)
            send(("pair", t, k), parts_ref.at[group_of[k], theirs], pair_in.at[k, t], partner)
            mine = lax.rem(h + hidden - 2 * t, hidden)
            loads[t, k] = pltpu.make_async_copy(
                parts_ref.at[group_of[k], mine], own.at[k, t], local_sems.at[k * chips + t]
            )
            loads[t, k].start()

    def half(k, t, part):
        return own.at[k, t, :, rows[part]]

    last = chips - 1
    for t in turns:
        before = t - 1 if t else last
        for k in range(groups):
            loads[t, k].wait()
            made["pair", t, k].wait_recv()
            add(own.at[k, t], pair_in.at[k, t])
            if t == 1:
                send(("ring1", t, k), half(k, t, 1), ring_in1.at[t, k], ahead)
            if k:
                send(("peer0", t, k), half(k, t, 0), peer_in0.at[t, k], peers[k])
        if t != 1:
            for k in list(range(1, groups)) + [0]:
                made["ring1", before, k].wait_recv()
                add(half(k, t, 1), ring_in1.at[before, k])
                if t:
                    send(("ring1", t, k), half(k, t, 1), ring_in1.at[t, k], ahead)
                elif k:
                    send(("peer1", 0, k), half(k, t, 1), peer_in1.at[k], peers[k])
        arrived = []
        for k in range(1, groups):
            made["peer0", t, k].wait_recv()
            arrived.append(peer_in0.at[t, k])
        if t != 1:
            made["ring0", before].wait_recv()
            arrived.append(ring_in0.at[before])
        add(half(0, t, 0), *arrived)
        if t:
            send(("ring0", t), half(0, t, 0), ring_in0.at[t], ahead)
    for k in range(1, groups):
        made["peer1", 0, k].wait_recv()
    add(half(0, 0, 1), *[peer_in1.at[k] for k in range(1, groups)])
    out_ref[...] = own[0, 0]
    for copy in made.values():
        copy.wait_send()


def reduce_parts(parts, collective_id):
    groups, hidden, pieces, tokens, width = parts.shape
    chips = hidden // 2
    block = 2 * pieces * tokens * width
    if 3 * groups * chips * block > 40 << 20:
        flat = parts.reshape((groups * hidden,) + parts.shape[2:])
        return lax.psum_scatter(flat, ("group", "hidden"), scatter_dimension=0, tiled=True)[0]
    copies = (chips - 1) * (1 + groups) + (groups - 1) * (1 + chips) + chips * groups
    cut = first_rows(tokens)
    first, second = (pieces, cut, width), (pieces, tokens - cut, width)
    bf = parts.dtype
    return pl.pallas_call(
        functools.partial(reduce_kernel, groups, hidden),
        out_shape=jax.ShapeDtypeStruct(parts.shape[2:], bf),
        in_specs=[pl.BlockSpec(memory_space=pl.ANY)],
        out_specs=pl.BlockSpec(memory_space=pltpu.VMEM),
        scratch_shapes=[
            pltpu.VMEM((groups, chips) + parts.shape[2:], bf),
            pltpu.VMEM((groups, chips) + parts.shape[2:], bf),
            pltpu.VMEM((chips, groups) + first, bf),
            pltpu.VMEM((groups,) + second, bf),
            pltpu.VMEM((chips,) + first, bf),
            pltpu.VMEM((chips, groups) + second, bf),
            pltpu.SemaphoreType.DMA((chips * groups,)),
            pltpu.SemaphoreType.DMA((copies,)),
            pltpu.SemaphoreType.DMA((copies,)),
        ],
        compiler_params=pltpu.CompilerParams(
            collective_id=collective_id, has_side_effects=True, vmem_limit_bytes=40 << 20
        ),
        name=f"reduce_parts_{collective_id}",
    )(parts)


def to_rows(values, rows, width):
    high = lax.reduce_precision(values, 8, 7)
    rest = values - high
    mid = lax.reduce_precision(rest, 8, 7)
    flat = jnp.stack([high, mid, rest - mid]).reshape(-1).astype(jnp.bfloat16)
    return jnp.pad(flat, (0, rows * width - flat.shape[0])).reshape(rows, width)


def from_rows(block, count):
    flat = block.reshape(block.shape[:2] + (-1,))[:, :, : 3 * count].astype(jnp.float32)
    high, mid, low = (flat[:, :, i * count : (i + 1) * count] for i in range(3))
    return high + mid + low


def experts(order, ids, y, scale, w_gate, w_up, w_down):
    groups, blocks, _, rows, width = y.shape
    tokens = scale.shape[1]
    model = blocks * width
    per_owner = ids.shape[1]
    units = w_down.shape[1]
    half = per_owner * units
    ids_end = groups * per_owner

    def pick(s):
        return pl.BlockSpec((1, units, model), lambda k, n: (n[k * per_owner + s], 0, 0))

    bf = jnp.bfloat16
    parts = jax.ShapeDtypeStruct((groups, blocks, 2, tokens, width), bf)
    return pl.pallas_call(
        functools.partial(expert_kernel, per_owner),
        grid_spec=pltpu.PrefetchScalarGridSpec(
            num_scalar_prefetch=1,
            grid=(groups,),
            in_specs=[pick(s) for s in range(per_owner)] * 3
            + [
                pl.BlockSpec(
                    (1, blocks, 2, rows, width), lambda k, n: (n[ids_end + k], 0, 0, 0, 0)
                ),
                pl.BlockSpec(
                    (1, tokens, scale.shape[2]), lambda k, n: (n[ids_end + k], 0, 0)
                ),
            ],
            out_specs=[
                pl.BlockSpec((1,) + parts.shape[1:], lambda k, n: (n[ids_end + k], 0, 0, 0, 0)),
            ]
            + [pl.BlockSpec(memory_space=pl.ANY)] * 3,
            scratch_shapes=[
                pltpu.VMEM((tokens, model), bf),
                pltpu.VMEM((tokens, model), bf),
                pltpu.VMEM((2 * half, model), bf),
                pltpu.VMEM((half, model), bf),
                pltpu.VMEM((tokens, half), bf),
                pltpu.VMEM((tokens, 2 * half), bf),
                pltpu.VMEM((half, tokens), bf),
                pltpu.VMEM((2 * half, tokens), bf),
                pltpu.VMEM(w_down.shape, bf),
                pltpu.VMEM(w_down.shape, bf),
                pltpu.VMEM(w_down.shape, bf),
                pltpu.SemaphoreType.DMA((3,)),
            ],
        ),
        out_shape=[parts] + [jax.ShapeDtypeStruct(w_down.shape, bf)] * 3,
        compiler_params=pltpu.CompilerParams(vmem_limit_bytes=56 << 20),
        name="experts",
    )(
        jnp.concatenate([ids.reshape(-1), order]),
        *([w_gate] * per_owner + [w_up] * per_owner + [w_down] * per_owner),
        y,
        scale,
    )


def pair_groups(g, i):
    across, along = 1 - i // 2, 1 - lax.rem(i, 2)
    gx, gy = lax.rem(g, 2), g // 2
    return lax.rem(gy + along, 2) * 2 + lax.rem(gx + across, 2)


def near_rows(count):
    return count // 40 * 32


def layer_kernel(
    groups, hidden,
    fetch_ref, q_ref, k_ref, v_ref, proj_ref, cot_ref, res_ref, gain_ref, seats_ref, shares_ref,
    gate_ref, up_ref, down_ref,
    layer_out, normed_out, w_gate, w_up, w_down, cot_all, x_all,
    q, k, v, proj, residual, mixed, f_own, f_stage, f_pair, f_ring, stream, y, slot_rows, slot_all,
    xs, cs, tails, w_in, w_out, act, grads, act_turned, grads_turned, slot_gate, slot_up, slot_down,
    own, stage, pair_in, diag_in, peer_in0, peer_in1, ring_in0, ring_in1,
    load_sems, slot_sems, cot_sems, f_pair_sems, f_ring_sems, y_sems, fetch_sems,
    pair_sems, ring1_sems, diag_sems, peer0_sems, peer1_sems, ring0_sems,
):
    g, h = lax.axis_index("group"), lax.axis_index("hidden")
    chips = hidden // 2
    owned, units, model = w_gate.shape
    tokens, width = layer_out.shape
    per_owner = fetch_ref.shape[1] // groups
    half = per_owner * units
    last, final = chips - 1, groups - 1
    turns = list(range(1, chips)) + [0]
    ahead = {"group": g, "hidden": lax.rem(h + 2, hidden)}
    behind = {"group": g, "hidden": lax.rem(h + hidden - 2, hidden)}
    partner_h = h + 1 - 2 * lax.rem(h, 2)
    partner = {"group": g, "hidden": partner_h}
    mesh_id = pl.DeviceIdType.MESH
    source = [pair_groups(g, i) for i in range(groups)]
    peers = [{"group": source[i], "hidden": h} for i in range(final)]
    turned = ((1,), (1,))

    barrier = pltpu.get_barrier_semaphore()
    greeted = [ahead, behind, partner] + peers
    for device in greeted:
        pl.semaphore_signal(barrier, inc=1, device_id=device, device_id_type=mesh_id)

    my_cols = pl.ds(pl.multiple_of(h * width, width), width)
    moves = (
        (q_ref, q), (k_ref, k), (v_ref, v), (proj_ref, proj), (res_ref.at[:, my_cols], residual),
        (gate_ref, w_gate), (up_ref, w_up), (down_ref, w_down),
    )
    loads = [pltpu.make_async_copy(a, b, load_sems.at[n]) for n, (a, b) in enumerate(moves)]
    for copy in loads:
        copy.start()

    slot_rows[...] = jnp.zeros_like(slot_rows)
    for f in range(groups * per_owner):
        named = jnp.where(seats_ref[...] == f, shares_ref[...], 0.0)
        slot_rows[f // per_owner, f % per_owner : f % per_owner + 1, :] = jnp.sum(
            named, axis=0, keepdims=True
        )
    for buffer in (slot_gate, slot_up, slot_down):
        buffer[per_owner] = jnp.zeros(buffer.shape[1:], buffer.dtype)
    slot_all[g] = slot_rows[g]

    def remote(source_ref, target, sems, index, device):
        return pltpu.make_async_remote_copy(
            src_ref=source_ref,
            dst_ref=target,
            send_sem=sems.at[(0,) + index],
            recv_sem=sems.at[(1,) + index],
            device_id=device,
            device_id_type=mesh_id,
        )

    def add(into, *others):
        total = into[...].astype(jnp.float32)
        for other in others:
            total = total + other[...].astype(jnp.float32)
        into[...] = total.astype(into.dtype)

    pl.semaphore_wait(barrier, len(greeted))

    quarter = tokens // 4
    base = lax.rem(h, 2) * (2 * quarter)
    cot_made = {}

    def piece(n):
        return pl.ds(pl.multiple_of(base + n * quarter, quarter), quarter)

    def landed(i, n):
        return cot_all.at[source[i], piece(n)]

    def send_cot(key, source_ref, target, device):
        copy = remote(source_ref, target, cot_sems, (len(cot_made),), device)
        copy.start()
        cot_made[key] = copy

    for i, n in ((1, 0), (2, 1), (1, 1), (2, 0)):
        send_cot(("near", i, n), cot_ref.at[piece(n)], cot_all.at[g, piece(n)], peers[i])
    slots = [
        remote(slot_rows.at[source[i]], slot_all.at[g], slot_sems, (i,), peers[i])
        for i in range(final)
    ]
    for copy in slots:
        copy.start()

    def pass_cot(i, n, forward):
        cot_made["far" if i == 0 else "near", i, n].wait_recv()
        if forward:
            send_cot(("far", 0, n), landed(i, n), landed(i, n), peers[3 - i])
        send_cot(("pair", i, n), landed(i, n), landed(i, n), partner)

    for copy in loads[:3]:
        copy.wait()
    heads_here = q.shape[1] // HEAD_DIM
    kv = h * heads_here // (HEADS // KV_HEADS)
    kv_cols = pl.ds(pl.multiple_of(kv * HEAD_DIM, HEAD_DIM), HEAD_DIM)
    keys, values = k[:, kv_cols], v[:, kv_cols]
    seen = lax.broadcasted_iota(jnp.int32, (tokens, tokens), 0) >= lax.broadcasted_iota(
        jnp.int32, (tokens, tokens), 1
    )
    for head in range(heads_here):
        cols = slice(head * HEAD_DIM, (head + 1) * HEAD_DIM)
        scores = dot(q[:, cols], keys, turned) / math.sqrt(HEAD_DIM)
        scores = jnp.where(seen, scores, -1e30)
        weights = jnp.exp(scores - jnp.max(scores, axis=-1, keepdims=True))
        total = jnp.sum(weights, axis=-1, keepdims=True)
        mixed[:, cols] = dot((weights / total).astype(mixed.dtype), values).astype(mixed.dtype)

    def f_pair_copy(t):
        return remote(f_stage.at[t], f_pair.at[t], f_pair_sems, (t,), partner)

    def f_ring_copy(t):
        return remote(f_own.at[t], f_ring.at[t], f_ring_sems, (t,), ahead)

    def reduce_task(t):
        f_pair_copy(t).wait_recv()
        if t == 1:
            add(f_own.at[t], f_pair.at[t])
        else:
            before = t - 1 if t else last
            f_ring_copy(before).wait_recv()
            add(f_own.at[t], f_pair.at[t], f_ring.at[before])
        if t:
            f_ring_copy(t).start()

    for copy in loads[3:5]:
        copy.wait()

    @pl.loop(0, chips)
    def _(j):
        t = lax.rem(j + 1, chips)
        for whose, target in ((partner_h, f_stage), (h, f_own)):
            first = pl.multiple_of(lax.rem(whose + hidden - 2 * t, hidden) * width, width)
            target[t] = dot(mixed[...], proj[:, pl.ds(first, width)]).astype(target.dtype)
            if whose is partner_h:
                f_pair_copy(t).start()

        @pl.when(j == 1)
        def _():
            reduce_task(1)

    pass_cot(1, 0, True)
    pass_cot(2, 1, True)
    for t in turns[1:]:
        reduce_task(t)
        if t == 2:
            pass_cot(1, 1, False)
            pass_cot(2, 0, False)

    stream[...] = residual[...].astype(jnp.float32) + f_own[0].astype(jnp.float32)
    y[:tokens, :] = (stream[...] * gain_ref[:, my_cols]).astype(y.dtype)
    squares = jnp.sum(stream[...] * stream[...], axis=-1, keepdims=True)
    squares = jnp.broadcast_to(squares, (tokens, 128)).T[:16]
    high = squares.astype(y.dtype).astype(jnp.float32)
    middle = (squares - high).astype(y.dtype).astype(jnp.float32)
    low = squares - high - middle
    row = lax.broadcasted_iota(jnp.int32, (16, width), 0)
    extras = jnp.zeros((16, width), jnp.float32)
    for c in range(-(-tokens // width)):
        count = min(width, tokens - c * width)
        for n, term in enumerate((high, middle, low)):
            term = term[:, c * width : c * width + count]
            if count < width:
                term = jnp.concatenate([term, jnp.zeros((16, width - count), jnp.float32)], axis=1)
            extras = jnp.where(row == 3 * c + n, term, extras)
    y[tokens:, :] = extras.astype(y.dtype)

    rows_all = y.shape[0]
    near = near_rows(rows_all)
    spans = {0: pl.ds(0, near), 1: pl.ds(near, rows_all - near)}
    spans["a"], spans["b"] = pl.ds(0, near // 2), pl.ds(near // 2, near // 2)
    behind_h = [lax.rem(h + hidden - 2 * t, hidden) for t in range(chips)]
    y_made = {}

    def send_y(key, mine, i, t, span, device):
        target = x_all.at[source[i], behind_h[t], spans[span]]
        copy = remote(
            y.at[spans[span]] if mine else target, target, y_sems, (len(y_made),), device
        )
        copy.start()
        y_made[key] = copy

    home = groups - 1

    def ring_y0(t):
        y_made["ring0", t].wait_recv()
        if t + 1 < chips:
            send_y(("ring0", t + 1), False, home, t, 0, ahead)
        for i in (1, 2):
            send_y(("near0", t, i), False, home, t, 0, peers[i])
        send_y(("pair", home, t, 0), False, home, t, 0, partner)

    def ring_y1(t, i):
        y_made["ring1", t, i].wait_recv()
        if t + 1 < chips:
            send_y(("ring1", t + 1, i), False, i, t, 1, ahead)
        send_y(("pair", i, t, 1), False, i, t, 1, partner)

    def near_y0(t):
        for i, span in ((1, "a"), (2, "b")):
            y_made["near0", t, i].wait_recv()
            send_y(("far0", t, span), False, i, t, span, peers[3 - i])
            send_y(("pair", i, t, 0), False, i, t, 0, partner)

    def far_y0(t):
        for span in ("a", "b"):
            y_made["far0", t, span].wait_recv()
            send_y(("pair", 0, t, span), False, 0, t, span, partner)

    local = pltpu.make_async_copy(y, x_all.at[g, h], load_sems.at[len(moves)])
    local.start()
    send_y(("ring0", 1), True, home, 0, 0, ahead)
    for i in (1, 2):
        send_y(("near0", 0, i), True, home, 0, 0, peers[i])
    for i in (1, 2, 0):
        send_y(("near1", i), True, home, 0, 1, peers[i])
    send_y(("ring1", 1, home), True, home, 0, 1, ahead)
    for span in (0, 1):
        send_y(("pair", home, 0, span), True, home, 0, span, partner)
    pass_cot(0, 0, False)
    pass_cot(0, 1, False)
    ring_y0(1)
    near_y0(0)
    for i in (1, 2, 0):
        y_made["near1", i].wait_recv()
        send_y(("ring1", 1, i), False, i, 0, 1, ahead)
        send_y(("pair", i, 0, 1), False, i, 0, 1, partner)
    ring_y1(1, home)
    for t in range(2, chips):
        ring_y0(t)
        near_y0(t - 1)
        far_y0(t - 2)
        for i in range(final):
            ring_y1(t - 1, i)
        ring_y1(t, home)
    near_y0(last)
    far_y0(last - 1)
    for i in range(final):
        ring_y1(last, i)
    far_y0(last)
    local.wait()
    for made in (cot_made, y_made):
        for key, copy in made.items():
            if key[0] == "pair":
                copy.wait_recv()
            copy.wait_send()
    for copy in slots:
        copy.wait()
    for t in turns:
        f_pair_copy(t).wait_send()
        if t:
            f_ring_copy(t).wait_send()
    for copy in loads[5:]:
        copy.wait()

    cut = first_rows(tokens)
    rows = (pl.ds(0, cut), pl.ds(cut, tokens - cut))
    via = (pl.ds(0, cut // 2), pl.ds(cut // 2, cut // 2))

    def peer(i):
        return {"group": pair_groups(g, i), "hidden": h}

    def fetch_x(i):
        slot = lax.rem(i, 2)
        group = pair_groups(g, i)
        copies = []
        for b in range(hidden):
            cols = pl.ds(b * width, width)
            copies.append(
                pltpu.make_async_copy(
                    x_all.at[group, b, pl.ds(0, tokens)], xs.at[slot, :, cols], fetch_sems.at[slot, b]
                )
            )
            copies.append(
                pltpu.make_async_copy(
                    x_all.at[group, b, pl.ds(tokens, 16)],
                    tails.at[slot, :, cols],
                    fetch_sems.at[slot, hidden + b],
                )
            )
        return copies

    def fetch_c(i, mine):
        slot = lax.rem(i, 2)
        origin = cot_ref if mine else cot_all.at[pair_groups(g, i)]
        return pltpu.make_async_copy(origin, cs.at[slot], fetch_sems.at[slot, 2 * hidden])

    def start_fetch(i):
        for copy in fetch_x(i):
            copy.start()

        @pl.when(i < final)
        def _():
            fetch_c(i, False).start()

        @pl.when(i == final)
        def _():
            fetch_c(i, True).start()

    def wait_fetch(i):
        for copy in fetch_x(i):
            copy.wait()
        fetch_c(i, False).wait()

    def part_of(i, t, part):
        return own.at[i, t, :, rows[part]]

    def pair_copy(i, t):
        return remote(stage.at[lax.rem(i, 2), t], pair_in.at[i, t], pair_sems, (i, t), partner)

    def ring1_copy(i, t):
        return remote(part_of(i, t, 1), ring_in1.at[i, t], ring1_sems, (i, t), ahead)

    def diag_copy(n, t):
        return remote(own.at[0, t, :, via[n]], diag_in.at[n, t], diag_sems, (n, t), peer(n + 1))

    def peer0_copy(i, t):
        return remote(part_of(i, t, 0), peer_in0.at[i - 1, t], peer0_sems, (i - 1, t), peer(i))

    def peer1_copy(i):
        return remote(part_of(i, 0, 1), peer_in1.at[i], peer1_sems, (i,), peer(i))

    def ring0_copy(t):
        return remote(part_of(final, t, 0), ring_in0.at[t], ring0_sems, (t,), ahead)

    def pair_task(i, t):
        pair_copy(i, t).wait_recv()
        add(own.at[i, t], pair_in.at[i, t])
        if t == 1:
            ring1_copy(i, t).start()

        @pl.when(i == 0)
        def _():
            for n in range(2):
                diag_copy(n, t).start()

        for n, step in ((1, 1), (0, 2)):

            @pl.when(i == step)
            def _():
                diag_copy(n, t).wait_recv()
                add(own.at[step, t, :, via[n]], diag_in.at[n, t])
                peer0_copy(step, t).start()

    def ring_task(i, t):
        before = t - 1 if t else last
        ring1_copy(i, before).wait_recv()
        add(part_of(i, t, 1), ring_in1.at[i, before])
        if t:
            ring1_copy(i, t).start()

    def finish_task(t):
        arrived = []
        for i in range(1, final):
            peer0_copy(i, t).wait_recv()
            arrived.append(peer_in0.at[i - 1, t])
        if t != 1:
            before = t - 1 if t else last
            ring0_copy(before).wait_recv()
            arrived.append(ring_in0.at[before])
        add(part_of(final, t, 0), *arrived)
        if t:
            ring0_copy(t).start()

    def finish_ring(i):
        ring_task(i, 0)
        peer1_copy(i).start()

    def scale_of(slot, group):
        terms = jnp.zeros((16, width), jnp.float32)
        for b in range(hidden):
            terms = terms + tails[slot, :, b * width : (b + 1) * width].astype(jnp.float32)
        chunks = []
        for c in range(-(-tokens // width)):
            count = min(width, tokens - c * width)
            total = terms[3 * c : 3 * c + 1] + terms[3 * c + 1 : 3 * c + 2] + terms[3 * c + 2 : 3 * c + 3]
            chunks.append(total[:, :count])
        inverse = lax.rsqrt(jnp.concatenate(chunks, axis=1) / model + epsilon)
        row = lax.broadcasted_iota(jnp.int32, (8, tokens), 0)
        both = jnp.where(row == per_owner, inverse, slot_all[group])
        return jnp.concatenate([both, jnp.zeros((120, tokens), jnp.float32)], axis=0).T

    start_fetch(0)

    @pl.loop(0, groups)
    def _(i):
        slot = lax.rem(i, 2)
        group = pair_groups(g, i)

        @pl.when(i > 0)
        def _():
            pair_task(i - 1, 1)

        @pl.when(i < final)
        def _():
            start_fetch(i + 1)

        for s in range(per_owner):
            e = lax.rem(fetch_ref[group, g * per_owner + s], owned)
            w_in[s * units : (s + 1) * units, :] = w_gate[e]
            w_in[half + s * units : half + (s + 1) * units, :] = w_up[e]
            w_out[s * units : (s + 1) * units, :] = w_down[e]
        wait_fetch(i)
        scale = scale_of(slot, group)
        inverse = scale[:, per_owner : per_owner + 1]
        lane = lax.broadcasted_iota(jnp.int32, (tokens, half), 1)
        weight = jnp.broadcast_to(scale[:, :1], (tokens, half))
        for s in range(1, per_owner):
            weight = jnp.where(lane >= s * units, scale[:, s : s + 1], weight)
        pre_gate = dot(xs[slot], w_in[:half, :], turned) * inverse

        @pl.when(i > 0)
        def _():
            pair_task(i - 1, 2)

        pre_up = dot(xs[slot], w_in[half:, :], turned) * inverse

        @pl.when(i > 0)
        def _():
            pair_task(i - 1, 3)

        @pl.when(i > 1)
        def _():
            ring_task(i - 2, 3)

        d_act = dot(cs[slot], w_out[...], turned) * weight

        @pl.when(i > 0)
        def _():
            pair_task(i - 1, 0)

        sig = jax.nn.sigmoid(pre_gate)
        swish = pre_gate * sig
        weighted = swish * pre_up * weight
        d_gate = d_act * pre_up * sig * (1.0 + pre_gate * (1.0 - sig))
        d_up = d_act * swish
        act[...] = weighted.astype(act.dtype)
        grads[:, :half] = d_gate.astype(grads.dtype)
        grads[:, half:] = d_up.astype(grads.dtype)
        act_turned[i] = act[...].T
        grads_turned[i, :half, :] = (d_gate * inverse).astype(grads.dtype).T
        grads_turned[i, half:, :] = (d_up * inverse).astype(grads.dtype).T

        @pl.loop(0, chips)
        def _(j):
            t = lax.rem(j + 1, chips)

            @pl.when(i > 1)
            def _():
                pair_copy(i - 2, t).wait_send()

            for whose, target, at in ((partner_h, stage, slot), (h, own, i)):
                first = pl.multiple_of(lax.rem(whose + hidden - 2 * t, hidden) * width, width)
                cols = pl.ds(first, width)
                target[at, t, 0] = dot(act[...], w_out[:, cols]).astype(target.dtype)
                target[at, t, 1] = dot(grads[...], w_in[:, cols]).astype(target.dtype)
                if whose is partner_h:
                    pair_copy(i, t).start()

        @pl.when(i > 0)
        def _():
            ring_task(i - 1, 2)

        @pl.when(i > 1)
        def _():
            finish_ring(i - 2)

    for buffer in (w_gate, w_up, w_down):
        buffer[...] = jnp.zeros_like(buffer)

    tasks = (
        (0, lambda: pair_task(final, 1)),
        (1, lambda: pair_task(final, 2)),
        (3, lambda: pair_task(final, 3)),
        (4, lambda: ring_task(final - 1, 3)),
        (5, lambda: pair_task(final, 0)),
        (6, lambda: finish_task(1)),
        (9, lambda: ring_task(final, 2)),
        (12, lambda: finish_ring(final - 1)),
        (15, lambda: finish_task(2)),
        (18, lambda: ring_task(final, 3)),
        (25, lambda: finish_task(3)),
        (27, lambda: ring_task(final, 0)),
    )

    @pl.loop(0, groups * hidden)
    def _(n):
        i, b = final - n // hidden, lax.rem(n, hidden)
        slot = lax.rem(i, 2)
        group = pair_groups(g, i)

        @pl.when((b == 0) & (n > 0) & (i > 0))
        def _():
            start_fetch(i - 1)

        @pl.when((b == 0) & (i < final - 1))
        def _():
            wait_fetch(i)

        cols = pl.ds(pl.multiple_of(b * width, width), width)
        down = dot(act_turned[i], cs[slot, :, cols])
        both = dot(grads_turned[i], xs[slot, :, cols])
        for s in range(per_owner):
            slot_down[s] = down[s * units : (s + 1) * units]
            slot_gate[s] = both[s * units : (s + 1) * units]
            slot_up[s] = both[half + s * units : half + (s + 1) * units]
        listed = [lax.rem(fetch_ref[group, g * per_owner + s], owned) for s in range(per_owner)]
        for e in range(owned):
            seat = jnp.int32(per_owner)
            for s in range(per_owner):
                seat = jnp.where(listed[s] == e, s, seat)
            for total, value in ((w_down, slot_down), (w_gate, slot_gate), (w_up, slot_up)):
                total[e, :, cols] = (total[e, :, cols].astype(jnp.float32) + value[seat]).astype(
                    total.dtype
                )
        for at, task in tasks:
            pl.when(n == at)(task)

    finish_task(0)
    for i in range(final):
        peer1_copy(i).wait_recv()
    add(part_of(final, 0, 1), *[peer_in1.at[i] for i in range(final)])
    layer_out[...] = (stream[...] + own[final, 0, 0].astype(jnp.float32)).astype(layer_out.dtype)
    normed_out[...] = own[final, 0, 1]
    for t in range(chips):
        for i in range(groups):
            if i + 2 >= groups:
                pair_copy(i, t).wait_send()
            if t:
                ring1_copy(i, t).wait_send()
            if 0 < i < final:
                peer0_copy(i, t).wait_send()
        for n in range(2):
            diag_copy(n, t).wait_send()
        if t:
            ring0_copy(t).wait_send()
    for i in range(final):
        peer1_copy(i).wait_send()


def layer(
    fetch_list, queries, key_rows, value_rows, out_proj, cotangent, residual, gain, seats, shares,
    w_gate, w_up, w_down, groups, hidden,
):
    tokens, model = cotangent.shape
    width = model // hidden
    chips = hidden // 2
    owned, units, _ = w_down.shape
    per_owner = fetch_list.shape[1] // groups
    half = per_owner * units
    bf = queries.dtype
    cut = first_rows(tokens)
    block = (2, tokens, width)
    vmem = pl.BlockSpec(memory_space=pltpu.VMEM)
    anywhere = pl.BlockSpec(memory_space=pl.ANY)
    dma = pltpu.SemaphoreType.DMA
    f32 = jnp.float32
    shape = jax.ShapeDtypeStruct
    scratch = [
        (queries.shape, bf), (key_rows.shape, bf), (value_rows.shape, bf), (out_proj.shape, bf),
        ((tokens, width), bf), (queries.shape, bf)
    ]
    scratch += [((chips, tokens, width), bf)] * 4
    scratch += [
        ((tokens, width), f32), ((tokens + 16, width), bf),
        ((groups, 8, tokens), f32), ((groups, 8, tokens), f32),
        ((2, tokens, model), bf), ((2, tokens, model), bf), ((2, 16, model), bf),
        ((2 * half, model), bf), ((half, model), bf), ((tokens, half), bf), ((tokens, 2 * half), bf),
        ((groups, half, tokens), bf), ((groups, 2 * half, tokens), bf),
    ]
    scratch += [((per_owner + 1, units, width), f32)] * 3
    scratch += [
        ((groups, chips) + block, bf), ((2, chips) + block, bf), ((groups, chips) + block, bf),
        ((2, chips, 2, cut // 2, width), bf),
        ((groups - 2, chips, 2, cut, width), bf), ((groups - 1, 2, tokens - cut, width), bf),
        ((chips, 2, cut, width), bf), ((groups, chips, 2, tokens - cut, width), bf),
    ]
    sems = [
        (9,), (2, groups - 1), (2, 12), (2, chips), (2, chips), (2, 72), (2, 2 * hidden + 1),
        (2, groups, chips), (2, groups, chips), (2, 2, chips), (2, groups - 2, chips),
        (2, groups - 1), (2, chips),
    ]
    return pl.pallas_call(
        functools.partial(layer_kernel, groups, hidden),
        in_specs=[pl.BlockSpec(memory_space=pltpu.SMEM)]
        + [anywhere] * 6 + [vmem] * 3 + [anywhere] * 3,
        out_specs=[vmem] * 5 + [anywhere] * 2,
        out_shape=[shape((tokens, width), bf)] * 2
        + [shape(w_down.shape, bf)] * 3
        + [
            shape((groups, tokens, model), bf),
            shape((groups, hidden, tokens + 16, width), bf),
        ],
        scratch_shapes=[pltpu.VMEM(*s) for s in scratch] + [dma(s) for s in sems],
        compiler_params=pltpu.CompilerParams(
            collective_id=1, has_side_effects=True, vmem_limit_bytes=61 << 20
        ),
        name="layer",
    )(
        fetch_list, queries, key_rows, value_rows, out_proj, cotangent, residual, gain, seats,
        shares, w_gate, w_up, w_down,
    )


def shards(
    queries,
    key_rows,
    value_rows,
    out_proj,
    residual,
    norm_gain,
    w_gate,
    w_up,
    w_down,
    route_slot,
    route_weight,
    fetch_list,
    cotangent,
):
    tokens_here, model = cotangent.shape
    hidden_index = lax.axis_index("hidden")
    hidden_count = lax.axis_size("hidden")
    group_index = lax.axis_index("group")
    group_count = lax.axis_size("group")
    per_owner = FETCH // group_count

    if group_count == 4:
        outs = layer(
            fetch_list, queries, key_rows, value_rows, out_proj, cotangent, residual,
            norm_gain[None], route_slot.T, route_weight.T,
            jnp.swapaxes(w_gate, 1, 2), jnp.swapaxes(w_up, 1, 2), w_down,
            group_count, hidden_count,
        )
        return (
            outs[0], outs[1], jnp.swapaxes(outs[2], 1, 2), jnp.swapaxes(outs[3], 1, 2), outs[4]
        )

    chosen = route_slot[:, :, None] == jnp.arange(FETCH, dtype=jnp.int32)[None, None, :]
    slot_weight = jnp.sum(jnp.where(chosen, route_weight[:, :, None], 0.0), axis=1)
    order = (group_index + jnp.arange(group_count, dtype=jnp.int32)) % group_count
    own_cols = lax.dynamic_slice_in_dim(fetch_list, group_index * per_owner, per_owner, 1)
    ids = jnp.take(own_cols - group_index * EXP_GROUP, order, axis=0)

    heads_here = queries.shape[1] // HEAD_DIM
    kv_index = hidden_index * heads_here // (HEADS // KV_HEADS)
    key_block = lax.dynamic_slice_in_dim(key_rows, kv_index * HEAD_DIM, HEAD_DIM, 1)
    value_block = lax.dynamic_slice_in_dim(value_rows, kv_index * HEAD_DIM, HEAD_DIM, 1)
    mixed = attention_rows(queries, key_block, value_block, heads_here)
    partial_value = jnp.dot(mixed, out_proj, preferred_element_type=jnp.float32)
    share_width = model // hidden_count
    first_col = hidden_index * share_width
    blocks = partial_value.astype(jnp.bfloat16).reshape(tokens_here, hidden_count, share_width)
    attn_share = reduce_parts(jnp.swapaxes(blocks, 0, 1)[None, :, None], 2)[0]
    stream = lax.dynamic_slice_in_dim(residual, first_col, share_width, 1).astype(
        jnp.float32
    ) + attn_share.astype(jnp.float32)
    gain = lax.dynamic_slice_in_dim(norm_gain, first_col, share_width, 0)
    squares = jnp.sum(stream * stream, axis=-1)
    gained = (stream * gain).astype(jnp.bfloat16)
    slots_here = FETCH // hidden_count
    slots = lax.dynamic_slice_in_dim(slot_weight.T, hidden_index * slots_here, slots_here, 0)
    extra = -(-3 * slots_here * tokens_here // (16 * share_width)) * 16
    cot_share = lax.dynamic_slice_in_dim(cotangent, first_col, share_width, 1)
    y = jnp.stack(
        [
            jnp.concatenate([gained, to_rows(squares, extra, share_width)]),
            jnp.concatenate([cot_share, to_rows(slots, extra, share_width)]),
        ]
    )
    y_all = gather_all(y, group_count, hidden_count)
    squares_all = from_rows(y_all[:, :, 0, tokens_here:], tokens_here).sum(axis=1)
    inverse = lax.rsqrt(squares_all / model + epsilon)
    weights = from_rows(y_all[:, :, 1, tokens_here:], slots_here * tokens_here)
    weights = weights.reshape(group_count, FETCH, tokens_here)
    weights = lax.dynamic_slice_in_dim(weights, group_index * per_owner, per_owner, 1)
    scale = jnp.concatenate([weights, inverse[:, None, :]], axis=1)
    scale = jnp.pad(scale, ((0, 0), (0, 8 - scale.shape[1]), (0, 0)))
    scale = jnp.swapaxes(scale, 1, 2)
    parts, grad_gate, grad_up, grad_down = experts(
        order,
        ids,
        y_all,
        scale,
        jnp.swapaxes(w_gate, 1, 2),
        jnp.swapaxes(w_up, 1, 2),
        w_down,
    )
    grad_gate = jnp.swapaxes(grad_gate, 1, 2)
    grad_up = jnp.swapaxes(grad_up, 1, 2)
    sums = reduce_parts(parts, 1)
    layer_out = (stream + sums[0].astype(jnp.float32)).astype(jnp.bfloat16)
    return (layer_out, sums[1], grad_gate, grad_up, grad_down)


def solution(mesh):
    return jax.shard_map(
        shards,
        mesh=mesh,
        in_specs=(
            P("group", "hidden"),
            P("group", None),
            P("group", None),
            P("hidden", None),
            P("group", None),
            P(),
            P("group", None, "hidden"),
            P("group", None, "hidden"),
            P("group", "hidden", None),
            P("group", None),
            P("group", None),
            P(),
            P("group", None),
        ),
        out_specs=(
            P("group", "hidden"),
            P("group", "hidden"),
            P("group", None, "hidden"),
            P("group", None, "hidden"),
            P("group", "hidden", None),
        ),
        check_vma=False,
    )
```

```python
import functools
import math

import jax
import jax.numpy as jnp
from jax import lax
from jax.experimental import pallas as pl
from jax.experimental.pallas import tpu as pltpu
from jax.sharding import PartitionSpec as P

HEADS = 32
KV_HEADS = 4
HEAD_DIM = 128
EXP_GROUP = 8
FETCH = 16

epsilon = 1e-06
STORE_LIMIT = 4 << 20


def attention_rows(query_in, key_block, value_block, heads_here):
    tokens_here = query_in.shape[0]
    query_heads = query_in.reshape(tokens_here, heads_here, HEAD_DIM)
    pos = jnp.arange(tokens_here, dtype=jnp.int32)
    scores = jnp.einsum(
        "thd,sd->hts", query_heads, key_block, preferred_element_type=jnp.float32
    ) / math.sqrt(HEAD_DIM)
    scores = jnp.where(pos[:, None] >= pos[None, :], scores, -1e30)
    row_peak = jnp.max(scores, axis=-1, keepdims=True)
    weights = jnp.exp(scores - row_peak)
    probabilities = (weights / jnp.sum(weights, axis=-1, keepdims=True)).astype(jnp.bfloat16)
    mixed = jnp.einsum("hts,sd->thd", probabilities, value_block, preferred_element_type=jnp.float32)
    return mixed.astype(jnp.bfloat16).reshape(tokens_here, heads_here * HEAD_DIM)


def dot(a, b, dims=((1,), (0,))):
    return lax.dot_general(a, b, (dims, ((), ())), preferred_element_type=jnp.float32)


def expert_kernel(per_owner, ids_ref, *refs):
    gates, refs = refs[:per_owner], refs[per_owner:]
    ups, refs = refs[:per_owner], refs[per_owner:]
    downs, refs = refs[:per_owner], refs[per_owner:]
    (
        y_ref, scale_ref,
        part_ref, gate_out, up_out, down_out,
        x2d, c2d, w_in, w_out, act, grads, act_turned, grads_turned, acc_gate, acc_up, acc_down, sems,
    ) = refs
    step = pl.program_id(0)
    blocks, width = y_ref.shape[1], y_ref.shape[4]
    tokens = x2d.shape[0]
    units = gates[0].shape[1]
    half = per_owner * units

    @pl.when(step == 0)
    def _():
        acc_gate[...] = jnp.zeros_like(acc_gate)
        acc_up[...] = jnp.zeros_like(acc_up)
        acc_down[...] = jnp.zeros_like(acc_down)

    for s in range(per_owner):
        w_in[s * units : (s + 1) * units, :] = gates[s][0]
        w_in[half + s * units : half + (s + 1) * units, :] = ups[s][0]
        w_out[s * units : (s + 1) * units, :] = downs[s][0]
    for h in range(blocks):
        x2d[:, h * width : (h + 1) * width] = y_ref[0, h, 0, :tokens]
        c2d[:, h * width : (h + 1) * width] = y_ref[0, h, 1, :tokens]

    scale = scale_ref[0]
    inverse = scale[:, per_owner : per_owner + 1]
    lane = lax.broadcasted_iota(jnp.int32, (tokens, half), 1)
    weight = jnp.broadcast_to(scale[:, :1], (tokens, half))
    for s in range(1, per_owner):
        weight = jnp.where(lane >= s * units, scale[:, s : s + 1], weight)
    turned = ((1,), (1,))
    pre_gate = dot(x2d[...], w_in[:half, :], turned) * inverse
    pre_up = dot(x2d[...], w_in[half:, :], turned) * inverse
    d_act = dot(c2d[...], w_out[...], turned) * weight
    sig = jax.nn.sigmoid(pre_gate)
    swish = pre_gate * sig
    weighted = swish * pre_up * weight
    d_gate = d_act * pre_up * sig * (1.0 + pre_gate * (1.0 - sig))
    d_up = d_act * swish
    act[...] = weighted.astype(act.dtype)
    grads[:, :half] = d_gate.astype(grads.dtype)
    grads[:, half:] = d_up.astype(grads.dtype)
    act_turned[...] = act[...].T
    grads_turned[:half, :] = (d_gate * inverse).astype(grads.dtype).T
    grads_turned[half:, :] = (d_up * inverse).astype(grads.dtype).T

    step_ids = [ids_ref[step * per_owner + s] for s in range(per_owner)]

    def add(acc, e, cols, value):
        acc[e, :, cols] = (acc[e, :, cols].astype(jnp.float32) + value).astype(acc.dtype)

    @pl.loop(0, blocks)
    def _(h):
        cols = pl.ds(pl.multiple_of(h * width, width), width)
        part_ref[0, h, 0] = dot(act[...], w_out[:, cols]).astype(part_ref.dtype)
        part_ref[0, h, 1] = dot(grads[...], w_in[:, cols]).astype(part_ref.dtype)
        down = dot(act_turned[...], c2d[:, cols])
        both = dot(grads_turned[...], x2d[:, cols])
        for s in range(per_owner):
            rows = slice(s * units, (s + 1) * units)
            add(acc_down, step_ids[s], cols, down[rows])
            add(acc_gate, step_ids[s], cols, both[rows])
            add(acc_up, step_ids[s], cols, both[half:][rows])

    @pl.when(step == pl.num_programs(0) - 1)
    def _():
        copies = [
            pltpu.make_async_copy(a, b, sems.at[i])
            for i, (a, b) in enumerate(
                ((acc_gate, gate_out), (acc_up, up_out), (acc_down, down_out))
            )
        ]
        for copy in copies:
            copy.start()
        for copy in copies:
            copy.wait()


def first_rows(count):
    return count // 24 * 16


def gather_kernel(groups, hidden, y_ref, out_ref, local_sem, send_sems, recv_sems):
    g, h = lax.axis_index("group"), lax.axis_index("hidden")
    chips = hidden // 2
    rows_all = y_ref.shape[1]
    cut = first_rows(rows_all)
    rows = (pl.ds(0, cut), pl.ds(cut, rows_all - cut))
    ahead = {"group": g, "hidden": lax.rem(h + 2, hidden)}
    behind = {"group": g, "hidden": lax.rem(h + hidden - 2, hidden)}
    partner = {"group": g, "hidden": h + 1 - 2 * lax.rem(h, 2)}
    peers = [{"group": lax.rem(g + k, groups), "hidden": h} for k in range(groups)]
    mesh_id = pl.DeviceIdType.MESH

    barrier = pltpu.get_barrier_semaphore()
    greeted = [ahead, behind, partner] + peers[1:]
    for device in greeted:
        pl.semaphore_signal(barrier, inc=1, device_id=device, device_id_type=mesh_id)
    pl.semaphore_wait(barrier, len(greeted))

    made = {}

    def send(key, source, g_from, h_from, part, device):
        number = len(made)
        target = out_ref.at[g_from, h_from, :, rows[part]]
        copy = pltpu.make_async_remote_copy(
            src_ref=target if source is None else source,
            dst_ref=target,
            send_sem=send_sems.at[number],
            recv_sem=recv_sems.at[number],
            device_id=device,
            device_id_type=mesh_id,
        )
        copy.start()
        made[key] = copy

    local = pltpu.make_async_copy(y_ref, out_ref.at[g, h], local_sem)
    local.start()
    own = [y_ref.at[:, rows[0]], y_ref.at[:, rows[1]]]
    group_of = [lax.rem(g + groups - k, groups) for k in range(groups)]
    hidden_of = [lax.rem(h + hidden - 2 * t, hidden) for t in range(chips)]
    send(("ring0", 1), own[0], g, h, 0, ahead)
    for k in range(1, groups):
        send(("peer1", 0, k), own[1], g, h, 1, peers[k])
    send(("ring1", 1, 0), own[1], g, h, 1, ahead)
    for k in range(1, groups):
        send(("peer0", 0, k), own[0], g, h, 0, peers[k])
    for part in range(2):
        send(("pair", part, 0, 0), own[part], g, h, part, partner)

    def arrive0(t):
        made[("ring0", t)].wait_recv()
        if t + 1 < chips:
            send(("ring0", t + 1), None, g, hidden_of[t], 0, ahead)
        for k in range(1, groups):
            send(("peer0", t, k), None, g, hidden_of[t], 0, peers[k])
        send(("pair", 0, t, 0), None, g, hidden_of[t], 0, partner)

    def arrive1(t, k):
        made[("ring1", t, k)].wait_recv()
        if t + 1 < chips:
            send(("ring1", t + 1, k), None, group_of[k], hidden_of[t], 1, ahead)
        send(("pair", 1, t, k), None, group_of[k], hidden_of[t], 1, partner)

    def arrive_peer(t, k):
        made[("peer0", t, k)].wait_recv()
        send(("pair", 0, t, k), None, group_of[k], hidden_of[t], 0, partner)

    arrive0(1)
    for k in range(1, groups):
        made[("peer1", 0, k)].wait_recv()
        send(("ring1", 1, k), None, group_of[k], h, 1, ahead)
        send(("pair", 1, 0, k), None, group_of[k], h, 1, partner)
    for t in range(1, chips):
        if t > 1:
            arrive0(t)
        for k in range(1, groups):
            arrive_peer(t - 1, k)
        for k in range(groups):
            arrive1(t, k)
    for k in range(1, groups):
        arrive_peer(chips - 1, k)
    for key, copy in made.items():
        if key[0] == "pair":
            copy.wait_recv()
        copy.wait_send()
    local.wait()


def gather_all(y, groups, hidden):
    chips = hidden // 2
    copies = (chips - 1) * (1 + groups) + (groups - 1) * (1 + chips) + 2 * chips * groups
    return pl.pallas_call(
        functools.partial(gather_kernel, groups, hidden),
        out_shape=jax.ShapeDtypeStruct((groups, hidden) + y.shape, y.dtype),
        in_specs=[pl.BlockSpec(memory_space=pltpu.VMEM)],
        out_specs=pl.BlockSpec(memory_space=pl.ANY),
        scratch_shapes=[
            pltpu.SemaphoreType.DMA,
            pltpu.SemaphoreType.DMA((copies,)),
            pltpu.SemaphoreType.DMA((copies,)),
        ],
        compiler_params=pltpu.CompilerParams(collective_id=0, has_side_effects=True),
        name="gather_all",
    )(y)


def reduce_kernel(
    groups, hidden, parts_ref, out_ref,
    own, pair_in, peer_in0, peer_in1, ring_in0, ring_in1, local_sems, send_sems, recv_sems,
):
    g, h = lax.axis_index("group"), lax.axis_index("hidden")
    chips = hidden // 2
    tokens = out_ref.shape[1]
    cut = first_rows(tokens)
    rows = (pl.ds(0, cut), pl.ds(cut, tokens - cut))
    ahead = {"group": g, "hidden": lax.rem(h + 2, hidden)}
    behind = {"group": g, "hidden": lax.rem(h + hidden - 2, hidden)}
    partner_h = h + 1 - 2 * lax.rem(h, 2)
    partner = {"group": g, "hidden": partner_h}
    group_of = [lax.rem(g + k, groups) for k in range(groups)]
    peers = [{"group": group_of[k], "hidden": h} for k in range(groups)]
    mesh_id = pl.DeviceIdType.MESH

    barrier = pltpu.get_barrier_semaphore()
    greeted = [ahead, behind, partner] + peers[1:]
    for device in greeted:
        pl.semaphore_signal(barrier, inc=1, device_id=device, device_id_type=mesh_id)
    pl.semaphore_wait(barrier, len(greeted))

    made = {}

    def send(key, source, target, device):
        number = len(made)
        copy = pltpu.make_async_remote_copy(
            src_ref=source,
            dst_ref=target,
            send_sem=send_sems.at[number],
            recv_sem=recv_sems.at[number],
            device_id=device,
            device_id_type=mesh_id,
        )
        copy.start()
        made[key] = copy

    def add(into, *others):
        total = into[...].astype(jnp.float32)
        for other in others:
            total = total + other[...].astype(jnp.float32)
        into[...] = total.astype(into.dtype)

    turns = list(range(1, chips)) + [0]
    loads = {}
    for t in turns:
        for k in range(groups):
            theirs = lax.rem(partner_h + hidden - 2 * t, hidden)
            send(("pair", t, k), parts_ref.at[group_of[k], theirs], pair_in.at[k, t], partner)
            mine = lax.rem(h + hidden - 2 * t, hidden)
            loads[t, k] = pltpu.make_async_copy(
                parts_ref.at[group_of[k], mine], own.at[k, t], local_sems.at[k * chips + t]
            )
            loads[t, k].start()

    def half(k, t, part):
        return own.at[k, t, :, rows[part]]

    last = chips - 1
    for t in turns:
        before = t - 1 if t else last
        for k in range(groups):
            loads[t, k].wait()
            made["pair", t, k].wait_recv()
            add(own.at[k, t], pair_in.at[k, t])
            if t == 1:
                send(("ring1", t, k), half(k, t, 1), ring_in1.at[t, k], ahead)
            if k:
                send(("peer0", t, k), half(k, t, 0), peer_in0.at[t, k], peers[k])
        if t != 1:
            for k in list(range(1, groups)) + [0]:
                made["ring1", before, k].wait_recv()
                add(half(k, t, 1), ring_in1.at[before, k])
                if t:
                    send(("ring1", t, k), half(k, t, 1), ring_in1.at[t, k], ahead)
                elif k:
                    send(("peer1", 0, k), half(k, t, 1), peer_in1.at[k], peers[k])
        arrived = []
        for k in range(1, groups):
            made["peer0", t, k].wait_recv()
            arrived.append(peer_in0.at[t, k])
        if t != 1:
            made["ring0", before].wait_recv()
            arrived.append(ring_in0.at[before])
        add(half(0, t, 0), *arrived)
        if t:
            send(("ring0", t), half(0, t, 0), ring_in0.at[t], ahead)
    for k in range(1, groups):
        made["peer1", 0, k].wait_recv()
    add(half(0, 0, 1), *[peer_in1.at[k] for k in range(1, groups)])
    out_ref[...] = own[0, 0]
    for copy in made.values():
        copy.wait_send()


def reduce_parts(parts, collective_id):
    groups, hidden, pieces, tokens, width = parts.shape
    chips = hidden // 2
    block = 2 * pieces * tokens * width
    if 3 * groups * chips * block > 40 << 20:
        flat = parts.reshape((groups * hidden,) + parts.shape[2:])
        return lax.psum_scatter(flat, ("group", "hidden"), scatter_dimension=0, tiled=True)[0]
    copies = (chips - 1) * (1 + groups) + (groups - 1) * (1 + chips) + chips * groups
    cut = first_rows(tokens)
    first, second = (pieces, cut, width), (pieces, tokens - cut, width)
    bf = parts.dtype
    return pl.pallas_call(
        functools.partial(reduce_kernel, groups, hidden),
        out_shape=jax.ShapeDtypeStruct(parts.shape[2:], bf),
        in_specs=[pl.BlockSpec(memory_space=pl.ANY)],
        out_specs=pl.BlockSpec(memory_space=pltpu.VMEM),
        scratch_shapes=[
            pltpu.VMEM((groups, chips) + parts.shape[2:], bf),
            pltpu.VMEM((groups, chips) + parts.shape[2:], bf),
            pltpu.VMEM((chips, groups) + first, bf),
            pltpu.VMEM((groups,) + second, bf),
            pltpu.VMEM((chips,) + first, bf),
            pltpu.VMEM((chips, groups) + second, bf),
            pltpu.SemaphoreType.DMA((chips * groups,)),
            pltpu.SemaphoreType.DMA((copies,)),
            pltpu.SemaphoreType.DMA((copies,)),
        ],
        compiler_params=pltpu.CompilerParams(
            collective_id=collective_id, has_side_effects=True, vmem_limit_bytes=40 << 20
        ),
        name=f"reduce_parts_{collective_id}",
    )(parts)


def to_rows(values, rows, width):
    high = lax.reduce_precision(values, 8, 7)
    rest = values - high
    mid = lax.reduce_precision(rest, 8, 7)
    flat = jnp.stack([high, mid, rest - mid]).reshape(-1).astype(jnp.bfloat16)
    return jnp.pad(flat, (0, rows * width - flat.shape[0])).reshape(rows, width)


def from_rows(block, count):
    flat = block.reshape(block.shape[:2] + (-1,))[:, :, : 3 * count].astype(jnp.float32)
    high, mid, low = (flat[:, :, i * count : (i + 1) * count] for i in range(3))
    return high + mid + low


def experts(order, ids, y, scale, w_gate, w_up, w_down):
    groups, blocks, _, rows, width = y.shape
    tokens = scale.shape[1]
    model = blocks * width
    per_owner = ids.shape[1]
    units = w_down.shape[1]
    half = per_owner * units
    ids_end = groups * per_owner

    def pick(s):
        return pl.BlockSpec((1, units, model), lambda k, n: (n[k * per_owner + s], 0, 0))

    bf = jnp.bfloat16
    parts = jax.ShapeDtypeStruct((groups, blocks, 2, tokens, width), bf)
    return pl.pallas_call(
        functools.partial(expert_kernel, per_owner),
        grid_spec=pltpu.PrefetchScalarGridSpec(
            num_scalar_prefetch=1,
            grid=(groups,),
            in_specs=[pick(s) for s in range(per_owner)] * 3
            + [
                pl.BlockSpec(
                    (1, blocks, 2, rows, width), lambda k, n: (n[ids_end + k], 0, 0, 0, 0)
                ),
                pl.BlockSpec(
                    (1, tokens, scale.shape[2]), lambda k, n: (n[ids_end + k], 0, 0)
                ),
            ],
            out_specs=[
                pl.BlockSpec((1,) + parts.shape[1:], lambda k, n: (n[ids_end + k], 0, 0, 0, 0)),
            ]
            + [pl.BlockSpec(memory_space=pl.ANY)] * 3,
            scratch_shapes=[
                pltpu.VMEM((tokens, model), bf),
                pltpu.VMEM((tokens, model), bf),
                pltpu.VMEM((2 * half, model), bf),
                pltpu.VMEM((half, model), bf),
                pltpu.VMEM((tokens, half), bf),
                pltpu.VMEM((tokens, 2 * half), bf),
                pltpu.VMEM((half, tokens), bf),
                pltpu.VMEM((2 * half, tokens), bf),
                pltpu.VMEM(w_down.shape, bf),
                pltpu.VMEM(w_down.shape, bf),
                pltpu.VMEM(w_down.shape, bf),
                pltpu.SemaphoreType.DMA((3,)),
            ],
        ),
        out_shape=[parts] + [jax.ShapeDtypeStruct(w_down.shape, bf)] * 3,
        compiler_params=pltpu.CompilerParams(vmem_limit_bytes=56 << 20),
        name="experts",
    )(
        jnp.concatenate([ids.reshape(-1), order]),
        *([w_gate] * per_owner + [w_up] * per_owner + [w_down] * per_owner),
        y,
        scale,
    )


def pair_groups(g, i):
    across, along = 1 - i // 2, 1 - lax.rem(i, 2)
    gx, gy = lax.rem(g, 2), g // 2
    return lax.rem(gy + along, 2) * 2 + lax.rem(gx + across, 2)


def near_rows(count):
    return count // 40 * 32


def layer_kernel(
    groups, hidden,
    fetch_ref, q_ref, k_ref, v_ref, proj_ref, cot_ref, res_ref, gain_ref, seats_ref, shares_ref,
    gate_ref, up_ref, down_ref,
    layer_out, normed_out, w_gate, w_up, w_down, cot_all, x_all,
    q, k, v, proj, residual, mixed, f_own, f_stage, f_pair, f_ring, stream, y, slot_rows, slot_all,
    xs, cs, tails, w_in, w_out, act, grads, act_turned, grads_turned, slot_gate, slot_up, slot_down,
    own, stage, pair_in, diag_in, peer_in0, peer_in1, ring_in0, ring_in1,
    load_sems, slot_sems, cot_sems, f_pair_sems, f_ring_sems, y_sems, fetch_sems,
    pair_sems, ring1_sems, diag_sems, peer0_sems, peer1_sems, ring0_sems,
):
    g, h = lax.axis_index("group"), lax.axis_index("hidden")
    chips = hidden // 2
    owned, units, model = w_gate.shape
    tokens, width = layer_out.shape
    per_owner = fetch_ref.shape[1] // groups
    half = per_owner * units
    last, final = chips - 1, groups - 1
    turns = list(range(1, chips)) + [0]
    ahead = {"group": g, "hidden": lax.rem(h + 2, hidden)}
    behind = {"group": g, "hidden": lax.rem(h + hidden - 2, hidden)}
    partner_h = h + 1 - 2 * lax.rem(h, 2)
    partner = {"group": g, "hidden": partner_h}
    mesh_id = pl.DeviceIdType.MESH
    source = [pair_groups(g, i) for i in range(groups)]
    peers = [{"group": source[i], "hidden": h} for i in range(final)]
    turned = ((1,), (1,))

    barrier = pltpu.get_barrier_semaphore()
    greeted = [ahead, behind, partner] + peers
    for device in greeted:
        pl.semaphore_signal(barrier, inc=1, device_id=device, device_id_type=mesh_id)

    my_cols = pl.ds(pl.multiple_of(h * width, width), width)
    moves = (
        (q_ref, q), (k_ref, k), (v_ref, v), (proj_ref, proj), (res_ref.at[:, my_cols], residual),
        (gate_ref, w_gate), (up_ref, w_up), (down_ref, w_down),
    )
    loads = [pltpu.make_async_copy(a, b, load_sems.at[n]) for n, (a, b) in enumerate(moves)]
    for copy in loads:
        copy.start()

    slot_rows[...] = jnp.zeros_like(slot_rows)
    for f in range(groups * per_owner):
        named = jnp.where(seats_ref[...] == f, shares_ref[...], 0.0)
        slot_rows[f // per_owner, f % per_owner : f % per_owner + 1, :] = jnp.sum(
            named, axis=0, keepdims=True
        )
    for buffer in (slot_gate, slot_up, slot_down):
        buffer[per_owner] = jnp.zeros(buffer.shape[1:], buffer.dtype)
    slot_all[g] = slot_rows[g]

    def remote(source_ref, target, sems, index, device):
        return pltpu.make_async_remote_copy(
            src_ref=source_ref,
            dst_ref=target,
            send_sem=sems.at[(0,) + index],
            recv_sem=sems.at[(1,) + index],
            device_id=device,
            device_id_type=mesh_id,
        )

    def add(into, *others):
        total = into[...].astype(jnp.float32)
        for other in others:
            total = total + other[...].astype(jnp.float32)
        into[...] = total.astype(into.dtype)

    pl.semaphore_wait(barrier, len(greeted))

    quarter = tokens // 4
    base = lax.rem(h, 2) * (2 * quarter)
    cot_made = {}

    def piece(n):
        return pl.ds(pl.multiple_of(base + n * quarter, quarter), quarter)

    def landed(i, n):
        return cot_all.at[source[i], piece(n)]

    def send_cot(key, source_ref, target, device):
        copy = remote(source_ref, target, cot_sems, (len(cot_made),), device)
        copy.start()
        cot_made[key] = copy

    for i, n in ((1, 0), (2, 1), (1, 1), (2, 0)):
        send_cot(("near", i, n), cot_ref.at[piece(n)], cot_all.at[g, piece(n)], peers[i])
    slots = [
        remote(slot_rows.at[source[i]], slot_all.at[g], slot_sems, (i,), peers[i])
        for i in range(final)
    ]
    for copy in slots:
        copy.start()

    def pass_cot(i, n, forward):
        cot_made["far" if i == 0 else "near", i, n].wait_recv()
        if forward:
            send_cot(("far", 0, n), landed(i, n), landed(i, n), peers[3 - i])
        send_cot(("pair", i, n), landed(i, n), landed(i, n), partner)

    for copy in loads[:3]:
        copy.wait()
    heads_here = q.shape[1] // HEAD_DIM
    kv = h * heads_here // (HEADS // KV_HEADS)
    kv_cols = pl.ds(pl.multiple_of(kv * HEAD_DIM, HEAD_DIM), HEAD_DIM)
    keys, values = k[:, kv_cols], v[:, kv_cols]
    seen = lax.broadcasted_iota(jnp.int32, (tokens, tokens), 0) >= lax.broadcasted_iota(
        jnp.int32, (tokens, tokens), 1
    )
    for head in range(heads_here):
        cols = slice(head * HEAD_DIM, (head + 1) * HEAD_DIM)
        scores = dot(q[:, cols], keys, turned) / math.sqrt(HEAD_DIM)
        scores = jnp.where(seen, scores, -1e30)
        weights = jnp.exp(scores - jnp.max(scores, axis=-1, keepdims=True))
        total = jnp.sum(weights, axis=-1, keepdims=True)
        mixed[:, cols] = dot((weights / total).astype(mixed.dtype), values).astype(mixed.dtype)

    def f_pair_copy(t):
        return remote(f_stage.at[t], f_pair.at[t], f_pair_sems, (t,), partner)

    def f_ring_copy(t):
        return remote(f_own.at[t], f_ring.at[t], f_ring_sems, (t,), ahead)

    def reduce_task(t):
        f_pair_copy(t).wait_recv()
        if t == 1:
            add(f_own.at[t], f_pair.at[t])
        else:
            before = t - 1 if t else last
            f_ring_copy(before).wait_recv()
            add(f_own.at[t], f_pair.at[t], f_ring.at[before])
        if t:
            f_ring_copy(t).start()

    for copy in loads[3:5]:
        copy.wait()

    @pl.loop(0, chips)
    def _(j):
        t = lax.rem(j + 1, chips)
        for whose, target in ((partner_h, f_stage), (h, f_own)):
            first = pl.multiple_of(lax.rem(whose + hidden - 2 * t, hidden) * width, width)
            target[t] = dot(mixed[...], proj[:, pl.ds(first, width)]).astype(target.dtype)
            if whose is partner_h:
                f_pair_copy(t).start()

        @pl.when(j == 1)
        def _():
            reduce_task(1)

    pass_cot(1, 0, True)
    pass_cot(2, 1, True)
    for t in turns[1:]:
        reduce_task(t)
        if t == 2:
            pass_cot(1, 1, False)
            pass_cot(2, 0, False)

    stream[...] = residual[...].astype(jnp.float32) + f_own[0].astype(jnp.float32)
    y[:tokens, :] = (stream[...] * gain_ref[:, my_cols]).astype(y.dtype)
    squares = jnp.sum(stream[...] * stream[...], axis=-1, keepdims=True)
    squares = jnp.broadcast_to(squares, (tokens, 128)).T[:16]
    high = squares.astype(y.dtype).astype(jnp.float32)
    middle = (squares - high).astype(y.dtype).astype(jnp.float32)
    low = squares - high - middle
    row = lax.broadcasted_iota(jnp.int32, (16, width), 0)
    extras = jnp.zeros((16, width), jnp.float32)
    for c in range(-(-tokens // width)):
        count = min(width, tokens - c * width)
        for n, term in enumerate((high, middle, low)):
            term = term[:, c * width : c * width + count]
            if count < width:
                term = jnp.concatenate([term, jnp.zeros((16, width - count), jnp.float32)], axis=1)
            extras = jnp.where(row == 3 * c + n, term, extras)
    y[tokens:, :] = extras.astype(y.dtype)

    rows_all = y.shape[0]
    near = near_rows(rows_all)
    spans = {0: pl.ds(0, near), 1: pl.ds(near, rows_all - near)}
    spans["a"], spans["b"] = pl.ds(0, near // 2), pl.ds(near // 2, near // 2)
    behind_h = [lax.rem(h + hidden - 2 * t, hidden) for t in range(chips)]
    y_made = {}

    def send_y(key, mine, i, t, span, device):
        target = x_all.at[source[i], behind_h[t], spans[span]]
        copy = remote(
            y.at[spans[span]] if mine else target, target, y_sems, (len(y_made),), device
        )
        copy.start()
        y_made[key] = copy

    home = groups - 1

    def ring_y0(t):
        y_made["ring0", t].wait_recv()
        if t + 1 < chips:
            send_y(("ring0", t + 1), False, home, t, 0, ahead)
        for i in (1, 2):
            send_y(("near0", t, i), False, home, t, 0, peers[i])
        send_y(("pair", home, t, 0), False, home, t, 0, partner)

    def ring_y1(t, i):
        y_made["ring1", t, i].wait_recv()
        if t + 1 < chips:
            send_y(("ring1", t + 1, i), False, i, t, 1, ahead)
        send_y(("pair", i, t, 1), False, i, t, 1, partner)

    def near_y0(t):
        for i, span in ((1, "a"), (2, "b")):
            y_made["near0", t, i].wait_recv()
            send_y(("far0", t, span), False, i, t, span, peers[3 - i])
            send_y(("pair", i, t, 0), False, i, t, 0, partner)

    def far_y0(t):
        for span in ("a", "b"):
            y_made["far0", t, span].wait_recv()
            send_y(("pair", 0, t, span), False, 0, t, span, partner)

    local = pltpu.make_async_copy(y, x_all.at[g, h], load_sems.at[len(moves)])
    local.start()
    send_y(("ring0", 1), True, home, 0, 0, ahead)
    for i in (1, 2):
        send_y(("near0", 0, i), True, home, 0, 0, peers[i])
    for i in (1, 2, 0):
        send_y(("near1", i), True, home, 0, 1, peers[i])
    send_y(("ring1", 1, home), True, home, 0, 1, ahead)
    for span in (0, 1):
        send_y(("pair", home, 0, span), True, home, 0, span, partner)
    pass_cot(0, 0, False)
    pass_cot(0, 1, False)
    ring_y0(1)
    near_y0(0)
    for i in (1, 2, 0):
        y_made["near1", i].wait_recv()
        send_y(("ring1", 1, i), False, i, 0, 1, ahead)
        send_y(("pair", i, 0, 1), False, i, 0, 1, partner)
    ring_y1(1, home)
    for t in range(2, chips):
        ring_y0(t)
        near_y0(t - 1)
        far_y0(t - 2)
        for i in range(final):
            ring_y1(t - 1, i)
        ring_y1(t, home)
    near_y0(last)
    far_y0(last - 1)
    for i in range(final):
        ring_y1(last, i)
    far_y0(last)
    local.wait()
    for made in (cot_made, y_made):
        for key, copy in made.items():
            if key[0] == "pair":
                copy.wait_recv()
            copy.wait_send()
    for copy in slots:
        copy.wait()
    for t in turns:
        f_pair_copy(t).wait_send()
        if t:
            f_ring_copy(t).wait_send()
    for copy in loads[5:]:
        copy.wait()

    cut = first_rows(tokens)
    rows = (pl.ds(0, cut), pl.ds(cut, tokens - cut))
    via = (pl.ds(0, cut // 2), pl.ds(cut // 2, cut // 2))

    def peer(i):
        return {"group": pair_groups(g, i), "hidden": h}

    def fetch_x(i):
        slot = lax.rem(i, 2)
        group = pair_groups(g, i)
        copies = []
        for b in range(hidden):
            cols = pl.ds(b * width, width)
            copies.append(
                pltpu.make_async_copy(
                    x_all.at[group, b, pl.ds(0, tokens)], xs.at[slot, :, cols], fetch_sems.at[slot, b]
                )
            )
            copies.append(
                pltpu.make_async_copy(
                    x_all.at[group, b, pl.ds(tokens, 16)],
                    tails.at[slot, :, cols],
                    fetch_sems.at[slot, hidden + b],
                )
            )
        return copies

    def fetch_c(i, mine):
        slot = lax.rem(i, 2)
        origin = cot_ref if mine else cot_all.at[pair_groups(g, i)]
        return pltpu.make_async_copy(origin, cs.at[slot], fetch_sems.at[slot, 2 * hidden])

    def start_fetch(i):
        for copy in fetch_x(i):
            copy.start()

        @pl.when(i < final)
        def _():
            fetch_c(i, False).start()

        @pl.when(i == final)
        def _():
            fetch_c(i, True).start()

    def wait_fetch(i):
        for copy in fetch_x(i):
            copy.wait()
        fetch_c(i, False).wait()

    def part_of(i, t, part):
        return own.at[i, t, :, rows[part]]

    def pair_copy(i, t):
        return remote(stage.at[lax.rem(i, 2), t], pair_in.at[i, t], pair_sems, (i, t), partner)

    def ring1_copy(i, t):
        return remote(part_of(i, t, 1), ring_in1.at[i, t], ring1_sems, (i, t), ahead)

    def diag_copy(n, t):
        return remote(own.at[0, t, :, via[n]], diag_in.at[n, t], diag_sems, (n, t), peer(n + 1))

    def peer0_copy(i, t):
        return remote(part_of(i, t, 0), peer_in0.at[i - 1, t], peer0_sems, (i - 1, t), peer(i))

    def peer1_copy(i):
        return remote(part_of(i, 0, 1), peer_in1.at[i], peer1_sems, (i,), peer(i))

    def ring0_copy(t):
        return remote(part_of(final, t, 0), ring_in0.at[t], ring0_sems, (t,), ahead)

    def pair_task(i, t):
        pair_copy(i, t).wait_recv()
        add(own.at[i, t], pair_in.at[i, t])
        if t == 1:
            ring1_copy(i, t).start()

        @pl.when(i == 0)
        def _():
            for n in range(2):
                diag_copy(n, t).start()

        for n, step in ((1, 1), (0, 2)):

            @pl.when(i == step)
            def _():
                diag_copy(n, t).wait_recv()
                add(own.at[step, t, :, via[n]], diag_in.at[n, t])
                peer0_copy(step, t).start()

    def ring_task(i, t):
        before = t - 1 if t else last
        ring1_copy(i, before).wait_recv()
        add(part_of(i, t, 1), ring_in1.at[i, before])
        if t:
            ring1_copy(i, t).start()

    def finish_task(t):
        arrived = []
        for i in range(1, final):
            peer0_copy(i, t).wait_recv()
            arrived.append(peer_in0.at[i - 1, t])
        if t != 1:
            before = t - 1 if t else last
            ring0_copy(before).wait_recv()
            arrived.append(ring_in0.at[before])
        add(part_of(final, t, 0), *arrived)
        if t:
            ring0_copy(t).start()

    def finish_ring(i):
        ring_task(i, 0)
        peer1_copy(i).start()

    def scale_of(slot, group):
        terms = jnp.zeros((16, width), jnp.float32)
        for b in range(hidden):
            terms = terms + tails[slot, :, b * width : (b + 1) * width].astype(jnp.float32)
        chunks = []
        for c in range(-(-tokens // width)):
            count = min(width, tokens - c * width)
            total = terms[3 * c : 3 * c + 1] + terms[3 * c + 1 : 3 * c + 2] + terms[3 * c + 2 : 3 * c + 3]
            chunks.append(total[:, :count])
        inverse = lax.rsqrt(jnp.concatenate(chunks, axis=1) / model + epsilon)
        row = lax.broadcasted_iota(jnp.int32, (8, tokens), 0)
        both = jnp.where(row == per_owner, inverse, slot_all[group])
        return jnp.concatenate([both, jnp.zeros((120, tokens), jnp.float32)], axis=0).T

    start_fetch(0)

    @pl.loop(0, groups)
    def _(i):
        slot = lax.rem(i, 2)
        group = pair_groups(g, i)

        @pl.when(i > 0)
        def _():
            pair_task(i - 1, 1)

        @pl.when(i < final)
        def _():
            start_fetch(i + 1)

        for s in range(per_owner):
            e = lax.rem(fetch_ref[group, g * per_owner + s], owned)
            w_in[s * units : (s + 1) * units, :] = w_gate[e]
            w_in[half + s * units : half + (s + 1) * units, :] = w_up[e]
            w_out[s * units : (s + 1) * units, :] = w_down[e]
        wait_fetch(i)
        scale = scale_of(slot, group)
        inverse = scale[:, per_owner : per_owner + 1]
        lane = lax.broadcasted_iota(jnp.int32, (tokens, half), 1)
        weight = jnp.broadcast_to(scale[:, :1], (tokens, half))
        for s in range(1, per_owner):
            weight = jnp.where(lane >= s * units, scale[:, s : s + 1], weight)
        pre_gate = dot(xs[slot], w_in[:half, :], turned) * inverse

        @pl.when(i > 0)
        def _():
            pair_task(i - 1, 2)

        pre_up = dot(xs[slot], w_in[half:, :], turned) * inverse

        @pl.when(i > 0)
        def _():
            pair_task(i - 1, 3)

        @pl.when(i > 1)
        def _():
            ring_task(i - 2, 3)

        d_act = dot(cs[slot], w_out[...], turned) * weight

        @pl.when(i > 0)
        def _():
            pair_task(i - 1, 0)

        sig = jax.nn.sigmoid(pre_gate)
        swish = pre_gate * sig
        weighted = swish * pre_up * weight
        d_gate = d_act * pre_up * sig * (1.0 + pre_gate * (1.0 - sig))
        d_up = d_act * swish
        act[...] = weighted.astype(act.dtype)
        grads[:, :half] = d_gate.astype(grads.dtype)
        grads[:, half:] = d_up.astype(grads.dtype)
        act_turned[i] = act[...].T
        grads_turned[i, :half, :] = (d_gate * inverse).astype(grads.dtype).T
        grads_turned[i, half:, :] = (d_up * inverse).astype(grads.dtype).T

        @pl.loop(0, chips)
        def _(j):
            t = lax.rem(j + 1, chips)

            @pl.when(i > 1)
            def _():
                pair_copy(i - 2, t).wait_send()

            for whose, target, at in ((partner_h, stage, slot), (h, own, i)):
                first = pl.multiple_of(lax.rem(whose + hidden - 2 * t, hidden) * width, width)
                cols = pl.ds(first, width)
                target[at, t, 0] = dot(act[...], w_out[:, cols]).astype(target.dtype)
                target[at, t, 1] = dot(grads[...], w_in[:, cols]).astype(target.dtype)
                if whose is partner_h:
                    pair_copy(i, t).start()

        @pl.when(i > 0)
        def _():
            ring_task(i - 1, 2)

        @pl.when(i > 1)
        def _():
            finish_ring(i - 2)

    for buffer in (w_gate, w_up, w_down):
        buffer[...] = jnp.zeros_like(buffer)

    tasks = (
        (0, lambda: pair_task(final, 1)),
        (1, lambda: pair_task(final, 2)),
        (3, lambda: pair_task(final, 3)),
        (4, lambda: ring_task(final - 1, 3)),
        (5, lambda: pair_task(final, 0)),
        (6, lambda: finish_task(1)),
        (9, lambda: ring_task(final, 2)),
        (12, lambda: finish_ring(final - 1)),
        (15, lambda: finish_task(2)),
        (18, lambda: ring_task(final, 3)),
        (25, lambda: finish_task(3)),
        (27, lambda: ring_task(final, 0)),
    )

    @pl.loop(0, groups * hidden)
    def _(n):
        i, b = final - n // hidden, lax.rem(n, hidden)
        slot = lax.rem(i, 2)
        group = pair_groups(g, i)

        @pl.when((b == 0) & (n > 0) & (i > 0))
        def _():
            start_fetch(i - 1)

        @pl.when((b == 0) & (i < final - 1))
        def _():
            wait_fetch(i)

        cols = pl.ds(pl.multiple_of(b * width, width), width)
        down = dot(act_turned[i], cs[slot, :, cols])
        both = dot(grads_turned[i], xs[slot, :, cols])
        for s in range(per_owner):
            slot_down[s] = down[s * units : (s + 1) * units]
            slot_gate[s] = both[s * units : (s + 1) * units]
            slot_up[s] = both[half + s * units : half + (s + 1) * units]
        listed = [lax.rem(fetch_ref[group, g * per_owner + s], owned) for s in range(per_owner)]
        for e in range(owned):
            seat = jnp.int32(per_owner)
            for s in range(per_owner):
                seat = jnp.where(listed[s] == e, s, seat)
            for total, value in ((w_down, slot_down), (w_gate, slot_gate), (w_up, slot_up)):
                total[e, :, cols] = (total[e, :, cols].astype(jnp.float32) + value[seat]).astype(
                    total.dtype
                )
        for at, task in tasks:
            pl.when(n == at)(task)

    finish_task(0)
    for i in range(final):
        peer1_copy(i).wait_recv()
    add(part_of(final, 0, 1), *[peer_in1.at[i] for i in range(final)])
    layer_out[...] = (stream[...] + own[final, 0, 0].astype(jnp.float32)).astype(layer_out.dtype)
    normed_out[...] = own[final, 0, 1]
    for t in range(chips):
        for i in range(groups):
            if i + 2 >= groups:
                pair_copy(i, t).wait_send()
            if t:
                ring1_copy(i, t).wait_send()
            if 0 < i < final:
                peer0_copy(i, t).wait_send()
        for n in range(2):
            diag_copy(n, t).wait_send()
        if t:
            ring0_copy(t).wait_send()
    for i in range(final):
        peer1_copy(i).wait_send()


def store_kernel(count, *refs):
    sources, targets, sems = refs[:count], refs[count:-1], refs[-1]
    copies = [
        pltpu.make_async_copy(a, b, sems.at[n]) for n, (a, b) in enumerate(zip(sources, targets))
    ]
    for copy in copies:
        copy.start()
    for copy in copies:
        copy.wait()


def store(*values):
    count = len(values)
    return pl.pallas_call(
        functools.partial(store_kernel, count),
        in_specs=[pl.BlockSpec(memory_space=pltpu.VMEM)] * count,
        out_specs=[pl.BlockSpec(memory_space=pl.ANY)] * count,
        out_shape=[jax.ShapeDtypeStruct(value.shape, value.dtype) for value in values],
        scratch_shapes=[pltpu.SemaphoreType.DMA((count,))],
        compiler_params=pltpu.CompilerParams(vmem_limit_bytes=STORE_LIMIT),
        name="store",
    )(*values)


def layer(
    fetch_list, queries, key_rows, value_rows, out_proj, cotangent, residual, gain, seats, shares,
    w_gate, w_up, w_down, groups, hidden,
):
    tokens, model = cotangent.shape
    width = model // hidden
    chips = hidden // 2
    owned, units, _ = w_down.shape
    per_owner = fetch_list.shape[1] // groups
    half = per_owner * units
    bf = queries.dtype
    cut = first_rows(tokens)
    block = (2, tokens, width)
    vmem = pl.BlockSpec(memory_space=pltpu.VMEM)
    anywhere = pl.BlockSpec(memory_space=pl.ANY)
    dma = pltpu.SemaphoreType.DMA
    f32 = jnp.float32
    shape = jax.ShapeDtypeStruct
    scratch = [
        (queries.shape, bf), (key_rows.shape, bf), (value_rows.shape, bf), (out_proj.shape, bf),
        ((tokens, width), bf), (queries.shape, bf)
    ]
    scratch += [((chips, tokens, width), bf)] * 4
    scratch += [
        ((tokens, width), f32), ((tokens + 16, width), bf),
        ((groups, 8, tokens), f32), ((groups, 8, tokens), f32),
        ((2, tokens, model), bf), ((2, tokens, model), bf), ((2, 16, model), bf),
        ((2 * half, model), bf), ((half, model), bf), ((tokens, half), bf), ((tokens, 2 * half), bf),
        ((groups, half, tokens), bf), ((groups, 2 * half, tokens), bf),
    ]
    scratch += [((per_owner + 1, units, width), f32)] * 3
    scratch += [
        ((groups, chips) + block, bf), ((2, chips) + block, bf), ((groups, chips) + block, bf),
        ((2, chips, 2, cut // 2, width), bf),
        ((groups - 2, chips, 2, cut, width), bf), ((groups - 1, 2, tokens - cut, width), bf),
        ((chips, 2, cut, width), bf), ((groups, chips, 2, tokens - cut, width), bf),
    ]
    sems = [
        (9,), (2, groups - 1), (2, 12), (2, chips), (2, chips), (2, 72), (2, 2 * hidden + 1),
        (2, groups, chips), (2, groups, chips), (2, 2, chips), (2, groups - 2, chips),
        (2, groups - 1), (2, chips),
    ]
    return pl.pallas_call(
        functools.partial(layer_kernel, groups, hidden),
        in_specs=[pl.BlockSpec(memory_space=pltpu.SMEM)]
        + [anywhere] * 6 + [vmem] * 3 + [anywhere] * 3,
        out_specs=[vmem] * 5 + [anywhere] * 2,
        out_shape=[pltpu.VMEM((tokens, width), bf)] * 2
        + [pltpu.VMEM(w_down.shape, bf)] * 3
        + [
            shape((groups, tokens, model), bf),
            shape((groups, hidden, tokens + 16, width), bf),
        ],
        scratch_shapes=[pltpu.VMEM(*s) for s in scratch] + [dma(s) for s in sems],
        compiler_params=pltpu.CompilerParams(
            collective_id=1, has_side_effects=True, vmem_limit_bytes=51 << 20
        ),
        name="layer",
    )(
        fetch_list, queries, key_rows, value_rows, out_proj, cotangent, residual, gain, seats,
        shares, w_gate, w_up, w_down,
    )


def shards(
    queries,
    key_rows,
    value_rows,
    out_proj,
    residual,
    norm_gain,
    w_gate,
    w_up,
    w_down,
    route_slot,
    route_weight,
    fetch_list,
    cotangent,
):
    tokens_here, model = cotangent.shape
    hidden_index = lax.axis_index("hidden")
    hidden_count = lax.axis_size("hidden")
    group_index = lax.axis_index("group")
    group_count = lax.axis_size("group")
    per_owner = FETCH // group_count

    if group_count == 4:
        outs = layer(
            fetch_list, queries, key_rows, value_rows, out_proj, cotangent, residual,
            norm_gain[None], route_slot.T, route_weight.T,
            jnp.swapaxes(w_gate, 1, 2), jnp.swapaxes(w_up, 1, 2), w_down,
            group_count, hidden_count,
        )
        outs = store(*outs[:5])
        return (
            outs[0], outs[1], jnp.swapaxes(outs[2], 1, 2), jnp.swapaxes(outs[3], 1, 2), outs[4]
        )

    chosen = route_slot[:, :, None] == jnp.arange(FETCH, dtype=jnp.int32)[None, None, :]
    slot_weight = jnp.sum(jnp.where(chosen, route_weight[:, :, None], 0.0), axis=1)
    order = (group_index + jnp.arange(group_count, dtype=jnp.int32)) % group_count
    own_cols = lax.dynamic_slice_in_dim(fetch_list, group_index * per_owner, per_owner, 1)
    ids = jnp.take(own_cols - group_index * EXP_GROUP, order, axis=0)

    heads_here = queries.shape[1] // HEAD_DIM
    kv_index = hidden_index * heads_here // (HEADS // KV_HEADS)
    key_block = lax.dynamic_slice_in_dim(key_rows, kv_index * HEAD_DIM, HEAD_DIM, 1)
    value_block = lax.dynamic_slice_in_dim(value_rows, kv_index * HEAD_DIM, HEAD_DIM, 1)
    mixed = attention_rows(queries, key_block, value_block, heads_here)
    partial_value = jnp.dot(mixed, out_proj, preferred_element_type=jnp.float32)
    share_width = model // hidden_count
    first_col = hidden_index * share_width
    blocks = partial_value.astype(jnp.bfloat16).reshape(tokens_here, hidden_count, share_width)
    attn_share = reduce_parts(jnp.swapaxes(blocks, 0, 1)[None, :, None], 2)[0]
    stream = lax.dynamic_slice_in_dim(residual, first_col, share_width, 1).astype(
        jnp.float32
    ) + attn_share.astype(jnp.float32)
    gain = lax.dynamic_slice_in_dim(norm_gain, first_col, share_width, 0)
    squares = jnp.sum(stream * stream, axis=-1)
    gained = (stream * gain).astype(jnp.bfloat16)
    slots_here = FETCH // hidden_count
    slots = lax.dynamic_slice_in_dim(slot_weight.T, hidden_index * slots_here, slots_here, 0)
    extra = -(-3 * slots_here * tokens_here // (16 * share_width)) * 16
    cot_share = lax.dynamic_slice_in_dim(cotangent, first_col, share_width, 1)
    y = jnp.stack(
        [
            jnp.concatenate([gained, to_rows(squares, extra, share_width)]),
            jnp.concatenate([cot_share, to_rows(slots, extra, share_width)]),
        ]
    )
    y_all = gather_all(y, group_count, hidden_count)
    squares_all = from_rows(y_all[:, :, 0, tokens_here:], tokens_here).sum(axis=1)
    inverse = lax.rsqrt(squares_all / model + epsilon)
    weights = from_rows(y_all[:, :, 1, tokens_here:], slots_here * tokens_here)
    weights = weights.reshape(group_count, FETCH, tokens_here)
    weights = lax.dynamic_slice_in_dim(weights, group_index * per_owner, per_owner, 1)
    scale = jnp.concatenate([weights, inverse[:, None, :]], axis=1)
    scale = jnp.pad(scale, ((0, 0), (0, 8 - scale.shape[1]), (0, 0)))
    scale = jnp.swapaxes(scale, 1, 2)
    parts, grad_gate, grad_up, grad_down = experts(
        order,
        ids,
        y_all,
        scale,
        jnp.swapaxes(w_gate, 1, 2),
        jnp.swapaxes(w_up, 1, 2),
        w_down,
    )
    grad_gate = jnp.swapaxes(grad_gate, 1, 2)
    grad_up = jnp.swapaxes(grad_up, 1, 2)
    sums = reduce_parts(parts, 1)
    layer_out = (stream + sums[0].astype(jnp.float32)).astype(jnp.bfloat16)
    return (layer_out, sums[1], grad_gate, grad_up, grad_down)


def solution(mesh):
    return jax.shard_map(
        shards,
        mesh=mesh,
        in_specs=(
            P("group", "hidden"),
            P("group", None),
            P("group", None),
            P("hidden", None),
            P("group", None),
            P(),
            P("group", None, "hidden"),
            P("group", None, "hidden"),
            P("group", "hidden", None),
            P("group", None),
            P("group", None),
            P(),
            P("group", None),
        ),
        out_specs=(
            P("group", "hidden"),
            P("group", "hidden"),
            P("group", None, "hidden"),
            P("group", None, "hidden"),
            P("group", "hidden", None),
        ),
        check_vma=False,
    )
```

```python
import functools
import math

import jax
import jax.numpy as jnp
from jax import lax
from jax.experimental import pallas as pl
from jax.experimental.pallas import tpu as pltpu
from jax.sharding import PartitionSpec as P

HEADS = 32
KV_HEADS = 4
HEAD_DIM = 128
EXP_GROUP = 8
FETCH = 16

epsilon = 1e-06
STORE_LIMIT = 4 << 20


def attention_rows(query_in, key_block, value_block, heads_here):
    tokens_here = query_in.shape[0]
    query_heads = query_in.reshape(tokens_here, heads_here, HEAD_DIM)
    pos = jnp.arange(tokens_here, dtype=jnp.int32)
    scores = jnp.einsum(
        "thd,sd->hts", query_heads, key_block, preferred_element_type=jnp.float32
    ) / math.sqrt(HEAD_DIM)
    scores = jnp.where(pos[:, None] >= pos[None, :], scores, -1e30)
    row_peak = jnp.max(scores, axis=-1, keepdims=True)
    weights = jnp.exp(scores - row_peak)
    probabilities = (weights / jnp.sum(weights, axis=-1, keepdims=True)).astype(jnp.bfloat16)
    mixed = jnp.einsum("hts,sd->thd", probabilities, value_block, preferred_element_type=jnp.float32)
    return mixed.astype(jnp.bfloat16).reshape(tokens_here, heads_here * HEAD_DIM)


def dot(a, b, dims=((1,), (0,))):
    return lax.dot_general(a, b, (dims, ((), ())), preferred_element_type=jnp.float32)


def expert_kernel(per_owner, ids_ref, *refs):
    gates, refs = refs[:per_owner], refs[per_owner:]
    ups, refs = refs[:per_owner], refs[per_owner:]
    downs, refs = refs[:per_owner], refs[per_owner:]
    (
        y_ref, scale_ref,
        part_ref, gate_out, up_out, down_out,
        x2d, c2d, w_in, w_out, act, grads, act_turned, grads_turned, acc_gate, acc_up, acc_down, sems,
    ) = refs
    step = pl.program_id(0)
    blocks, width = y_ref.shape[1], y_ref.shape[4]
    tokens = x2d.shape[0]
    units = gates[0].shape[1]
    half = per_owner * units

    @pl.when(step == 0)
    def _():
        acc_gate[...] = jnp.zeros_like(acc_gate)
        acc_up[...] = jnp.zeros_like(acc_up)
        acc_down[...] = jnp.zeros_like(acc_down)

    for s in range(per_owner):
        w_in[s * units : (s + 1) * units, :] = gates[s][0]
        w_in[half + s * units : half + (s + 1) * units, :] = ups[s][0]
        w_out[s * units : (s + 1) * units, :] = downs[s][0]
    for h in range(blocks):
        x2d[:, h * width : (h + 1) * width] = y_ref[0, h, 0, :tokens]
        c2d[:, h * width : (h + 1) * width] = y_ref[0, h, 1, :tokens]

    scale = scale_ref[0]
    inverse = scale[:, per_owner : per_owner + 1]
    lane = lax.broadcasted_iota(jnp.int32, (tokens, half), 1)
    weight = jnp.broadcast_to(scale[:, :1], (tokens, half))
    for s in range(1, per_owner):
        weight = jnp.where(lane >= s * units, scale[:, s : s + 1], weight)
    turned = ((1,), (1,))
    pre_gate = dot(x2d[...], w_in[:half, :], turned) * inverse
    pre_up = dot(x2d[...], w_in[half:, :], turned) * inverse
    d_act = dot(c2d[...], w_out[...], turned) * weight
    sig = jax.nn.sigmoid(pre_gate)
    swish = pre_gate * sig
    weighted = swish * pre_up * weight
    d_gate = d_act * pre_up * sig * (1.0 + pre_gate * (1.0 - sig))
    d_up = d_act * swish
    act[...] = weighted.astype(act.dtype)
    grads[:, :half] = d_gate.astype(grads.dtype)
    grads[:, half:] = d_up.astype(grads.dtype)
    act_turned[...] = act[...].T
    grads_turned[:half, :] = (d_gate * inverse).astype(grads.dtype).T
    grads_turned[half:, :] = (d_up * inverse).astype(grads.dtype).T

    step_ids = [ids_ref[step * per_owner + s] for s in range(per_owner)]

    def add(acc, e, cols, value):
        acc[e, :, cols] = (acc[e, :, cols].astype(jnp.float32) + value).astype(acc.dtype)

    @pl.loop(0, blocks)
    def _(h):
        cols = pl.ds(pl.multiple_of(h * width, width), width)
        part_ref[0, h, 0] = dot(act[...], w_out[:, cols]).astype(part_ref.dtype)
        part_ref[0, h, 1] = dot(grads[...], w_in[:, cols]).astype(part_ref.dtype)
        down = dot(act_turned[...], c2d[:, cols])
        both = dot(grads_turned[...], x2d[:, cols])
        for s in range(per_owner):
            rows = slice(s * units, (s + 1) * units)
            add(acc_down, step_ids[s], cols, down[rows])
            add(acc_gate, step_ids[s], cols, both[rows])
            add(acc_up, step_ids[s], cols, both[half:][rows])

    @pl.when(step == pl.num_programs(0) - 1)
    def _():
        copies = [
            pltpu.make_async_copy(a, b, sems.at[i])
            for i, (a, b) in enumerate(
                ((acc_gate, gate_out), (acc_up, up_out), (acc_down, down_out))
            )
        ]
        for copy in copies:
            copy.start()
        for copy in copies:
            copy.wait()


def first_rows(count):
    return count // 24 * 16


def gather_kernel(groups, hidden, y_ref, out_ref, local_sem, send_sems, recv_sems):
    g, h = lax.axis_index("group"), lax.axis_index("hidden")
    chips = hidden // 2
    rows_all = y_ref.shape[1]
    cut = first_rows(rows_all)
    rows = (pl.ds(0, cut), pl.ds(cut, rows_all - cut))
    ahead = {"group": g, "hidden": lax.rem(h + 2, hidden)}
    behind = {"group": g, "hidden": lax.rem(h + hidden - 2, hidden)}
    partner = {"group": g, "hidden": h + 1 - 2 * lax.rem(h, 2)}
    peers = [{"group": lax.rem(g + k, groups), "hidden": h} for k in range(groups)]
    mesh_id = pl.DeviceIdType.MESH

    barrier = pltpu.get_barrier_semaphore()
    greeted = [ahead, behind, partner] + peers[1:]
    for device in greeted:
        pl.semaphore_signal(barrier, inc=1, device_id=device, device_id_type=mesh_id)
    pl.semaphore_wait(barrier, len(greeted))

    made = {}

    def send(key, source, g_from, h_from, part, device):
        number = len(made)
        target = out_ref.at[g_from, h_from, :, rows[part]]
        copy = pltpu.make_async_remote_copy(
            src_ref=target if source is None else source,
            dst_ref=target,
            send_sem=send_sems.at[number],
            recv_sem=recv_sems.at[number],
            device_id=device,
            device_id_type=mesh_id,
        )
        copy.start()
        made[key] = copy

    local = pltpu.make_async_copy(y_ref, out_ref.at[g, h], local_sem)
    local.start()
    own = [y_ref.at[:, rows[0]], y_ref.at[:, rows[1]]]
    group_of = [lax.rem(g + groups - k, groups) for k in range(groups)]
    hidden_of = [lax.rem(h + hidden - 2 * t, hidden) for t in range(chips)]
    send(("ring0", 1), own[0], g, h, 0, ahead)
    for k in range(1, groups):
        send(("peer1", 0, k), own[1], g, h, 1, peers[k])
    send(("ring1", 1, 0), own[1], g, h, 1, ahead)
    for k in range(1, groups):
        send(("peer0", 0, k), own[0], g, h, 0, peers[k])
    for part in range(2):
        send(("pair", part, 0, 0), own[part], g, h, part, partner)

    def arrive0(t):
        made[("ring0", t)].wait_recv()
        if t + 1 < chips:
            send(("ring0", t + 1), None, g, hidden_of[t], 0, ahead)
        for k in range(1, groups):
            send(("peer0", t, k), None, g, hidden_of[t], 0, peers[k])
        send(("pair", 0, t, 0), None, g, hidden_of[t], 0, partner)

    def arrive1(t, k):
        made[("ring1", t, k)].wait_recv()
        if t + 1 < chips:
            send(("ring1", t + 1, k), None, group_of[k], hidden_of[t], 1, ahead)
        send(("pair", 1, t, k), None, group_of[k], hidden_of[t], 1, partner)

    def arrive_peer(t, k):
        made[("peer0", t, k)].wait_recv()
        send(("pair", 0, t, k), None, group_of[k], hidden_of[t], 0, partner)

    arrive0(1)
    for k in range(1, groups):
        made[("peer1", 0, k)].wait_recv()
        send(("ring1", 1, k), None, group_of[k], h, 1, ahead)
        send(("pair", 1, 0, k), None, group_of[k], h, 1, partner)
    for t in range(1, chips):
        if t > 1:
            arrive0(t)
        for k in range(1, groups):
            arrive_peer(t - 1, k)
        for k in range(groups):
            arrive1(t, k)
    for k in range(1, groups):
        arrive_peer(chips - 1, k)
    for key, copy in made.items():
        if key[0] == "pair":
            copy.wait_recv()
        copy.wait_send()
    local.wait()


def gather_all(y, groups, hidden):
    chips = hidden // 2
    copies = (chips - 1) * (1 + groups) + (groups - 1) * (1 + chips) + 2 * chips * groups
    return pl.pallas_call(
        functools.partial(gather_kernel, groups, hidden),
        out_shape=jax.ShapeDtypeStruct((groups, hidden) + y.shape, y.dtype),
        in_specs=[pl.BlockSpec(memory_space=pltpu.VMEM)],
        out_specs=pl.BlockSpec(memory_space=pl.ANY),
        scratch_shapes=[
            pltpu.SemaphoreType.DMA,
            pltpu.SemaphoreType.DMA((copies,)),
            pltpu.SemaphoreType.DMA((copies,)),
        ],
        compiler_params=pltpu.CompilerParams(collective_id=0, has_side_effects=True),
        name="gather_all",
    )(y)


def reduce_kernel(
    groups, hidden, parts_ref, out_ref,
    own, pair_in, peer_in0, peer_in1, ring_in0, ring_in1, local_sems, send_sems, recv_sems,
):
    g, h = lax.axis_index("group"), lax.axis_index("hidden")
    chips = hidden // 2
    tokens = out_ref.shape[1]
    cut = first_rows(tokens)
    rows = (pl.ds(0, cut), pl.ds(cut, tokens - cut))
    ahead = {"group": g, "hidden": lax.rem(h + 2, hidden)}
    behind = {"group": g, "hidden": lax.rem(h + hidden - 2, hidden)}
    partner_h = h + 1 - 2 * lax.rem(h, 2)
    partner = {"group": g, "hidden": partner_h}
    group_of = [lax.rem(g + k, groups) for k in range(groups)]
    peers = [{"group": group_of[k], "hidden": h} for k in range(groups)]
    mesh_id = pl.DeviceIdType.MESH

    barrier = pltpu.get_barrier_semaphore()
    greeted = [ahead, behind, partner] + peers[1:]
    for device in greeted:
        pl.semaphore_signal(barrier, inc=1, device_id=device, device_id_type=mesh_id)
    pl.semaphore_wait(barrier, len(greeted))

    made = {}

    def send(key, source, target, device):
        number = len(made)
        copy = pltpu.make_async_remote_copy(
            src_ref=source,
            dst_ref=target,
            send_sem=send_sems.at[number],
            recv_sem=recv_sems.at[number],
            device_id=device,
            device_id_type=mesh_id,
        )
        copy.start()
        made[key] = copy

    def add(into, *others):
        total = into[...].astype(jnp.float32)
        for other in others:
            total = total + other[...].astype(jnp.float32)
        into[...] = total.astype(into.dtype)

    turns = list(range(1, chips)) + [0]
    loads = {}
    for t in turns:
        for k in range(groups):
            theirs = lax.rem(partner_h + hidden - 2 * t, hidden)
            send(("pair", t, k), parts_ref.at[group_of[k], theirs], pair_in.at[k, t], partner)
            mine = lax.rem(h + hidden - 2 * t, hidden)
            loads[t, k] = pltpu.make_async_copy(
                parts_ref.at[group_of[k], mine], own.at[k, t], local_sems.at[k * chips + t]
            )
            loads[t, k].start()

    def half(k, t, part):
        return own.at[k, t, :, rows[part]]

    last = chips - 1
    for t in turns:
        before = t - 1 if t else last
        for k in range(groups):
            loads[t, k].wait()
            made["pair", t, k].wait_recv()
            add(own.at[k, t], pair_in.at[k, t])
            if t == 1:
                send(("ring1", t, k), half(k, t, 1), ring_in1.at[t, k], ahead)
            if k:
                send(("peer0", t, k), half(k, t, 0), peer_in0.at[t, k], peers[k])
        if t != 1:
            for k in list(range(1, groups)) + [0]:
                made["ring1", before, k].wait_recv()
                add(half(k, t, 1), ring_in1.at[before, k])
                if t:
                    send(("ring1", t, k), half(k, t, 1), ring_in1.at[t, k], ahead)
                elif k:
                    send(("peer1", 0, k), half(k, t, 1), peer_in1.at[k], peers[k])
        arrived = []
        for k in range(1, groups):
            made["peer0", t, k].wait_recv()
            arrived.append(peer_in0.at[t, k])
        if t != 1:
            made["ring0", before].wait_recv()
            arrived.append(ring_in0.at[before])
        add(half(0, t, 0), *arrived)
        if t:
            send(("ring0", t), half(0, t, 0), ring_in0.at[t], ahead)
    for k in range(1, groups):
        made["peer1", 0, k].wait_recv()
    add(half(0, 0, 1), *[peer_in1.at[k] for k in range(1, groups)])
    out_ref[...] = own[0, 0]
    for copy in made.values():
        copy.wait_send()


def reduce_parts(parts, collective_id):
    groups, hidden, pieces, tokens, width = parts.shape
    chips = hidden // 2
    block = 2 * pieces * tokens * width
    if 3 * groups * chips * block > 40 << 20:
        flat = parts.reshape((groups * hidden,) + parts.shape[2:])
        return lax.psum_scatter(flat, ("group", "hidden"), scatter_dimension=0, tiled=True)[0]
    copies = (chips - 1) * (1 + groups) + (groups - 1) * (1 + chips) + chips * groups
    cut = first_rows(tokens)
    first, second = (pieces, cut, width), (pieces, tokens - cut, width)
    bf = parts.dtype
    return pl.pallas_call(
        functools.partial(reduce_kernel, groups, hidden),
        out_shape=jax.ShapeDtypeStruct(parts.shape[2:], bf),
        in_specs=[pl.BlockSpec(memory_space=pl.ANY)],
        out_specs=pl.BlockSpec(memory_space=pltpu.VMEM),
        scratch_shapes=[
            pltpu.VMEM((groups, chips) + parts.shape[2:], bf),
            pltpu.VMEM((groups, chips) + parts.shape[2:], bf),
            pltpu.VMEM((chips, groups) + first, bf),
            pltpu.VMEM((groups,) + second, bf),
            pltpu.VMEM((chips,) + first, bf),
            pltpu.VMEM((chips, groups) + second, bf),
            pltpu.SemaphoreType.DMA((chips * groups,)),
            pltpu.SemaphoreType.DMA((copies,)),
            pltpu.SemaphoreType.DMA((copies,)),
        ],
        compiler_params=pltpu.CompilerParams(
            collective_id=collective_id, has_side_effects=True, vmem_limit_bytes=40 << 20
        ),
        name=f"reduce_parts_{collective_id}",
    )(parts)


def to_rows(values, rows, width):
    high = lax.reduce_precision(values, 8, 7)
    rest = values - high
    mid = lax.reduce_precision(rest, 8, 7)
    flat = jnp.stack([high, mid, rest - mid]).reshape(-1).astype(jnp.bfloat16)
    return jnp.pad(flat, (0, rows * width - flat.shape[0])).reshape(rows, width)


def from_rows(block, count):
    flat = block.reshape(block.shape[:2] + (-1,))[:, :, : 3 * count].astype(jnp.float32)
    high, mid, low = (flat[:, :, i * count : (i + 1) * count] for i in range(3))
    return high + mid + low


def experts(order, ids, y, scale, w_gate, w_up, w_down):
    groups, blocks, _, rows, width = y.shape
    tokens = scale.shape[1]
    model = blocks * width
    per_owner = ids.shape[1]
    units = w_down.shape[1]
    half = per_owner * units
    ids_end = groups * per_owner

    def pick(s):
        return pl.BlockSpec((1, units, model), lambda k, n: (n[k * per_owner + s], 0, 0))

    bf = jnp.bfloat16
    parts = jax.ShapeDtypeStruct((groups, blocks, 2, tokens, width), bf)
    return pl.pallas_call(
        functools.partial(expert_kernel, per_owner),
        grid_spec=pltpu.PrefetchScalarGridSpec(
            num_scalar_prefetch=1,
            grid=(groups,),
            in_specs=[pick(s) for s in range(per_owner)] * 3
            + [
                pl.BlockSpec(
                    (1, blocks, 2, rows, width), lambda k, n: (n[ids_end + k], 0, 0, 0, 0)
                ),
                pl.BlockSpec(
                    (1, tokens, scale.shape[2]), lambda k, n: (n[ids_end + k], 0, 0)
                ),
            ],
            out_specs=[
                pl.BlockSpec((1,) + parts.shape[1:], lambda k, n: (n[ids_end + k], 0, 0, 0, 0)),
            ]
            + [pl.BlockSpec(memory_space=pl.ANY)] * 3,
            scratch_shapes=[
                pltpu.VMEM((tokens, model), bf),
                pltpu.VMEM((tokens, model), bf),
                pltpu.VMEM((2 * half, model), bf),
                pltpu.VMEM((half, model), bf),
                pltpu.VMEM((tokens, half), bf),
                pltpu.VMEM((tokens, 2 * half), bf),
                pltpu.VMEM((half, tokens), bf),
                pltpu.VMEM((2 * half, tokens), bf),
                pltpu.VMEM(w_down.shape, bf),
                pltpu.VMEM(w_down.shape, bf),
                pltpu.VMEM(w_down.shape, bf),
                pltpu.SemaphoreType.DMA((3,)),
            ],
        ),
        out_shape=[parts] + [jax.ShapeDtypeStruct(w_down.shape, bf)] * 3,
        compiler_params=pltpu.CompilerParams(vmem_limit_bytes=56 << 20),
        name="experts",
    )(
        jnp.concatenate([ids.reshape(-1), order]),
        *([w_gate] * per_owner + [w_up] * per_owner + [w_down] * per_owner),
        y,
        scale,
    )


def pair_groups(g, i):
    across, along = 1 - i // 2, 1 - lax.rem(i, 2)
    gx, gy = lax.rem(g, 2), g // 2
    return lax.rem(gy + along, 2) * 2 + lax.rem(gx + across, 2)


def near_rows(count):
    return count // 36 * 32


def direct_rows(count):
    return count * 5 // 192 * 32


def layer_kernel(
    groups, hidden,
    fetch_ref, q_ref, k_ref, v_ref, proj_ref, cot_ref, res_ref, gain_ref, seats_ref, shares_ref,
    gate_ref, up_ref, down_ref,
    layer_out, normed_out, w_gate, w_up, w_down, cot_all, x_all,
    q, k, v, proj, residual, mixed, f_own, f_stage, f_pair, f_ring, stream, y, slot_rows, slot_all,
    xs, cs, tails, w_in, w_out, act, grads, act_turned, grads_turned, slot_gate, slot_up, slot_down,
    own, stage, pair_in, diag_in, peer_in0, peer_in1, ring_in0, ring_in1,
    load_sems, slot_sems, cot_sems, f_pair_sems, f_ring_sems, y_sems, fetch_sems,
    pair_sems, ring1_sems, diag_sems, peer0_sems, peer1_sems, ring0_sems,
):
    g, h = lax.axis_index("group"), lax.axis_index("hidden")
    chips = hidden // 2
    owned, units, model = w_gate.shape
    tokens, width = layer_out.shape
    per_owner = fetch_ref.shape[1] // groups
    half = per_owner * units
    last, final = chips - 1, groups - 1
    turns = list(range(1, chips)) + [0]
    ahead = {"group": g, "hidden": lax.rem(h + 2, hidden)}
    behind = {"group": g, "hidden": lax.rem(h + hidden - 2, hidden)}
    partner_h = h + 1 - 2 * lax.rem(h, 2)
    partner = {"group": g, "hidden": partner_h}
    mesh_id = pl.DeviceIdType.MESH
    source = [pair_groups(g, i) for i in range(groups)]
    peers = [{"group": source[i], "hidden": h} for i in range(final)]
    turned = ((1,), (1,))

    barrier = pltpu.get_barrier_semaphore()
    greeted = [ahead, behind, partner] + peers
    for device in greeted:
        pl.semaphore_signal(barrier, inc=1, device_id=device, device_id_type=mesh_id)

    my_cols = pl.ds(pl.multiple_of(h * width, width), width)
    moves = (
        (q_ref, q), (k_ref, k), (v_ref, v), (proj_ref, proj), (res_ref.at[:, my_cols], residual),
        (gate_ref, w_gate), (up_ref, w_up), (down_ref, w_down),
    )
    loads = [pltpu.make_async_copy(a, b, load_sems.at[n]) for n, (a, b) in enumerate(moves)]
    for copy in loads:
        copy.start()

    slot_rows[...] = jnp.zeros_like(slot_rows)
    for f in range(groups * per_owner):
        named = jnp.where(seats_ref[...] == f, shares_ref[...], 0.0)
        slot_rows[f // per_owner, f % per_owner : f % per_owner + 1, :] = jnp.sum(
            named, axis=0, keepdims=True
        )
    for buffer in (slot_gate, slot_up, slot_down):
        buffer[per_owner] = jnp.zeros(buffer.shape[1:], buffer.dtype)
    slot_all[g] = slot_rows[g]

    def remote(source_ref, target, sems, index, device):
        return pltpu.make_async_remote_copy(
            src_ref=source_ref,
            dst_ref=target,
            send_sem=sems.at[(0,) + index],
            recv_sem=sems.at[(1,) + index],
            device_id=device,
            device_id_type=mesh_id,
        )

    def add(into, *others):
        total = into[...].astype(jnp.float32)
        for other in others:
            total = total + other[...].astype(jnp.float32)
        into[...] = total.astype(into.dtype)

    pl.semaphore_wait(barrier, len(greeted))

    quarter = tokens // 4
    base = lax.rem(h, 2) * (2 * quarter)
    cot_made = {}

    def piece(n):
        return pl.ds(pl.multiple_of(base + n * quarter, quarter), quarter)

    def landed(i, n):
        return cot_all.at[source[i], piece(n)]

    def send_cot(key, source_ref, target, device):
        copy = remote(source_ref, target, cot_sems, (len(cot_made),), device)
        copy.start()
        cot_made[key] = copy

    for i, n in ((1, 0), (2, 1), (1, 1), (2, 0)):
        send_cot(("near", i, n), cot_ref.at[piece(n)], cot_all.at[g, piece(n)], peers[i])
    slots = [
        remote(slot_rows.at[source[i]], slot_all.at[g], slot_sems, (i,), peers[i])
        for i in range(final)
    ]
    for copy in slots:
        copy.start()

    def pass_cot(i, n, forward):
        cot_made["far" if i == 0 else "near", i, n].wait_recv()
        if forward:
            send_cot(("far", 0, n), landed(i, n), landed(i, n), peers[3 - i])
        send_cot(("pair", i, n), landed(i, n), landed(i, n), partner)

    for copy in loads[:3]:
        copy.wait()
    heads_here = q.shape[1] // HEAD_DIM
    kv = h * heads_here // (HEADS // KV_HEADS)
    kv_cols = pl.ds(pl.multiple_of(kv * HEAD_DIM, HEAD_DIM), HEAD_DIM)
    keys, values = k[:, kv_cols], v[:, kv_cols]
    seen = lax.broadcasted_iota(jnp.int32, (tokens, tokens), 0) >= lax.broadcasted_iota(
        jnp.int32, (tokens, tokens), 1
    )
    for head in range(heads_here):
        cols = slice(head * HEAD_DIM, (head + 1) * HEAD_DIM)
        scores = dot(q[:, cols], keys, turned) / math.sqrt(HEAD_DIM)
        scores = jnp.where(seen, scores, -1e30)
        weights = jnp.exp(scores - jnp.max(scores, axis=-1, keepdims=True))
        total = jnp.sum(weights, axis=-1, keepdims=True)
        mixed[:, cols] = dot((weights / total).astype(mixed.dtype), values).astype(mixed.dtype)

    def f_pair_copy(t):
        return remote(f_stage.at[t], f_pair.at[t], f_pair_sems, (t,), partner)

    middle_row = tokens // 32 * 16
    halves = (pl.ds(0, middle_row), pl.ds(middle_row, tokens - middle_row))

    def f_ring_copy(t, part):
        span = halves[part]
        return remote(f_own.at[t, span], f_ring.at[t, span], f_ring_sems, (t, part), ahead)

    def reduce_task(t, part):
        span = halves[part]
        if part == 0:
            f_pair_copy(t).wait_recv()
        if t == 1:
            add(f_own.at[t, span], f_pair.at[t, span])
        else:
            before = t - 1 if t else last
            f_ring_copy(before, part).wait_recv()
            add(f_own.at[t, span], f_pair.at[t, span], f_ring.at[before, span])
        if t:
            f_ring_copy(t, part).start()

    for copy in loads[3:5]:
        copy.wait()

    @pl.loop(0, chips)
    def _(j):
        t = lax.rem(j + 1, chips)
        for whose, target in ((partner_h, f_stage), (h, f_own)):
            first = pl.multiple_of(lax.rem(whose + hidden - 2 * t, hidden) * width, width)
            target[t] = dot(mixed[...], proj[:, pl.ds(first, width)]).astype(target.dtype)
            if whose is partner_h:
                f_pair_copy(t).start()

        @pl.when(j == 1)
        def _():
            reduce_task(1, 0)
            reduce_task(1, 1)

    pass_cot(1, 0, True)
    pass_cot(2, 1, True)
    for t in turns[1:]:
        for part in range(2):
            reduce_task(t, part)

    stream[...] = residual[...].astype(jnp.float32) + f_own[0].astype(jnp.float32)
    y[:tokens, :] = (stream[...] * gain_ref[:, my_cols]).astype(y.dtype)
    squares = jnp.sum(stream[...] * stream[...], axis=-1, keepdims=True)
    squares = jnp.broadcast_to(squares, (tokens, 128)).T[:16]
    high = squares.astype(y.dtype).astype(jnp.float32)
    middle = (squares - high).astype(y.dtype).astype(jnp.float32)
    low = squares - high - middle
    row = lax.broadcasted_iota(jnp.int32, (16, width), 0)
    extras = jnp.zeros((16, width), jnp.float32)
    for c in range(-(-tokens // width)):
        count = min(width, tokens - c * width)
        for n, term in enumerate((high, middle, low)):
            term = term[:, c * width : c * width + count]
            if count < width:
                term = jnp.concatenate([term, jnp.zeros((16, width - count), jnp.float32)], axis=1)
            extras = jnp.where(row == 3 * c + n, term, extras)
    y[tokens:, :] = extras.astype(y.dtype)

    rows_all = y.shape[0]
    near = near_rows(rows_all)
    spans = {0: pl.ds(0, near), 1: pl.ds(near, rows_all - near)}
    spans["a"], spans["b"] = pl.ds(0, near // 2), pl.ds(near // 2, near // 2)
    behind_h = [lax.rem(h + hidden - 2 * t, hidden) for t in range(chips)]
    y_made = {}

    def y_copy(number, mine, i, t, span, device):
        target = x_all.at[source[i], behind_h[t], spans[span]]
        return remote(y.at[spans[span]] if mine else target, target, y_sems, (number,), device)

    def send_y(key, *what):
        y_made[key] = (len(y_made),) + what
        y_copy(*y_made[key]).start()

    def y_arrived(*key):
        y_copy(*y_made[key]).wait_recv()

    home = groups - 1

    def ring_y0(t):
        y_arrived("ring0", t)
        if t + 1 < chips:
            send_y(("ring0", t + 1), False, home, t, 0, ahead)
        for i in (1, 2):
            send_y(("near0", t, i), False, home, t, 0, peers[i])
        send_y(("pair", home, t, 0), False, home, t, 0, partner)

    def ring_y1(t, i):
        y_arrived("ring1", t, i)
        if t + 1 < chips:
            send_y(("ring1", t + 1, i), False, i, t, 1, ahead)
        send_y(("pair", i, t, 1), False, i, t, 1, partner)

    def near_y0(t):
        for i, span in ((1, "a"), (2, "b")):
            y_arrived("near0", t, i)
            send_y(("far0", t, span), False, i, t, span, peers[3 - i])
            send_y(("pair", i, t, 0), False, i, t, 0, partner)

    def far_y0(t):
        for span in ("a", "b"):
            y_arrived("far0", t, span)
            send_y(("pair", 0, t, span), False, 0, t, span, partner)

    local = pltpu.make_async_copy(y, x_all.at[g, h], load_sems.at[len(moves)])
    local.start()
    send_y(("ring0", 1), True, home, 0, 0, ahead)
    for i in (1, 2):
        send_y(("near0", 0, i), True, home, 0, 0, peers[i])
    for i in (1, 2, 0):
        send_y(("near1", i), True, home, 0, 1, peers[i])
    send_y(("ring1", 1, home), True, home, 0, 1, ahead)
    for span in (0, 1):
        send_y(("pair", home, 0, span), True, home, 0, span, partner)
    pass_cot(1, 1, False)
    pass_cot(2, 0, False)
    ring_y0(1)
    near_y0(0)
    for i in (1, 2, 0):
        y_arrived("near1", i)
        send_y(("ring1", 1, i), False, i, 0, 1, ahead)
        send_y(("pair", i, 0, 1), False, i, 0, 1, partner)
    ring_y1(1, home)
    pass_cot(0, 0, False)
    pass_cot(0, 1, False)
    for t in range(2, chips):
        ring_y0(t)
        near_y0(t - 1)
        for i in range(final):
            ring_y1(t - 1, i)
        ring_y1(t, home)
        if t > 2:
            far_y0(t - 3)
    for t in turns:
        if t:
            f_pair_copy(t).wait_send()
            for part in range(2):
                f_ring_copy(t, part).wait_send()
    f_pair_copy(0).wait_send()
    for copy in loads[5:]:
        copy.wait()
    local.wait()
    for copy in slots:
        copy.wait_recv()
    for t in range(chips):
        for span in (0, 1):
            y_arrived("pair", home, t, span)

    def gather_task(n):
        if n == 0:
            near_y0(last)
        elif n == 1:
            for i in range(final):
                ring_y1(last, i)
        elif n == 2:
            far_y0(last - 2)
            far_y0(last - 1)
        else:
            far_y0(last)
            for key in y_made:
                if key[0] == "pair" and key[1] != home:
                    y_arrived(*key)
            for key, copy in cot_made.items():
                if key[0] == "pair":
                    copy.wait_recv()

    cut = direct_rows(tokens)
    rows = (pl.ds(0, cut), pl.ds(cut, tokens - cut))
    via = (pl.ds(0, cut // 2), pl.ds(cut // 2, cut // 2))

    def peer(i):
        return {"group": pair_groups(g, i), "hidden": h}

    def fetch_x(i):
        slot = lax.rem(i, 2)
        group = pair_groups(g, i)
        copies = []
        for b in range(hidden):
            cols = pl.ds(b * width, width)
            copies.append(
                pltpu.make_async_copy(
                    x_all.at[group, b, pl.ds(0, tokens)], xs.at[slot, :, cols], fetch_sems.at[slot, b]
                )
            )
            copies.append(
                pltpu.make_async_copy(
                    x_all.at[group, b, pl.ds(tokens, 16)],
                    tails.at[slot, :, cols],
                    fetch_sems.at[slot, hidden + b],
                )
            )
        return copies

    def fetch_c(i, mine):
        slot = lax.rem(i, 2)
        origin = cot_ref if mine else cot_all.at[pair_groups(g, i)]
        return pltpu.make_async_copy(origin, cs.at[slot], fetch_sems.at[slot, 2 * hidden])

    def start_fetch(i):
        for copy in fetch_x(i):
            copy.start()

        @pl.when(i < final)
        def _():
            fetch_c(i, False).start()

        @pl.when(i == final)
        def _():
            fetch_c(i, True).start()

    def wait_fetch(i):
        for copy in fetch_x(i):
            copy.wait()
        fetch_c(i, False).wait()

    def part_of(i, t, part):
        return own.at[i, t, :, rows[part]]

    def pair_copy(i, t):
        return remote(stage.at[lax.rem(i, 2), t], pair_in.at[i, t], pair_sems, (i, t), partner)

    def ring1_copy(i, t):
        return remote(part_of(i, t, 1), ring_in1.at[i, t], ring1_sems, (i, t), ahead)

    def diag_copy(n, t):
        return remote(own.at[0, t, :, via[n]], diag_in.at[n, t], diag_sems, (n, t), peer(n + 1))

    def peer0_copy(i, t):
        return remote(part_of(i, t, 0), peer_in0.at[i - 1, t], peer0_sems, (i - 1, t), peer(i))

    def peer1_copy(i):
        return remote(part_of(i, 0, 1), peer_in1.at[i], peer1_sems, (i,), peer(i))

    def ring0_copy(t):
        return remote(part_of(final, t, 0), ring_in0.at[t], ring0_sems, (t,), ahead)

    def pair_task(i, t):
        pair_copy(i, t).wait_recv()
        add(own.at[i, t], pair_in.at[i, t])
        if t == 1:
            ring1_copy(i, t).start()

        @pl.when(i == 0)
        def _():
            for n in range(2):
                diag_copy(n, t).start()

        for n, step in ((1, 1), (0, 2)):

            @pl.when(i == step)
            def _():
                diag_copy(n, t).wait_recv()
                add(own.at[step, t, :, via[n]], diag_in.at[n, t])
                peer0_copy(step, t).start()

    def ring_task(i, t):
        before = t - 1 if t else last
        ring1_copy(i, before).wait_recv()
        add(part_of(i, t, 1), ring_in1.at[i, before])
        if t:
            ring1_copy(i, t).start()

    def finish_task(t):
        arrived = []
        for i in range(1, final):
            peer0_copy(i, t).wait_recv()
            arrived.append(peer_in0.at[i - 1, t])
        if t != 1:
            before = t - 1 if t else last
            ring0_copy(before).wait_recv()
            arrived.append(ring_in0.at[before])
        add(part_of(final, t, 0), *arrived)
        if t:
            ring0_copy(t).start()

    def finish_ring(i):
        ring_task(i, 0)

        @pl.when(i < final)
        def _():
            peer1_copy(i).start()

    def scale_of(slot, group):
        terms = jnp.zeros((16, width), jnp.float32)
        for b in range(hidden):
            terms = terms + tails[slot, :, b * width : (b + 1) * width].astype(jnp.float32)
        chunks = []
        for c in range(-(-tokens // width)):
            count = min(width, tokens - c * width)
            total = terms[3 * c : 3 * c + 1] + terms[3 * c + 1 : 3 * c + 2] + terms[3 * c + 2 : 3 * c + 3]
            chunks.append(total[:, :count])
        inverse = lax.rsqrt(jnp.concatenate(chunks, axis=1) / model + epsilon)
        row = lax.broadcasted_iota(jnp.int32, (8, tokens), 0)
        both = jnp.where(row == per_owner, inverse, slot_all[group])
        return jnp.concatenate([both, jnp.zeros((120, tokens), jnp.float32)], axis=0).T

    start_fetch(home)

    @pl.loop(0, groups)
    def _(step):
        i, one, two = (lax.rem(step + groups - 1 - d, groups) for d in range(3))
        slot = lax.rem(i, 2)
        group = pair_groups(g, i)

        @pl.when(step > 0)
        def _():
            pair_task(one, 1)

        @pl.when((step > 0) & (step < final))
        def _():
            start_fetch(i + 1)

        for s in range(per_owner):
            e = lax.rem(fetch_ref[group, g * per_owner + s], owned)
            w_in[s * units : (s + 1) * units, :] = w_gate[e]
            w_in[half + s * units : half + (s + 1) * units, :] = w_up[e]
            w_out[s * units : (s + 1) * units, :] = w_down[e]
        wait_fetch(i)
        scale = scale_of(slot, group)
        inverse = scale[:, per_owner : per_owner + 1]
        lane = lax.broadcasted_iota(jnp.int32, (tokens, half), 1)
        weight = jnp.broadcast_to(scale[:, :1], (tokens, half))
        for s in range(1, per_owner):
            weight = jnp.where(lane >= s * units, scale[:, s : s + 1], weight)
        pre_gate = dot(xs[slot], w_in[:half, :], turned) * inverse

        @pl.when(step == 0)
        def _():
            gather_task(0)

        @pl.when(step > 0)
        def _():
            pair_task(one, 2)

        pre_up = dot(xs[slot], w_in[half:, :], turned) * inverse

        @pl.when(step == 0)
        def _():
            gather_task(1)

        @pl.when(step > 0)
        def _():
            pair_task(one, 3)

        @pl.when(step > 1)
        def _():
            ring_task(two, 3)

        d_act = dot(cs[slot], w_out[...], turned) * weight

        @pl.when(step == 0)
        def _():
            gather_task(2)

        @pl.when(step > 0)
        def _():
            pair_task(one, 0)

        sig = jax.nn.sigmoid(pre_gate)
        swish = pre_gate * sig
        weighted = swish * pre_up * weight
        d_gate = d_act * pre_up * sig * (1.0 + pre_gate * (1.0 - sig))
        d_up = d_act * swish
        act[...] = weighted.astype(act.dtype)
        grads[:, :half] = d_gate.astype(grads.dtype)
        grads[:, half:] = d_up.astype(grads.dtype)
        act_turned[i] = act[...].T
        grads_turned[i, :half, :] = (d_gate * inverse).astype(grads.dtype).T
        grads_turned[i, half:, :] = (d_up * inverse).astype(grads.dtype).T

        @pl.loop(0, chips)
        def _(j):
            t = lax.rem(j + 1, chips)

            @pl.when(step > 1)
            def _():
                pair_copy(two, t).wait_send()

            for whose, target, at in ((partner_h, stage, slot), (h, own, i)):
                first = pl.multiple_of(lax.rem(whose + hidden - 2 * t, hidden) * width, width)
                cols = pl.ds(first, width)
                target[at, t, 0] = dot(act[...], w_out[:, cols]).astype(target.dtype)
                target[at, t, 1] = dot(grads[...], w_in[:, cols]).astype(target.dtype)
                if whose is partner_h:
                    pair_copy(i, t).start()

        @pl.when(step > 0)
        def _():
            ring_task(one, 2)

        @pl.when(step > 1)
        def _():
            finish_ring(two)

        @pl.when(step == 0)
        def _():
            gather_task(3)
            start_fetch(0)

    for buffer in (w_gate, w_up, w_down):
        buffer[...] = jnp.zeros_like(buffer)

    tasks = (
        (0, lambda: pair_task(final - 1, 1)),
        (1, lambda: pair_task(final - 1, 2)),
        (2, lambda: pair_task(final - 1, 3)),
        (3, lambda: pair_task(final - 1, 0)),
        (5, lambda: ring_task(final - 2, 3)),
        (8, lambda: ring_task(final - 1, 2)),
        (9, lambda: finish_task(1)),
        (11, lambda: finish_ring(final - 2)),
        (14, lambda: ring_task(final - 1, 3)),
        (18, lambda: finish_task(2)),
        (22, lambda: finish_ring(final - 1)),
        (27, lambda: finish_task(3)),
    )

    @pl.loop(0, groups * hidden)
    def _(n):
        turn, b = n // hidden, lax.rem(n, hidden)
        i = lax.rem(2 * groups - 2 - turn, groups)
        slot = lax.rem(i, 2)
        group = pair_groups(g, i)

        @pl.when((b == 0) & (turn > 0) & (turn < final))
        def _():
            start_fetch(lax.rem(i + groups - 1, groups))

        @pl.when((b == 0) & (turn > 1))
        def _():
            wait_fetch(i)

        cols = pl.ds(pl.multiple_of(b * width, width), width)
        down = dot(act_turned[i], cs[slot, :, cols])
        both = dot(grads_turned[i], xs[slot, :, cols])
        for s in range(per_owner):
            slot_down[s] = down[s * units : (s + 1) * units]
            slot_gate[s] = both[s * units : (s + 1) * units]
            slot_up[s] = both[half + s * units : half + (s + 1) * units]
        listed = [lax.rem(fetch_ref[group, g * per_owner + s], owned) for s in range(per_owner)]
        for e in range(owned):
            seat = jnp.int32(per_owner)
            for s in range(per_owner):
                seat = jnp.where(listed[s] == e, s, seat)
            for total, value in ((w_down, slot_down), (w_gate, slot_gate), (w_up, slot_up)):
                total[e, :, cols] = (total[e, :, cols].astype(jnp.float32) + value[seat]).astype(
                    total.dtype
                )
        for at, task in tasks:
            pl.when(n == at)(task)

    finish_task(0)
    for i in range(final):
        peer1_copy(i).wait_recv()
    add(part_of(final, 0, 1), *[peer_in1.at[i] for i in range(final)])
    layer_out[...] = (stream[...] + own[final, 0, 0].astype(jnp.float32)).astype(layer_out.dtype)
    normed_out[...] = own[final, 0, 1]
    for t in range(chips):
        for i in range(groups):
            if final - 2 <= i < final:
                pair_copy(i, t).wait_send()
            if t:
                ring1_copy(i, t).wait_send()
            if 0 < i < final:
                peer0_copy(i, t).wait_send()
        for n in range(2):
            diag_copy(n, t).wait_send()
        if t:
            ring0_copy(t).wait_send()
    for i in range(final):
        peer1_copy(i).wait_send()
    for key in y_made:
        y_copy(*y_made[key]).wait_send()
    for copy in cot_made.values():
        copy.wait_send()
    for copy in slots:
        copy.wait_send()


def store_kernel(count, *refs):
    sources, targets, sems = refs[:count], refs[count:-1], refs[-1]
    copies = [
        pltpu.make_async_copy(a, b, sems.at[n]) for n, (a, b) in enumerate(zip(sources, targets))
    ]
    for copy in copies:
        copy.start()
    for copy in copies:
        copy.wait()


def store(*values):
    count = len(values)
    return pl.pallas_call(
        functools.partial(store_kernel, count),
        in_specs=[pl.BlockSpec(memory_space=pltpu.VMEM)] * count,
        out_specs=[pl.BlockSpec(memory_space=pl.ANY)] * count,
        out_shape=[jax.ShapeDtypeStruct(value.shape, value.dtype) for value in values],
        scratch_shapes=[pltpu.SemaphoreType.DMA((count,))],
        compiler_params=pltpu.CompilerParams(vmem_limit_bytes=STORE_LIMIT),
        name="store",
    )(*values)


def layer(
    fetch_list, queries, key_rows, value_rows, out_proj, cotangent, residual, gain, seats, shares,
    w_gate, w_up, w_down, groups, hidden,
):
    tokens, model = cotangent.shape
    width = model // hidden
    chips = hidden // 2
    owned, units, _ = w_down.shape
    per_owner = fetch_list.shape[1] // groups
    half = per_owner * units
    bf = queries.dtype
    cut = direct_rows(tokens)
    block = (2, tokens, width)
    vmem = pl.BlockSpec(memory_space=pltpu.VMEM)
    anywhere = pl.BlockSpec(memory_space=pl.ANY)
    dma = pltpu.SemaphoreType.DMA
    f32 = jnp.float32
    shape = jax.ShapeDtypeStruct
    scratch = [
        (queries.shape, bf), (key_rows.shape, bf), (value_rows.shape, bf), (out_proj.shape, bf),
        ((tokens, width), bf), (queries.shape, bf)
    ]
    scratch += [((chips, tokens, width), bf)] * 4
    scratch += [
        ((tokens, width), f32), ((tokens + 16, width), bf),
        ((groups, 8, tokens), f32), ((groups, 8, tokens), f32),
        ((2, tokens, model), bf), ((2, tokens, model), bf), ((2, 16, model), bf),
        ((2 * half, model), bf), ((half, model), bf), ((tokens, half), bf), ((tokens, 2 * half), bf),
        ((groups, half, tokens), bf), ((groups, 2 * half, tokens), bf),
    ]
    scratch += [((per_owner + 1, units, width), f32)] * 3
    scratch += [
        ((groups, chips) + block, bf), ((2, chips) + block, bf), ((groups, chips) + block, bf),
        ((2, chips, 2, cut // 2, width), bf),
        ((groups - 2, chips, 2, cut, width), bf), ((groups - 1, 2, tokens - cut, width), bf),
        ((chips, 2, cut, width), bf), ((groups, chips, 2, tokens - cut, width), bf),
    ]
    sems = [
        (9,), (2, groups - 1), (2, 12), (2, chips), (2, chips, 2), (2, 72), (2, 2 * hidden + 1),
        (2, groups, chips), (2, groups, chips), (2, 2, chips), (2, groups - 2, chips),
        (2, groups - 1), (2, chips),
    ]
    return pl.pallas_call(
        functools.partial(layer_kernel, groups, hidden),
        in_specs=[pl.BlockSpec(memory_space=pltpu.SMEM)]
        + [anywhere] * 6 + [vmem] * 3 + [anywhere] * 3,
        out_specs=[vmem] * 5 + [anywhere] * 2,
        out_shape=[pltpu.VMEM((tokens, width), bf)] * 2
        + [pltpu.VMEM(w_down.shape, bf)] * 3
        + [
            shape((groups, tokens, model), bf),
            shape((groups, hidden, tokens + 16, width), bf),
        ],
        scratch_shapes=[pltpu.VMEM(*s) for s in scratch] + [dma(s) for s in sems],
        compiler_params=pltpu.CompilerParams(
            collective_id=1, has_side_effects=True, vmem_limit_bytes=51 << 20
        ),
        name="layer",
    )(
        fetch_list, queries, key_rows, value_rows, out_proj, cotangent, residual, gain, seats,
        shares, w_gate, w_up, w_down,
    )


def shards(
    queries,
    key_rows,
    value_rows,
    out_proj,
    residual,
    norm_gain,
    w_gate,
    w_up,
    w_down,
    route_slot,
    route_weight,
    fetch_list,
    cotangent,
):
    tokens_here, model = cotangent.shape
    hidden_index = lax.axis_index("hidden")
    hidden_count = lax.axis_size("hidden")
    group_index = lax.axis_index("group")
    group_count = lax.axis_size("group")
    per_owner = FETCH // group_count

    if group_count == 4:
        outs = layer(
            fetch_list, queries, key_rows, value_rows, out_proj, cotangent, residual,
            norm_gain[None], route_slot.T, route_weight.T,
            jnp.swapaxes(w_gate, 1, 2), jnp.swapaxes(w_up, 1, 2), w_down,
            group_count, hidden_count,
        )
        outs = store(*outs[:5])
        return (
            outs[0], outs[1], jnp.swapaxes(outs[2], 1, 2), jnp.swapaxes(outs[3], 1, 2), outs[4]
        )

    chosen = route_slot[:, :, None] == jnp.arange(FETCH, dtype=jnp.int32)[None, None, :]
    slot_weight = jnp.sum(jnp.where(chosen, route_weight[:, :, None], 0.0), axis=1)
    order = (group_index + jnp.arange(group_count, dtype=jnp.int32)) % group_count
    own_cols = lax.dynamic_slice_in_dim(fetch_list, group_index * per_owner, per_owner, 1)
    ids = jnp.take(own_cols - group_index * EXP_GROUP, order, axis=0)

    heads_here = queries.shape[1] // HEAD_DIM
    kv_index = hidden_index * heads_here // (HEADS // KV_HEADS)
    key_block = lax.dynamic_slice_in_dim(key_rows, kv_index * HEAD_DIM, HEAD_DIM, 1)
    value_block = lax.dynamic_slice_in_dim(value_rows, kv_index * HEAD_DIM, HEAD_DIM, 1)
    mixed = attention_rows(queries, key_block, value_block, heads_here)
    partial_value = jnp.dot(mixed, out_proj, preferred_element_type=jnp.float32)
    share_width = model // hidden_count
    first_col = hidden_index * share_width
    blocks = partial_value.astype(jnp.bfloat16).reshape(tokens_here, hidden_count, share_width)
    attn_share = reduce_parts(jnp.swapaxes(blocks, 0, 1)[None, :, None], 2)[0]
    stream = lax.dynamic_slice_in_dim(residual, first_col, share_width, 1).astype(
        jnp.float32
    ) + attn_share.astype(jnp.float32)
    gain = lax.dynamic_slice_in_dim(norm_gain, first_col, share_width, 0)
    squares = jnp.sum(stream * stream, axis=-1)
    gained = (stream * gain).astype(jnp.bfloat16)
    slots_here = FETCH // hidden_count
    slots = lax.dynamic_slice_in_dim(slot_weight.T, hidden_index * slots_here, slots_here, 0)
    extra = -(-3 * slots_here * tokens_here // (16 * share_width)) * 16
    cot_share = lax.dynamic_slice_in_dim(cotangent, first_col, share_width, 1)
    y = jnp.stack(
        [
            jnp.concatenate([gained, to_rows(squares, extra, share_width)]),
            jnp.concatenate([cot_share, to_rows(slots, extra, share_width)]),
        ]
    )
    y_all = gather_all(y, group_count, hidden_count)
    squares_all = from_rows(y_all[:, :, 0, tokens_here:], tokens_here).sum(axis=1)
    inverse = lax.rsqrt(squares_all / model + epsilon)
    weights = from_rows(y_all[:, :, 1, tokens_here:], slots_here * tokens_here)
    weights = weights.reshape(group_count, FETCH, tokens_here)
    weights = lax.dynamic_slice_in_dim(weights, group_index * per_owner, per_owner, 1)
    scale = jnp.concatenate([weights, inverse[:, None, :]], axis=1)
    scale = jnp.pad(scale, ((0, 0), (0, 8 - scale.shape[1]), (0, 0)))
    scale = jnp.swapaxes(scale, 1, 2)
    parts, grad_gate, grad_up, grad_down = experts(
        order,
        ids,
        y_all,
        scale,
        jnp.swapaxes(w_gate, 1, 2),
        jnp.swapaxes(w_up, 1, 2),
        w_down,
    )
    grad_gate = jnp.swapaxes(grad_gate, 1, 2)
    grad_up = jnp.swapaxes(grad_up, 1, 2)
    sums = reduce_parts(parts, 1)
    layer_out = (stream + sums[0].astype(jnp.float32)).astype(jnp.bfloat16)
    return (layer_out, sums[1], grad_gate, grad_up, grad_down)


def solution(mesh):
    return jax.shard_map(
        shards,
        mesh=mesh,
        in_specs=(
            P("group", "hidden"),
            P("group", None),
            P("group", None),
            P("hidden", None),
            P("group", None),
            P(),
            P("group", None, "hidden"),
            P("group", None, "hidden"),
            P("group", "hidden", None),
            P("group", None),
            P("group", None),
            P(),
            P("group", None),
        ),
        out_specs=(
            P("group", "hidden"),
            P("group", "hidden"),
            P("group", None, "hidden"),
            P("group", None, "hidden"),
            P("group", "hidden", None),
        ),
        check_vma=False,
    )
```

```python
import functools
import math

import jax
import jax.numpy as jnp
from jax import lax
from jax.experimental import pallas as pl
from jax.experimental.pallas import tpu as pltpu
from jax.sharding import PartitionSpec as P

HEADS = 32
KV_HEADS = 4
HEAD_DIM = 128
EXP_GROUP = 8
FETCH = 16

epsilon = 1e-06
STORE_LIMIT = 4 << 20


def attention_rows(query_in, key_block, value_block, heads_here):
    tokens_here = query_in.shape[0]
    query_heads = query_in.reshape(tokens_here, heads_here, HEAD_DIM)
    pos = jnp.arange(tokens_here, dtype=jnp.int32)
    scores = jnp.einsum(
        "thd,sd->hts", query_heads, key_block, preferred_element_type=jnp.float32
    ) / math.sqrt(HEAD_DIM)
    scores = jnp.where(pos[:, None] >= pos[None, :], scores, -1e30)
    row_peak = jnp.max(scores, axis=-1, keepdims=True)
    weights = jnp.exp(scores - row_peak)
    probabilities = (weights / jnp.sum(weights, axis=-1, keepdims=True)).astype(jnp.bfloat16)
    mixed = jnp.einsum("hts,sd->thd", probabilities, value_block, preferred_element_type=jnp.float32)
    return mixed.astype(jnp.bfloat16).reshape(tokens_here, heads_here * HEAD_DIM)


def dot(a, b, dims=((1,), (0,))):
    return lax.dot_general(a, b, (dims, ((), ())), preferred_element_type=jnp.float32)


def expert_kernel(per_owner, ids_ref, *refs):
    gates, refs = refs[:per_owner], refs[per_owner:]
    ups, refs = refs[:per_owner], refs[per_owner:]
    downs, refs = refs[:per_owner], refs[per_owner:]
    (
        y_ref, scale_ref,
        part_ref, gate_out, up_out, down_out,
        x2d, c2d, w_in, w_out, act, grads, act_turned, grads_turned, acc_gate, acc_up, acc_down, sems,
    ) = refs
    step = pl.program_id(0)
    blocks, width = y_ref.shape[1], y_ref.shape[4]
    tokens = x2d.shape[0]
    units = gates[0].shape[1]
    half = per_owner * units

    @pl.when(step == 0)
    def _():
        acc_gate[...] = jnp.zeros_like(acc_gate)
        acc_up[...] = jnp.zeros_like(acc_up)
        acc_down[...] = jnp.zeros_like(acc_down)

    for s in range(per_owner):
        w_in[s * units : (s + 1) * units, :] = gates[s][0]
        w_in[half + s * units : half + (s + 1) * units, :] = ups[s][0]
        w_out[s * units : (s + 1) * units, :] = downs[s][0]
    for h in range(blocks):
        x2d[:, h * width : (h + 1) * width] = y_ref[0, h, 0, :tokens]
        c2d[:, h * width : (h + 1) * width] = y_ref[0, h, 1, :tokens]

    scale = scale_ref[0]
    inverse = scale[:, per_owner : per_owner + 1]
    lane = lax.broadcasted_iota(jnp.int32, (tokens, half), 1)
    weight = jnp.broadcast_to(scale[:, :1], (tokens, half))
    for s in range(1, per_owner):
        weight = jnp.where(lane >= s * units, scale[:, s : s + 1], weight)
    turned = ((1,), (1,))
    pre_gate = dot(x2d[...], w_in[:half, :], turned) * inverse
    pre_up = dot(x2d[...], w_in[half:, :], turned) * inverse
    d_act = dot(c2d[...], w_out[...], turned) * weight
    sig = jax.nn.sigmoid(pre_gate)
    swish = pre_gate * sig
    weighted = swish * pre_up * weight
    d_gate = d_act * pre_up * sig * (1.0 + pre_gate * (1.0 - sig))
    d_up = d_act * swish
    act[...] = weighted.astype(act.dtype)
    grads[:, :half] = d_gate.astype(grads.dtype)
    grads[:, half:] = d_up.astype(grads.dtype)
    act_turned[...] = act[...].T
    grads_turned[:half, :] = (d_gate * inverse).astype(grads.dtype).T
    grads_turned[half:, :] = (d_up * inverse).astype(grads.dtype).T

    step_ids = [ids_ref[step * per_owner + s] for s in range(per_owner)]

    def add(acc, e, cols, value):
        acc[e, :, cols] = (acc[e, :, cols].astype(jnp.float32) + value).astype(acc.dtype)

    @pl.loop(0, blocks)
    def _(h):
        cols = pl.ds(pl.multiple_of(h * width, width), width)
        part_ref[0, h, 0] = dot(act[...], w_out[:, cols]).astype(part_ref.dtype)
        part_ref[0, h, 1] = dot(grads[...], w_in[:, cols]).astype(part_ref.dtype)
        down = dot(act_turned[...], c2d[:, cols])
        both = dot(grads_turned[...], x2d[:, cols])
        for s in range(per_owner):
            rows = slice(s * units, (s + 1) * units)
            add(acc_down, step_ids[s], cols, down[rows])
            add(acc_gate, step_ids[s], cols, both[rows])
            add(acc_up, step_ids[s], cols, both[half:][rows])

    @pl.when(step == pl.num_programs(0) - 1)
    def _():
        copies = [
            pltpu.make_async_copy(a, b, sems.at[i])
            for i, (a, b) in enumerate(
                ((acc_gate, gate_out), (acc_up, up_out), (acc_down, down_out))
            )
        ]
        for copy in copies:
            copy.start()
        for copy in copies:
            copy.wait()


def first_rows(count):
    return count // 24 * 16


def gather_kernel(groups, hidden, y_ref, out_ref, local_sem, send_sems, recv_sems):
    g, h = lax.axis_index("group"), lax.axis_index("hidden")
    chips = hidden // 2
    rows_all = y_ref.shape[1]
    cut = first_rows(rows_all)
    rows = (pl.ds(0, cut), pl.ds(cut, rows_all - cut))
    ahead = {"group": g, "hidden": lax.rem(h + 2, hidden)}
    behind = {"group": g, "hidden": lax.rem(h + hidden - 2, hidden)}
    partner = {"group": g, "hidden": h + 1 - 2 * lax.rem(h, 2)}
    peers = [{"group": lax.rem(g + k, groups), "hidden": h} for k in range(groups)]
    mesh_id = pl.DeviceIdType.MESH

    barrier = pltpu.get_barrier_semaphore()
    greeted = [ahead, behind, partner] + peers[1:]
    for device in greeted:
        pl.semaphore_signal(barrier, inc=1, device_id=device, device_id_type=mesh_id)
    pl.semaphore_wait(barrier, len(greeted))

    made = {}

    def send(key, source, g_from, h_from, part, device):
        number = len(made)
        target = out_ref.at[g_from, h_from, :, rows[part]]
        copy = pltpu.make_async_remote_copy(
            src_ref=target if source is None else source,
            dst_ref=target,
            send_sem=send_sems.at[number],
            recv_sem=recv_sems.at[number],
            device_id=device,
            device_id_type=mesh_id,
        )
        copy.start()
        made[key] = copy

    local = pltpu.make_async_copy(y_ref, out_ref.at[g, h], local_sem)
    local.start()
    own = [y_ref.at[:, rows[0]], y_ref.at[:, rows[1]]]
    group_of = [lax.rem(g + groups - k, groups) for k in range(groups)]
    hidden_of = [lax.rem(h + hidden - 2 * t, hidden) for t in range(chips)]
    send(("ring0", 1), own[0], g, h, 0, ahead)
    for k in range(1, groups):
        send(("peer1", 0, k), own[1], g, h, 1, peers[k])
    send(("ring1", 1, 0), own[1], g, h, 1, ahead)
    for k in range(1, groups):
        send(("peer0", 0, k), own[0], g, h, 0, peers[k])
    for part in range(2):
        send(("pair", part, 0, 0), own[part], g, h, part, partner)

    def arrive0(t):
        made[("ring0", t)].wait_recv()
        if t + 1 < chips:
            send(("ring0", t + 1), None, g, hidden_of[t], 0, ahead)
        for k in range(1, groups):
            send(("peer0", t, k), None, g, hidden_of[t], 0, peers[k])
        send(("pair", 0, t, 0), None, g, hidden_of[t], 0, partner)

    def arrive1(t, k):
        made[("ring1", t, k)].wait_recv()
        if t + 1 < chips:
            send(("ring1", t + 1, k), None, group_of[k], hidden_of[t], 1, ahead)
        send(("pair", 1, t, k), None, group_of[k], hidden_of[t], 1, partner)

    def arrive_peer(t, k):
        made[("peer0", t, k)].wait_recv()
        send(("pair", 0, t, k), None, group_of[k], hidden_of[t], 0, partner)

    arrive0(1)
    for k in range(1, groups):
        made[("peer1", 0, k)].wait_recv()
        send(("ring1", 1, k), None, group_of[k], h, 1, ahead)
        send(("pair", 1, 0, k), None, group_of[k], h, 1, partner)
    for t in range(1, chips):
        if t > 1:
            arrive0(t)
        for k in range(1, groups):
            arrive_peer(t - 1, k)
        for k in range(groups):
            arrive1(t, k)
    for k in range(1, groups):
        arrive_peer(chips - 1, k)
    for key, copy in made.items():
        if key[0] == "pair":
            copy.wait_recv()
        copy.wait_send()
    local.wait()


def gather_all(y, groups, hidden):
    chips = hidden // 2
    copies = (chips - 1) * (1 + groups) + (groups - 1) * (1 + chips) + 2 * chips * groups
    return pl.pallas_call(
        functools.partial(gather_kernel, groups, hidden),
        out_shape=jax.ShapeDtypeStruct((groups, hidden) + y.shape, y.dtype),
        in_specs=[pl.BlockSpec(memory_space=pltpu.VMEM)],
        out_specs=pl.BlockSpec(memory_space=pl.ANY),
        scratch_shapes=[
            pltpu.SemaphoreType.DMA,
            pltpu.SemaphoreType.DMA((copies,)),
            pltpu.SemaphoreType.DMA((copies,)),
        ],
        compiler_params=pltpu.CompilerParams(collective_id=0, has_side_effects=True),
        name="gather_all",
    )(y)


def reduce_kernel(
    groups, hidden, parts_ref, out_ref,
    own, pair_in, peer_in0, peer_in1, ring_in0, ring_in1, local_sems, send_sems, recv_sems,
):
    g, h = lax.axis_index("group"), lax.axis_index("hidden")
    chips = hidden // 2
    tokens = out_ref.shape[1]
    cut = first_rows(tokens)
    rows = (pl.ds(0, cut), pl.ds(cut, tokens - cut))
    ahead = {"group": g, "hidden": lax.rem(h + 2, hidden)}
    behind = {"group": g, "hidden": lax.rem(h + hidden - 2, hidden)}
    partner_h = h + 1 - 2 * lax.rem(h, 2)
    partner = {"group": g, "hidden": partner_h}
    group_of = [lax.rem(g + k, groups) for k in range(groups)]
    peers = [{"group": group_of[k], "hidden": h} for k in range(groups)]
    mesh_id = pl.DeviceIdType.MESH

    barrier = pltpu.get_barrier_semaphore()
    greeted = [ahead, behind, partner] + peers[1:]
    for device in greeted:
        pl.semaphore_signal(barrier, inc=1, device_id=device, device_id_type=mesh_id)
    pl.semaphore_wait(barrier, len(greeted))

    made = {}

    def send(key, source, target, device):
        number = len(made)
        copy = pltpu.make_async_remote_copy(
            src_ref=source,
            dst_ref=target,
            send_sem=send_sems.at[number],
            recv_sem=recv_sems.at[number],
            device_id=device,
            device_id_type=mesh_id,
        )
        copy.start()
        made[key] = copy

    def add(into, *others):
        total = into[...].astype(jnp.float32)
        for other in others:
            total = total + other[...].astype(jnp.float32)
        into[...] = total.astype(into.dtype)

    turns = list(range(1, chips)) + [0]
    loads = {}
    for t in turns:
        for k in range(groups):
            theirs = lax.rem(partner_h + hidden - 2 * t, hidden)
            send(("pair", t, k), parts_ref.at[group_of[k], theirs], pair_in.at[k, t], partner)
            mine = lax.rem(h + hidden - 2 * t, hidden)
            loads[t, k] = pltpu.make_async_copy(
                parts_ref.at[group_of[k], mine], own.at[k, t], local_sems.at[k * chips + t]
            )
            loads[t, k].start()

    def half(k, t, part):
        return own.at[k, t, :, rows[part]]

    last = chips - 1
    for t in turns:
        before = t - 1 if t else last
        for k in range(groups):
            loads[t, k].wait()
            made["pair", t, k].wait_recv()
            add(own.at[k, t], pair_in.at[k, t])
            if t == 1:
                send(("ring1", t, k), half(k, t, 1), ring_in1.at[t, k], ahead)
            if k:
                send(("peer0", t, k), half(k, t, 0), peer_in0.at[t, k], peers[k])
        if t != 1:
            for k in list(range(1, groups)) + [0]:
                made["ring1", before, k].wait_recv()
                add(half(k, t, 1), ring_in1.at[before, k])
                if t:
                    send(("ring1", t, k), half(k, t, 1), ring_in1.at[t, k], ahead)
                elif k:
                    send(("peer1", 0, k), half(k, t, 1), peer_in1.at[k], peers[k])
        arrived = []
        for k in range(1, groups):
            made["peer0", t, k].wait_recv()
            arrived.append(peer_in0.at[t, k])
        if t != 1:
            made["ring0", before].wait_recv()
            arrived.append(ring_in0.at[before])
        add(half(0, t, 0), *arrived)
        if t:
            send(("ring0", t), half(0, t, 0), ring_in0.at[t], ahead)
    for k in range(1, groups):
        made["peer1", 0, k].wait_recv()
    add(half(0, 0, 1), *[peer_in1.at[k] for k in range(1, groups)])
    out_ref[...] = own[0, 0]
    for copy in made.values():
        copy.wait_send()


def reduce_parts(parts, collective_id):
    groups, hidden, pieces, tokens, width = parts.shape
    chips = hidden // 2
    block = 2 * pieces * tokens * width
    if 3 * groups * chips * block > 40 << 20:
        flat = parts.reshape((groups * hidden,) + parts.shape[2:])
        return lax.psum_scatter(flat, ("group", "hidden"), scatter_dimension=0, tiled=True)[0]
    copies = (chips - 1) * (1 + groups) + (groups - 1) * (1 + chips) + chips * groups
    cut = first_rows(tokens)
    first, second = (pieces, cut, width), (pieces, tokens - cut, width)
    bf = parts.dtype
    return pl.pallas_call(
        functools.partial(reduce_kernel, groups, hidden),
        out_shape=jax.ShapeDtypeStruct(parts.shape[2:], bf),
        in_specs=[pl.BlockSpec(memory_space=pl.ANY)],
        out_specs=pl.BlockSpec(memory_space=pltpu.VMEM),
        scratch_shapes=[
            pltpu.VMEM((groups, chips) + parts.shape[2:], bf),
            pltpu.VMEM((groups, chips) + parts.shape[2:], bf),
            pltpu.VMEM((chips, groups) + first, bf),
            pltpu.VMEM((groups,) + second, bf),
            pltpu.VMEM((chips,) + first, bf),
            pltpu.VMEM((chips, groups) + second, bf),
            pltpu.SemaphoreType.DMA((chips * groups,)),
            pltpu.SemaphoreType.DMA((copies,)),
            pltpu.SemaphoreType.DMA((copies,)),
        ],
        compiler_params=pltpu.CompilerParams(
            collective_id=collective_id, has_side_effects=True, vmem_limit_bytes=40 << 20
        ),
        name=f"reduce_parts_{collective_id}",
    )(parts)


def to_rows(values, rows, width):
    high = lax.reduce_precision(values, 8, 7)
    rest = values - high
    mid = lax.reduce_precision(rest, 8, 7)
    flat = jnp.stack([high, mid, rest - mid]).reshape(-1).astype(jnp.bfloat16)
    return jnp.pad(flat, (0, rows * width - flat.shape[0])).reshape(rows, width)


def from_rows(block, count):
    flat = block.reshape(block.shape[:2] + (-1,))[:, :, : 3 * count].astype(jnp.float32)
    high, mid, low = (flat[:, :, i * count : (i + 1) * count] for i in range(3))
    return high + mid + low


def experts(order, ids, y, scale, w_gate, w_up, w_down):
    groups, blocks, _, rows, width = y.shape
    tokens = scale.shape[1]
    model = blocks * width
    per_owner = ids.shape[1]
    units = w_down.shape[1]
    half = per_owner * units
    ids_end = groups * per_owner

    def pick(s):
        return pl.BlockSpec((1, units, model), lambda k, n: (n[k * per_owner + s], 0, 0))

    bf = jnp.bfloat16
    parts = jax.ShapeDtypeStruct((groups, blocks, 2, tokens, width), bf)
    return pl.pallas_call(
        functools.partial(expert_kernel, per_owner),
        grid_spec=pltpu.PrefetchScalarGridSpec(
            num_scalar_prefetch=1,
            grid=(groups,),
            in_specs=[pick(s) for s in range(per_owner)] * 3
            + [
                pl.BlockSpec(
                    (1, blocks, 2, rows, width), lambda k, n: (n[ids_end + k], 0, 0, 0, 0)
                ),
                pl.BlockSpec(
                    (1, tokens, scale.shape[2]), lambda k, n: (n[ids_end + k], 0, 0)
                ),
            ],
            out_specs=[
                pl.BlockSpec((1,) + parts.shape[1:], lambda k, n: (n[ids_end + k], 0, 0, 0, 0)),
            ]
            + [pl.BlockSpec(memory_space=pl.ANY)] * 3,
            scratch_shapes=[
                pltpu.VMEM((tokens, model), bf),
                pltpu.VMEM((tokens, model), bf),
                pltpu.VMEM((2 * half, model), bf),
                pltpu.VMEM((half, model), bf),
                pltpu.VMEM((tokens, half), bf),
                pltpu.VMEM((tokens, 2 * half), bf),
                pltpu.VMEM((half, tokens), bf),
                pltpu.VMEM((2 * half, tokens), bf),
                pltpu.VMEM(w_down.shape, bf),
                pltpu.VMEM(w_down.shape, bf),
                pltpu.VMEM(w_down.shape, bf),
                pltpu.SemaphoreType.DMA((3,)),
            ],
        ),
        out_shape=[parts] + [jax.ShapeDtypeStruct(w_down.shape, bf)] * 3,
        compiler_params=pltpu.CompilerParams(vmem_limit_bytes=56 << 20),
        name="experts",
    )(
        jnp.concatenate([ids.reshape(-1), order]),
        *([w_gate] * per_owner + [w_up] * per_owner + [w_down] * per_owner),
        y,
        scale,
    )


def pair_groups(g, i):
    across, along = 1 - i // 2, 1 - lax.rem(i, 2)
    gx, gy = lax.rem(g, 2), g // 2
    return lax.rem(gy + along, 2) * 2 + lax.rem(gx + across, 2)


def near_rows(count):
    return count // 36 * 32


def direct_rows(count):
    return count // 48 * 32


def layer_kernel(
    groups, hidden,
    fetch_ref, q_ref, k_ref, v_ref, proj_ref, cot_ref, res_ref, gain_ref, seats_ref, shares_ref,
    gate_ref, up_ref, down_ref,
    layer_out, normed_out, w_gate, w_up, w_down, cot_all, x_all,
    q, k, v, proj, residual, mixed, f_own, f_stage, f_pair, f_ring, stream, y, slot_rows, slot_all,
    xs, cs, tails, w_in, w_out, act, grads, act_turned, grads_turned, slot_gate, slot_up, slot_down,
    own, stage, pair_in, diag_in, peer_in0, peer_in1, ring_in0, ring_in1,
    load_sems, slot_sems, cot_sems, f_pair_sems, f_ring_sems, y_sems, fetch_sems,
    pair_sems, ring1_sems, diag_sems, peer0_sems, peer1_sems, ring0_sems,
):
    g, h = lax.axis_index("group"), lax.axis_index("hidden")
    chips = hidden // 2
    owned, units, model = w_gate.shape
    tokens, width = layer_out.shape
    per_owner = fetch_ref.shape[1] // groups
    half = per_owner * units
    last, final = chips - 1, groups - 1
    turns = list(range(1, chips)) + [0]
    ahead = {"group": g, "hidden": lax.rem(h + 2, hidden)}
    behind = {"group": g, "hidden": lax.rem(h + hidden - 2, hidden)}
    partner_h = h + 1 - 2 * lax.rem(h, 2)
    partner = {"group": g, "hidden": partner_h}
    mesh_id = pl.DeviceIdType.MESH
    source = [pair_groups(g, i) for i in range(groups)]
    peers = [{"group": source[i], "hidden": h} for i in range(final)]
    turned = ((1,), (1,))

    barrier = pltpu.get_barrier_semaphore()
    greeted = [ahead, behind, partner] + peers
    for device in greeted:
        pl.semaphore_signal(barrier, inc=1, device_id=device, device_id_type=mesh_id)

    my_cols = pl.ds(pl.multiple_of(h * width, width), width)
    moves = (
        (q_ref, q), (k_ref, k), (v_ref, v), (proj_ref, proj), (res_ref.at[:, my_cols], residual),
        (gate_ref, w_gate), (up_ref, w_up), (down_ref, w_down),
    )
    loads = [pltpu.make_async_copy(a, b, load_sems.at[n]) for n, (a, b) in enumerate(moves)]
    for copy in loads:
        copy.start()

    slot_rows[...] = jnp.zeros_like(slot_rows)
    for f in range(groups * per_owner):
        named = jnp.where(seats_ref[...] == f, shares_ref[...], 0.0)
        slot_rows[f // per_owner, f % per_owner : f % per_owner + 1, :] = jnp.sum(
            named, axis=0, keepdims=True
        )
    for buffer in (slot_gate, slot_up, slot_down):
        buffer[per_owner] = jnp.zeros(buffer.shape[1:], buffer.dtype)
    slot_all[g] = slot_rows[g]

    def remote(source_ref, target, sems, index, device):
        return pltpu.make_async_remote_copy(
            src_ref=source_ref,
            dst_ref=target,
            send_sem=sems.at[(0,) + index],
            recv_sem=sems.at[(1,) + index],
            device_id=device,
            device_id_type=mesh_id,
        )

    def add(into, *others):
        total = into[...].astype(jnp.float32)
        for other in others:
            total = total + other[...].astype(jnp.float32)
        into[...] = total.astype(into.dtype)

    pl.semaphore_wait(barrier, len(greeted))

    quarter = tokens // 4
    base = lax.rem(h, 2) * (2 * quarter)
    cot_made = {}

    def piece(n):
        return pl.ds(pl.multiple_of(base + n * quarter, quarter), quarter)

    def landed(i, n):
        return cot_all.at[source[i], piece(n)]

    def send_cot(key, source_ref, target, device):
        copy = remote(source_ref, target, cot_sems, (len(cot_made),), device)
        copy.start()
        cot_made[key] = copy

    for i, n in ((1, 0), (2, 1), (1, 1), (2, 0)):
        send_cot(("near", i, n), cot_ref.at[piece(n)], cot_all.at[g, piece(n)], peers[i])
    slots = [
        remote(slot_rows.at[source[i]], slot_all.at[g], slot_sems, (i,), peers[i])
        for i in range(final)
    ]
    for copy in slots:
        copy.start()

    def pass_cot(i, n, forward):
        cot_made["far" if i == 0 else "near", i, n].wait_recv()
        if forward:
            send_cot(("far", 0, n), landed(i, n), landed(i, n), peers[3 - i])
        send_cot(("pair", i, n), landed(i, n), landed(i, n), partner)

    for copy in loads[:3]:
        copy.wait()
    heads_here = q.shape[1] // HEAD_DIM
    kv = h * heads_here // (HEADS // KV_HEADS)
    kv_cols = pl.ds(pl.multiple_of(kv * HEAD_DIM, HEAD_DIM), HEAD_DIM)
    keys, values = k[:, kv_cols], v[:, kv_cols]
    seen = lax.broadcasted_iota(jnp.int32, (tokens, tokens), 0) >= lax.broadcasted_iota(
        jnp.int32, (tokens, tokens), 1
    )
    for head in range(heads_here):
        cols = slice(head * HEAD_DIM, (head + 1) * HEAD_DIM)
        scores = dot(q[:, cols], keys, turned) / math.sqrt(HEAD_DIM)
        scores = jnp.where(seen, scores, -1e30)
        weights = jnp.exp(scores - jnp.max(scores, axis=-1, keepdims=True))
        total = jnp.sum(weights, axis=-1, keepdims=True)
        mixed[:, cols] = dot((weights / total).astype(mixed.dtype), values).astype(mixed.dtype)

    def f_pair_copy(t):
        return remote(f_stage.at[t], f_pair.at[t], f_pair_sems, (t,), partner)

    middle_row = tokens // 32 * 16
    halves = (pl.ds(0, middle_row), pl.ds(middle_row, tokens - middle_row))

    def f_ring_copy(t, part):
        span = halves[part]
        return remote(f_own.at[t, span], f_ring.at[t, span], f_ring_sems, (t, part), ahead)

    def reduce_task(t, part):
        span = halves[part]
        if part == 0:
            f_pair_copy(t).wait_recv()
        if t == 1:
            add(f_own.at[t, span], f_pair.at[t, span])
        else:
            before = t - 1 if t else last
            f_ring_copy(before, part).wait_recv()
            add(f_own.at[t, span], f_pair.at[t, span], f_ring.at[before, span])
        if t:
            f_ring_copy(t, part).start()

    for copy in loads[3:5]:
        copy.wait()

    @pl.loop(0, chips)
    def _(j):
        t = lax.rem(j + 1, chips)
        for whose, target in ((partner_h, f_stage), (h, f_own)):
            first = pl.multiple_of(lax.rem(whose + hidden - 2 * t, hidden) * width, width)
            target[t] = dot(mixed[...], proj[:, pl.ds(first, width)]).astype(target.dtype)
            if whose is partner_h:
                f_pair_copy(t).start()

        @pl.when(j == 1)
        def _():
            reduce_task(1, 0)
            reduce_task(1, 1)

    pass_cot(1, 0, True)
    pass_cot(2, 1, True)
    for t in turns[1:]:
        for part in range(2):
            reduce_task(t, part)

    stream[...] = residual[...].astype(jnp.float32) + f_own[0].astype(jnp.float32)
    y[:tokens, :] = (stream[...] * gain_ref[:, my_cols]).astype(y.dtype)
    squares = jnp.sum(stream[...] * stream[...], axis=-1, keepdims=True)
    squares = jnp.broadcast_to(squares, (tokens, 128)).T[:16]
    high = squares.astype(y.dtype).astype(jnp.float32)
    middle = (squares - high).astype(y.dtype).astype(jnp.float32)
    low = squares - high - middle
    row = lax.broadcasted_iota(jnp.int32, (16, width), 0)
    extras = jnp.zeros((16, width), jnp.float32)
    for c in range(-(-tokens // width)):
        count = min(width, tokens - c * width)
        for n, term in enumerate((high, middle, low)):
            term = term[:, c * width : c * width + count]
            if count < width:
                term = jnp.concatenate([term, jnp.zeros((16, width - count), jnp.float32)], axis=1)
            extras = jnp.where(row == 3 * c + n, term, extras)
    y[tokens:, :] = extras.astype(y.dtype)

    rows_all = y.shape[0]
    near = near_rows(rows_all)
    spans = {0: pl.ds(0, near), 1: pl.ds(near, rows_all - near)}
    spans["a"], spans["b"] = pl.ds(0, near // 2), pl.ds(near // 2, near // 2)
    behind_h = [lax.rem(h + hidden - 2 * t, hidden) for t in range(chips)]
    y_made = {}

    def y_copy(number, mine, i, t, span, device):
        target = x_all.at[source[i], behind_h[t], spans[span]]
        return remote(y.at[spans[span]] if mine else target, target, y_sems, (number,), device)

    def send_y(key, *what):
        y_made[key] = (len(y_made),) + what
        y_copy(*y_made[key]).start()

    def y_arrived(*key):
        y_copy(*y_made[key]).wait_recv()

    home = groups - 1

    def ring_y0(t):
        y_arrived("ring0", t)
        if t + 1 < chips:
            send_y(("ring0", t + 1), False, home, t, 0, ahead)
        for i in (1, 2):
            send_y(("near0", t, i), False, home, t, 0, peers[i])
        send_y(("pair", home, t, 0), False, home, t, 0, partner)

    def ring_y1(t, i):
        y_arrived("ring1", t, i)
        if t + 1 < chips:
            send_y(("ring1", t + 1, i), False, i, t, 1, ahead)
        send_y(("pair", i, t, 1), False, i, t, 1, partner)

    def near_y0(t):
        for i, span in ((1, "a"), (2, "b")):
            y_arrived("near0", t, i)
            send_y(("far0", t, span), False, i, t, span, peers[3 - i])
            send_y(("pair", i, t, 0), False, i, t, 0, partner)

    def far_y0(t):
        for span in ("a", "b"):
            y_arrived("far0", t, span)
            send_y(("pair", 0, t, span), False, 0, t, span, partner)

    local = pltpu.make_async_copy(y, x_all.at[g, h], load_sems.at[len(moves)])
    local.start()
    send_y(("ring0", 1), True, home, 0, 0, ahead)
    for i in (1, 2):
        send_y(("near0", 0, i), True, home, 0, 0, peers[i])
    for i in (1, 2, 0):
        send_y(("near1", i), True, home, 0, 1, peers[i])
    send_y(("ring1", 1, home), True, home, 0, 1, ahead)
    for span in (0, 1):
        send_y(("pair", home, 0, span), True, home, 0, span, partner)
    pass_cot(1, 1, False)
    pass_cot(2, 0, False)
    ring_y0(1)
    near_y0(0)
    for i in (1, 2, 0):
        y_arrived("near1", i)
        send_y(("ring1", 1, i), False, i, 0, 1, ahead)
        send_y(("pair", i, 0, 1), False, i, 0, 1, partner)
    ring_y1(1, home)
    pass_cot(0, 0, False)
    pass_cot(0, 1, False)
    for t in range(2, chips):
        ring_y0(t)
        near_y0(t - 1)
        for i in range(final):
            ring_y1(t - 1, i)
        ring_y1(t, home)
        if t > 2:
            far_y0(t - 3)
    for t in turns:
        if t:
            f_pair_copy(t).wait_send()
            for part in range(2):
                f_ring_copy(t, part).wait_send()
    f_pair_copy(0).wait_send()
    for copy in loads[5:]:
        copy.wait()
    local.wait()
    for copy in slots:
        copy.wait_recv()
    for t in range(chips):
        for span in (0, 1):
            y_arrived("pair", home, t, span)

    def gather_task(n):
        if n == 0:
            near_y0(last)
        elif n == 1:
            for i in range(final):
                ring_y1(last, i)
        elif n == 2:
            far_y0(last - 2)
            far_y0(last - 1)
        else:
            far_y0(last)
            for key in y_made:
                if key[0] == "pair" and key[1] != home:
                    y_arrived(*key)
            for key, copy in cot_made.items():
                if key[0] == "pair":
                    copy.wait_recv()

    cut = direct_rows(tokens)
    rows = (pl.ds(0, cut), pl.ds(cut, tokens - cut))
    via = (pl.ds(0, cut // 2), pl.ds(cut // 2, cut // 2))

    def peer(i):
        return {"group": pair_groups(g, i), "hidden": h}

    def fetch_x(i):
        slot = lax.rem(i, 2)
        group = pair_groups(g, i)
        copies = []
        for b in range(hidden):
            cols = pl.ds(b * width, width)
            copies.append(
                pltpu.make_async_copy(
                    x_all.at[group, b, pl.ds(0, tokens)], xs.at[slot, :, cols], fetch_sems.at[slot, b]
                )
            )
            copies.append(
                pltpu.make_async_copy(
                    x_all.at[group, b, pl.ds(tokens, 16)],
                    tails.at[slot, :, cols],
                    fetch_sems.at[slot, hidden + b],
                )
            )
        return copies

    def fetch_c(i, mine):
        slot = lax.rem(i, 2)
        origin = cot_ref if mine else cot_all.at[pair_groups(g, i)]
        return pltpu.make_async_copy(origin, cs.at[slot], fetch_sems.at[slot, 2 * hidden])

    def start_fetch(i):
        for copy in fetch_x(i):
            copy.start()

        @pl.when(i < final)
        def _():
            fetch_c(i, False).start()

        @pl.when(i == final)
        def _():
            fetch_c(i, True).start()

    def wait_fetch(i):
        for copy in fetch_x(i):
            copy.wait()
        fetch_c(i, False).wait()

    def part_of(i, t, part):
        return own.at[i, t, :, rows[part]]

    def pair_copy(i, t):
        return remote(stage.at[lax.rem(i, 2), t], pair_in.at[i, t], pair_sems, (i, t), partner)

    def ring1_copy(i, t):
        return remote(part_of(i, t, 1), ring_in1.at[i, t], ring1_sems, (i, t), ahead)

    def diag_copy(n, t):
        return remote(own.at[0, t, :, via[n]], diag_in.at[n, t], diag_sems, (n, t), peer(n + 1))

    def peer0_copy(i, t):
        return remote(part_of(i, t, 0), peer_in0.at[i - 1, t], peer0_sems, (i - 1, t), peer(i))

    def peer1_copy(i):
        return remote(part_of(i, 0, 1), peer_in1.at[i], peer1_sems, (i,), peer(i))

    def ring0_copy(t):
        return remote(part_of(final, t, 0), ring_in0.at[t], ring0_sems, (t,), ahead)

    def pair_task(i, t):
        pair_copy(i, t).wait_recv()
        add(own.at[i, t], pair_in.at[i, t])
        if t == 1:
            ring1_copy(i, t).start()

        @pl.when(i == 0)
        def _():
            for n in range(2):
                diag_copy(n, t).start()

        for n, step in ((1, 1), (0, 2)):

            @pl.when(i == step)
            def _():
                diag_copy(n, t).wait_recv()
                add(own.at[step, t, :, via[n]], diag_in.at[n, t])
                peer0_copy(step, t).start()

    def ring_task(i, t):
        before = t - 1 if t else last
        ring1_copy(i, before).wait_recv()
        add(part_of(i, t, 1), ring_in1.at[i, before])
        if t:
            ring1_copy(i, t).start()

    def finish_task(t):
        arrived = []
        for i in range(1, final):
            peer0_copy(i, t).wait_recv()
            arrived.append(peer_in0.at[i - 1, t])
        if t != 1:
            before = t - 1 if t else last
            ring0_copy(before).wait_recv()
            arrived.append(ring_in0.at[before])
        add(part_of(final, t, 0), *arrived)
        if t:
            ring0_copy(t).start()

    def finish_ring(i):
        ring_task(i, 0)

        @pl.when(i < final)
        def _():
            peer1_copy(i).start()

    def scale_of(slot, group):
        terms = jnp.zeros((16, width), jnp.float32)
        for b in range(hidden):
            terms = terms + tails[slot, :, b * width : (b + 1) * width].astype(jnp.float32)
        chunks = []
        for c in range(-(-tokens // width)):
            count = min(width, tokens - c * width)
            total = terms[3 * c : 3 * c + 1] + terms[3 * c + 1 : 3 * c + 2] + terms[3 * c + 2 : 3 * c + 3]
            chunks.append(total[:, :count])
        inverse = lax.rsqrt(jnp.concatenate(chunks, axis=1) / model + epsilon)
        row = lax.broadcasted_iota(jnp.int32, (8, tokens), 0)
        both = jnp.where(row == per_owner, inverse, slot_all[group])
        return jnp.concatenate([both, jnp.zeros((120, tokens), jnp.float32)], axis=0).T

    start_fetch(home)

    @pl.loop(0, groups)
    def _(step):
        i, one, two = (lax.rem(step + groups - 1 - d, groups) for d in range(3))
        slot = lax.rem(i, 2)
        group = pair_groups(g, i)

        @pl.when(step > 0)
        def _():
            pair_task(one, 1)

        @pl.when((step > 0) & (step < final))
        def _():
            start_fetch(i + 1)

        for s in range(per_owner):
            e = lax.rem(fetch_ref[group, g * per_owner + s], owned)
            w_in[s * units : (s + 1) * units, :] = w_gate[e]
            w_in[half + s * units : half + (s + 1) * units, :] = w_up[e]
            w_out[s * units : (s + 1) * units, :] = w_down[e]
        wait_fetch(i)
        scale = scale_of(slot, group)
        inverse = scale[:, per_owner : per_owner + 1]
        lane = lax.broadcasted_iota(jnp.int32, (tokens, half), 1)
        weight = jnp.broadcast_to(scale[:, :1], (tokens, half))
        for s in range(1, per_owner):
            weight = jnp.where(lane >= s * units, scale[:, s : s + 1], weight)
        pre_gate = dot(xs[slot], w_in[:half, :], turned) * inverse

        @pl.when(step == 0)
        def _():
            gather_task(0)

        @pl.when(step > 0)
        def _():
            pair_task(one, 2)

        pre_up = dot(xs[slot], w_in[half:, :], turned) * inverse

        @pl.when(step == 0)
        def _():
            gather_task(1)

        @pl.when(step > 0)
        def _():
            pair_task(one, 3)

        @pl.when(step > 1)
        def _():
            ring_task(two, 3)

        d_act = dot(cs[slot], w_out[...], turned) * weight

        @pl.when(step == 0)
        def _():
            gather_task(2)

        @pl.when(step > 0)
        def _():
            pair_task(one, 0)

        sig = jax.nn.sigmoid(pre_gate)
        swish = pre_gate * sig
        weighted = swish * pre_up * weight
        d_gate = d_act * pre_up * sig * (1.0 + pre_gate * (1.0 - sig))
        d_up = d_act * swish
        act[...] = weighted.astype(act.dtype)
        grads[:, :half] = d_gate.astype(grads.dtype)
        grads[:, half:] = d_up.astype(grads.dtype)
        act_turned[i] = act[...].T
        grads_turned[i, :half, :] = (d_gate * inverse).astype(grads.dtype).T
        grads_turned[i, half:, :] = (d_up * inverse).astype(grads.dtype).T

        @pl.loop(0, chips)
        def _(j):
            t = lax.rem(j + 1, chips)

            @pl.when(step > 1)
            def _():
                pair_copy(two, t).wait_send()

            for whose, target, at in ((partner_h, stage, slot), (h, own, i)):
                first = pl.multiple_of(lax.rem(whose + hidden - 2 * t, hidden) * width, width)
                cols = pl.ds(first, width)
                target[at, t, 0] = dot(act[...], w_out[:, cols]).astype(target.dtype)
                target[at, t, 1] = dot(grads[...], w_in[:, cols]).astype(target.dtype)
                if whose is partner_h:
                    pair_copy(i, t).start()

        @pl.when(step > 0)
        def _():
            ring_task(one, 2)

        @pl.when(step > 1)
        def _():
            finish_ring(two)

        @pl.when(step == 0)
        def _():
            gather_task(3)
            start_fetch(0)

    for buffer in (w_gate, w_up, w_down):
        buffer[...] = jnp.zeros_like(buffer)

    tasks = (
        (0, lambda: pair_task(final - 1, 1)),
        (1, lambda: pair_task(final - 1, 2)),
        (2, lambda: pair_task(final - 1, 3)),
        (3, lambda: pair_task(final - 1, 0)),
        (5, lambda: ring_task(final - 2, 3)),
        (8, lambda: ring_task(final - 1, 2)),
        (9, lambda: finish_task(1)),
        (11, lambda: finish_ring(final - 2)),
        (14, lambda: ring_task(final - 1, 3)),
        (18, lambda: finish_task(2)),
        (22, lambda: finish_ring(final - 1)),
        (27, lambda: finish_task(3)),
    )

    @pl.loop(0, groups * hidden)
    def _(n):
        turn, b = n // hidden, lax.rem(n, hidden)
        i = lax.rem(2 * groups - 2 - turn, groups)
        slot = lax.rem(i, 2)
        group = pair_groups(g, i)

        @pl.when((b == 0) & (turn > 0) & (turn < final))
        def _():
            start_fetch(lax.rem(i + groups - 1, groups))

        @pl.when((b == 0) & (turn > 1))
        def _():
            wait_fetch(i)

        cols = pl.ds(pl.multiple_of(b * width, width), width)
        down = dot(act_turned[i], cs[slot, :, cols])
        both = dot(grads_turned[i], xs[slot, :, cols])
        for s in range(per_owner):
            slot_down[s] = down[s * units : (s + 1) * units]
            slot_gate[s] = both[s * units : (s + 1) * units]
            slot_up[s] = both[half + s * units : half + (s + 1) * units]
        listed = [lax.rem(fetch_ref[group, g * per_owner + s], owned) for s in range(per_owner)]
        for e in range(owned):
            seat = jnp.int32(per_owner)
            for s in range(per_owner):
                seat = jnp.where(listed[s] == e, s, seat)
            for total, value in ((w_down, slot_down), (w_gate, slot_gate), (w_up, slot_up)):
                total[e, :, cols] = (total[e, :, cols].astype(jnp.float32) + value[seat]).astype(
                    total.dtype
                )
        for at, task in tasks:
            pl.when(n == at)(task)

    finish_task(0)
    for i in range(final):
        peer1_copy(i).wait_recv()
    add(part_of(final, 0, 1), *[peer_in1.at[i] for i in range(final)])
    layer_out[...] = (stream[...] + own[final, 0, 0].astype(jnp.float32)).astype(layer_out.dtype)
    normed_out[...] = own[final, 0, 1]
    for t in range(chips):
        for i in range(groups):
            if final - 2 <= i < final:
                pair_copy(i, t).wait_send()
            if t:
                ring1_copy(i, t).wait_send()
            if 0 < i < final:
                peer0_copy(i, t).wait_send()
        for n in range(2):
            diag_copy(n, t).wait_send()
        if t:
            ring0_copy(t).wait_send()
    for i in range(final):
        peer1_copy(i).wait_send()
    for key in y_made:
        y_copy(*y_made[key]).wait_send()
    for copy in cot_made.values():
        copy.wait_send()
    for copy in slots:
        copy.wait_send()


def store_kernel(count, *refs):
    sources, targets, sems = refs[:count], refs[count:-1], refs[-1]
    copies = [
        pltpu.make_async_copy(a, b, sems.at[n]) for n, (a, b) in enumerate(zip(sources, targets))
    ]
    for copy in copies:
        copy.start()
    for copy in copies:
        copy.wait()


def store(*values):
    count = len(values)
    return pl.pallas_call(
        functools.partial(store_kernel, count),
        in_specs=[pl.BlockSpec(memory_space=pltpu.VMEM)] * count,
        out_specs=[pl.BlockSpec(memory_space=pl.ANY)] * count,
        out_shape=[jax.ShapeDtypeStruct(value.shape, value.dtype) for value in values],
        scratch_shapes=[pltpu.SemaphoreType.DMA((count,))],
        compiler_params=pltpu.CompilerParams(vmem_limit_bytes=STORE_LIMIT),
        name="store",
    )(*values)


def layer(
    fetch_list, queries, key_rows, value_rows, out_proj, cotangent, residual, gain, seats, shares,
    w_gate, w_up, w_down, groups, hidden,
):
    tokens, model = cotangent.shape
    width = model // hidden
    chips = hidden // 2
    owned, units, _ = w_down.shape
    per_owner = fetch_list.shape[1] // groups
    half = per_owner * units
    bf = queries.dtype
    cut = direct_rows(tokens)
    block = (2, tokens, width)
    vmem = pl.BlockSpec(memory_space=pltpu.VMEM)
    anywhere = pl.BlockSpec(memory_space=pl.ANY)
    dma = pltpu.SemaphoreType.DMA
    f32 = jnp.float32
    shape = jax.ShapeDtypeStruct
    scratch = [
        (queries.shape, bf), (key_rows.shape, bf), (value_rows.shape, bf), (out_proj.shape, bf),
        ((tokens, width), bf), (queries.shape, bf)
    ]
    scratch += [((chips, tokens, width), bf)] * 4
    scratch += [
        ((tokens, width), f32), ((tokens + 16, width), bf),
        ((groups, 8, tokens), f32), ((groups, 8, tokens), f32),
        ((2, tokens, model), bf), ((2, tokens, model), bf), ((2, 16, model), bf),
        ((2 * half, model), bf), ((half, model), bf), ((tokens, half), bf), ((tokens, 2 * half), bf),
        ((groups, half, tokens), bf), ((groups, 2 * half, tokens), bf),
    ]
    scratch += [((per_owner + 1, units, width), f32)] * 3
    scratch += [
        ((groups, chips) + block, bf), ((2, chips) + block, bf), ((groups, chips) + block, bf),
        ((2, chips, 2, cut // 2, width), bf),
        ((groups - 2, chips, 2, cut, width), bf), ((groups - 1, 2, tokens - cut, width), bf),
        ((chips, 2, cut, width), bf), ((groups, chips, 2, tokens - cut, width), bf),
    ]
    sems = [
        (9,), (2, groups - 1), (2, 12), (2, chips), (2, chips, 2), (2, 72), (2, 2 * hidden + 1),
        (2, groups, chips), (2, groups, chips), (2, 2, chips), (2, groups - 2, chips),
        (2, groups - 1), (2, chips),
    ]
    return pl.pallas_call(
        functools.partial(layer_kernel, groups, hidden),
        in_specs=[pl.BlockSpec(memory_space=pltpu.SMEM)]
        + [anywhere] * 6 + [vmem] * 3 + [anywhere] * 3,
        out_specs=[vmem] * 5 + [anywhere] * 2,
        out_shape=[pltpu.VMEM((tokens, width), bf)] * 2
        + [pltpu.VMEM(w_down.shape, bf)] * 3
        + [
            shape((groups, tokens, model), bf),
            shape((groups, hidden, tokens + 16, width), bf),
        ],
        scratch_shapes=[pltpu.VMEM(*s) for s in scratch] + [dma(s) for s in sems],
        compiler_params=pltpu.CompilerParams(
            collective_id=1, has_side_effects=True, vmem_limit_bytes=51 << 20
        ),
        name="layer",
    )(
        fetch_list, queries, key_rows, value_rows, out_proj, cotangent, residual, gain, seats,
        shares, w_gate, w_up, w_down,
    )


def shards(
    queries,
    key_rows,
    value_rows,
    out_proj,
    residual,
    norm_gain,
    w_gate,
    w_up,
    w_down,
    route_slot,
    route_weight,
    fetch_list,
    cotangent,
):
    tokens_here, model = cotangent.shape
    hidden_index = lax.axis_index("hidden")
    hidden_count = lax.axis_size("hidden")
    group_index = lax.axis_index("group")
    group_count = lax.axis_size("group")
    per_owner = FETCH // group_count

    if group_count == 4:
        outs = layer(
            fetch_list, queries, key_rows, value_rows, out_proj, cotangent, residual,
            norm_gain[None], route_slot.T, route_weight.T,
            jnp.swapaxes(w_gate, 1, 2), jnp.swapaxes(w_up, 1, 2), w_down,
            group_count, hidden_count,
        )
        outs = store(*outs[:5])
        return (
            outs[0], outs[1], jnp.swapaxes(outs[2], 1, 2), jnp.swapaxes(outs[3], 1, 2), outs[4]
        )

    chosen = route_slot[:, :, None] == jnp.arange(FETCH, dtype=jnp.int32)[None, None, :]
    slot_weight = jnp.sum(jnp.where(chosen, route_weight[:, :, None], 0.0), axis=1)
    order = (group_index + jnp.arange(group_count, dtype=jnp.int32)) % group_count
    own_cols = lax.dynamic_slice_in_dim(fetch_list, group_index * per_owner, per_owner, 1)
    ids = jnp.take(own_cols - group_index * EXP_GROUP, order, axis=0)

    heads_here = queries.shape[1] // HEAD_DIM
    kv_index = hidden_index * heads_here // (HEADS // KV_HEADS)
    key_block = lax.dynamic_slice_in_dim(key_rows, kv_index * HEAD_DIM, HEAD_DIM, 1)
    value_block = lax.dynamic_slice_in_dim(value_rows, kv_index * HEAD_DIM, HEAD_DIM, 1)
    mixed = attention_rows(queries, key_block, value_block, heads_here)
    partial_value = jnp.dot(mixed, out_proj, preferred_element_type=jnp.float32)
    share_width = model // hidden_count
    first_col = hidden_index * share_width
    blocks = partial_value.astype(jnp.bfloat16).reshape(tokens_here, hidden_count, share_width)
    attn_share = reduce_parts(jnp.swapaxes(blocks, 0, 1)[None, :, None], 2)[0]
    stream = lax.dynamic_slice_in_dim(residual, first_col, share_width, 1).astype(
        jnp.float32
    ) + attn_share.astype(jnp.float32)
    gain = lax.dynamic_slice_in_dim(norm_gain, first_col, share_width, 0)
    squares = jnp.sum(stream * stream, axis=-1)
    gained = (stream * gain).astype(jnp.bfloat16)
    slots_here = FETCH // hidden_count
    slots = lax.dynamic_slice_in_dim(slot_weight.T, hidden_index * slots_here, slots_here, 0)
    extra = -(-3 * slots_here * tokens_here // (16 * share_width)) * 16
    cot_share = lax.dynamic_slice_in_dim(cotangent, first_col, share_width, 1)
    y = jnp.stack(
        [
            jnp.concatenate([gained, to_rows(squares, extra, share_width)]),
            jnp.concatenate([cot_share, to_rows(slots, extra, share_width)]),
        ]
    )
    y_all = gather_all(y, group_count, hidden_count)
    squares_all = from_rows(y_all[:, :, 0, tokens_here:], tokens_here).sum(axis=1)
    inverse = lax.rsqrt(squares_all / model + epsilon)
    weights = from_rows(y_all[:, :, 1, tokens_here:], slots_here * tokens_here)
    weights = weights.reshape(group_count, FETCH, tokens_here)
    weights = lax.dynamic_slice_in_dim(weights, group_index * per_owner, per_owner, 1)
    scale = jnp.concatenate([weights, inverse[:, None, :]], axis=1)
    scale = jnp.pad(scale, ((0, 0), (0, 8 - scale.shape[1]), (0, 0)))
    scale = jnp.swapaxes(scale, 1, 2)
    parts, grad_gate, grad_up, grad_down = experts(
        order,
        ids,
        y_all,
        scale,
        jnp.swapaxes(w_gate, 1, 2),
        jnp.swapaxes(w_up, 1, 2),
        w_down,
    )
    grad_gate = jnp.swapaxes(grad_gate, 1, 2)
    grad_up = jnp.swapaxes(grad_up, 1, 2)
    sums = reduce_parts(parts, 1)
    layer_out = (stream + sums[0].astype(jnp.float32)).astype(jnp.bfloat16)
    return (layer_out, sums[1], grad_gate, grad_up, grad_down)


def solution(mesh):
    return jax.shard_map(
        shards,
        mesh=mesh,
        in_specs=(
            P("group", "hidden"),
            P("group", None),
            P("group", None),
            P("hidden", None),
            P("group", None),
            P(),
            P("group", None, "hidden"),
            P("group", None, "hidden"),
            P("group", "hidden", None),
            P("group", None),
            P("group", None),
            P(),
            P("group", None),
        ),
        out_specs=(
            P("group", "hidden"),
            P("group", "hidden"),
            P("group", None, "hidden"),
            P("group", None, "hidden"),
            P("group", "hidden", None),
        ),
        check_vma=False,
    )
```
